32 devices in a mesh: dp: 4 (over y, core), px: 2 (over x), py: 4 (over z).
Axes of the slice: x: 2, y: 2, z: 4, core: 2. Of those that a mesh axis runs over, the one named last changes fastest.
Arguments:
- state_a: bfloat16 [4, 16, 128, 128, 128], P('dp', None, 'px', 'py'), may hold values from -6 to 6
- state_b: bfloat16 [4, 16, 128, 128, 128], P('dp', None, 'px', 'py'), may hold values from -6 to 6
- cotan_a: bfloat16 [4, 16, 128, 128, 128], P('dp', None, 'px', 'py'), may hold values from -6 to 6
- cotan_b: bfloat16 [4, 16, 128, 128, 128], P('dp', None, 'px', 'py'), may hold values from -6 to 6
- spectral_weight: bfloat16 [32, 8, 32, 2, 16, 16], P('py', None, 'px'), may hold values from -1 to 1
- point_weight: bfloat16 [16, 16], replicated, may hold values from -1.5 to 1.5
Outputs:
- input_a: bfloat16 [4, 16, 128, 128, 128], P('dp', None, 'px', 'py')
- grad_b: bfloat16 [4, 16, 128, 128, 128], P('dp', None, 'px', 'py')
- spectral_grad: float32 [32, 8, 32, 2, 16, 16], P('py', None, 'px', None, None, 'dp')
- point_grad: float32 [16, 16], replicated
The draws below stay inside these ranges and needn't reach their ends.
All inputs are finite; a program needn't handle non-finite values.
Results may differ from the reference program's by a relative error of at most 0.0038.
Values sent between devices are 32-bit elements; how exact they have to be, the bound alone decides.
A program may use at most 384 MiB of HBM per device.

```python
import math
import jax
import jax.numpy as jnp
from jax import lax

CH = 16
NX = 128
NY = 128
NZ = 128
MX = 32
MY = 32
MZ = 8
BATCH = 4


def block_levels(own_key, extent, split, smallest, largest):
    loudness, own = 1.0, jax.random.fold_in(own_key, 6)
    for position, parts in split:
        steps = jnp.exp(jax.random.uniform(jax.random.fold_in(own, position), (parts,), jnp.float32, smallest / len(split), largest / len(split)))
        loudness = loudness * jnp.repeat(steps, extent[position] // parts).reshape([-1 if axis == position else 1 for axis in range(len(extent))])
    return loudness


def bell_draw(rng, extent, deviation, most, cuts=(), kind=jnp.bfloat16):
    level = block_levels(rng, extent, cuts, -0.22, 0.18) if cuts else 1.0
    result = jax.random.normal(rng, extent, jnp.float32) * deviation * level
    return jnp.minimum(jnp.maximum(result, -most), most).astype(kind)


def setup_inputs(seed: int = 0) -> dict:
    streams_of = jax.random.split(jax.random.key(seed), 7)
    return {
        "state_a": bell_draw(streams_of[0], (BATCH, CH, NY, NZ, NX), 1.0, 6.0, ((0, 4), (2, 2), (3, 4))),
        "state_b": bell_draw(streams_of[1], (BATCH, CH, NY, NZ, NX), 1.0, 6.0, ((0, 4), (2, 2), (3, 4))),
        "cotan_a": bell_draw(streams_of[2], (BATCH, CH, NY, NZ, NX), 1.0, 6.0, ((0, 4), (2, 2), (3, 4))),
        "cotan_b": bell_draw(streams_of[3], (BATCH, CH, NY, NZ, NX), 1.0, 6.0, ((0, 4), (2, 2), (3, 4))),
        "spectral_weight": bell_draw(streams_of[4], (MY, MZ, MX, 2, CH, CH), (2 * CH) ** -0.5, 1.0, ((0, 4), (2, 2))),
        "point_weight": bell_draw(streams_of[5], (CH, CH), CH ** -0.5, 1.5),
    }


HIGHEST = lax.Precision.HIGHEST

def kept_frequencies(length_all, length_kept):
    positions = jnp.arange(length_kept, dtype=jnp.int32)
    return jnp.where(positions < length_kept // 2, positions, length_all - length_kept + positions).astype(jnp.int32)

def forward_plain(field_in):
    along_x = jnp.fft.fft(field_in, axis=3)[:, :, :, :MX]
    along_y = jnp.take(jnp.fft.fft(along_x, axis=1), kept_frequencies(NY, MY), axis=1)
    along_z = jnp.take(jnp.fft.fft(along_y, axis=2), kept_frequencies(NZ, MZ), axis=2)
    return jnp.stack([jnp.real(along_z), jnp.imag(along_z)], axis=3)

def inverse_plain(spectrum):
    values = spectrum[:, :, :, 0] + 1j * spectrum[:, :, :, 1]
    chans = values.shape[0]
    full_z = jnp.zeros((chans, MY, NZ, MX), values.dtype).at[:, :, kept_frequencies(NZ, MZ)].set(values)
    back_z = jnp.fft.ifft(full_z, axis=2) * NZ
    full_y = jnp.zeros((chans, NY, NZ, MX), values.dtype).at[:, kept_frequencies(NY, MY)].set(back_z)
    back_y = jnp.fft.ifft(full_y, axis=1) * NY
    full_x = jnp.zeros((chans, NY, NZ, NX), values.dtype).at[:, :, :, :MX].set(back_y)
    return jnp.real(jnp.fft.ifft(full_x, axis=3)) * NX

def spectral_product(spectrum, weight):
    pattern = 'cjlk,jlkcd->djlk'
    real_in = spectrum[:, :, :, 0]
    imag_in = spectrum[:, :, :, 1]
    w_real = weight[:, :, :, 0]
    w_imag = weight[:, :, :, 1]
    out_real = jnp.einsum(pattern, real_in, w_real, precision=HIGHEST) - jnp.einsum(pattern, imag_in, w_imag, precision=HIGHEST)
    out_imag = jnp.einsum(pattern, real_in, w_imag, precision=HIGHEST) + jnp.einsum(pattern, imag_in, w_real, precision=HIGHEST)
    return jnp.stack([out_real, out_imag], axis=3)

def spectral_adjoint(back_spec, weight):
    pattern = 'djlk,jlkcd->cjlk'
    real_in = back_spec[:, :, :, 0]
    imag_in = back_spec[:, :, :, 1]
    w_real = weight[:, :, :, 0]
    w_imag = weight[:, :, :, 1]
    out_real = jnp.einsum(pattern, real_in, w_real, precision=HIGHEST) + jnp.einsum(pattern, imag_in, w_imag, precision=HIGHEST)
    out_imag = jnp.einsum(pattern, imag_in, w_real, precision=HIGHEST) - jnp.einsum(pattern, real_in, w_imag, precision=HIGHEST)
    return jnp.stack([out_real, out_imag], axis=3)

def spectral_outer(spectrum, back_spec):
    pattern = 'cjlk,djlk->jlkcd'
    spec_real = spectrum[:, :, :, 0]
    spec_imag = spectrum[:, :, :, 1]
    back_real = back_spec[:, :, :, 0]
    back_imag = back_spec[:, :, :, 1]
    grad_real = jnp.einsum(pattern, spec_real, back_real, precision=HIGHEST) + jnp.einsum(pattern, spec_imag, back_imag, precision=HIGHEST)
    grad_imag = jnp.einsum(pattern, spec_real, back_imag, precision=HIGHEST) - jnp.einsum(pattern, spec_imag, back_real, precision=HIGHEST)
    return jnp.stack([grad_real, grad_imag], axis=3)

def reference(state_a, state_b, cotan_a, cotan_b, spectral_weight, point_weight):
    samples = state_a.shape[0]
    scale_f = 1.0 / math.sqrt(NX * NY * NZ)
    scale_i = 1.0 / math.sqrt(MX * MY * MZ)
    grad_scale = math.sqrt(MX * MY * MZ / (samples * NX * NY * NZ))
    point_scale = 1.0 / math.sqrt(samples * NX * NY * NZ)
    weight = spectral_weight.astype(jnp.float32)
    pointwise = point_weight.astype(jnp.float32)
    rebuilt = []
    grads_second = []
    spectral_total = jnp.zeros(spectral_weight.shape, jnp.float32)
    point_total = jnp.zeros(point_weight.shape, jnp.float32)
    for sample in range(samples):
        field_wide = state_b[sample].astype(jnp.float32)
        spectrum = forward_plain(field_wide) * scale_f
        mixed_spec = spectral_product(spectrum, weight)
        local_point = jnp.einsum('cyzn,cd->dyzn', field_wide, pointwise, precision=HIGHEST)
        hidden = inverse_plain(mixed_spec) * scale_i + local_point
        activated, pullback = jax.vjp(jax.nn.gelu, hidden)
        rebuilt.append((state_a[sample].astype(jnp.float32) - activated).astype(jnp.bfloat16))
        slope_grad = pullback(cotan_a[sample].astype(jnp.float32))[0].astype(jnp.bfloat16)
        slope_wide = slope_grad.astype(jnp.float32)
        back_spec = forward_plain(slope_wide) * scale_i
        spectral_total = spectral_total + spectral_outer(spectrum, back_spec)
        spec_grad = spectral_adjoint(back_spec, weight)
        point_back = jnp.einsum('dyzn,cd->cyzn', slope_wide, pointwise, precision=HIGHEST)
        second = cotan_b[sample].astype(jnp.float32) + inverse_plain(spec_grad) * scale_f + point_back
        grads_second.append(second.astype(jnp.bfloat16))
        point_total = point_total + jnp.einsum('cyzn,dyzn->cd', field_wide, slope_wide, precision=HIGHEST)
    return (jnp.stack(rebuilt), jnp.stack(grads_second), spectral_total * grad_scale, point_total * point_scale)
```

```python
import math

import jax
import jax.numpy as jnp
import numpy as np
from jax import lax
from jax.experimental import pallas as pl
from jax.experimental.pallas import tpu as pltpu
from jax.sharding import PartitionSpec as P

MX = 32
MY = 32
MZ = 8
GROUP = 4
SUB = 16
LIMIT = 56 * 1024 * 1024
INTERPRET = False
F32 = jnp.float32
BF16 = jnp.bfloat16


def kept(length_all, length_kept, position):
    return jnp.where(position < length_kept // 2, position, length_all - length_kept + position)


def angle(product, length_all):
    return (product % length_all).astype(F32) * (2.0 * math.pi / length_all)


def synthesis_table(shape):
    ys, zs, ny, nz = shape
    mode = lax.broadcasted_iota(jnp.int32, (1, MY * MZ), 1)
    fy = kept(ny, MY, mode // MZ)
    fz = kept(nz, MZ, mode % MZ)
    y = lax.axis_index("px") * ys + lax.broadcasted_iota(jnp.int32, (ys, 1), 0)
    z = lax.axis_index("py") * zs + lax.broadcasted_iota(jnp.int32, (zs, 1), 0)
    ay = angle(fy * y, ny)
    az = angle(fz * z, nz)
    cy, sy = jnp.cos(ay)[:, None, :], jnp.sin(ay)[:, None, :]
    cz, sz = jnp.cos(az)[None], jnp.sin(az)[None]
    table = jnp.concatenate([cy * cz - sy * sz, -(sy * cz + cy * sz)], axis=2)
    return table.reshape(ys * zs, 2 * MY * MZ)


def analysis_table(shape):
    ys, zs, ny, nz = shape
    cell = lax.broadcasted_iota(jnp.int32, (1, ys * zs), 1)
    y = lax.axis_index("px") * ys + cell // zs
    z = lax.axis_index("py") * zs + cell % zs
    fy = kept(ny, MY, lax.broadcasted_iota(jnp.int32, (MY, 1), 0))
    fz = kept(nz, MZ, lax.broadcasted_iota(jnp.int32, (MZ, 1), 0))
    ay = angle(fy * y, ny)
    az = angle(fz * z, nz)
    cy, sy = jnp.cos(ay)[:, None, :], jnp.sin(ay)[:, None, :]
    cz, sz = jnp.cos(az)[None], jnp.sin(az)[None]
    table = jnp.stack([cy * cz - sy * sz, -(sy * cz + cy * sz)])
    return table.reshape(2 * MY * MZ, ys * zs)


def x_tables(px, nx):
    kk = MX // px
    k = np.arange(MX).reshape(px, kk)
    phase = 2.0 * np.pi / nx * (k[:, :, None] * np.arange(nx) % nx)
    cosine, sine = np.cos(phase), np.sin(phase)
    table = np.zeros((2, px, GROUP, 2, kk, GROUP, nx))
    for c in range(GROUP):
        table[0, :, c, 0, :, c] = cosine
        table[0, :, c, 1, :, c] = -sine
        table[1, :, c, 0, :, c] = sine
        table[1, :, c, 1, :, c] = cosine
    table = table.reshape(2, 2 * MX * GROUP, GROUP * nx)
    high = table.astype(BF16)
    low = (table - high.astype(np.float64)).astype(BF16)
    return high, low


def dot(a, b):
    return jnp.dot(a, b, preferred_element_type=F32)


def cut(value):
    high = value.astype(BF16)
    return high, (value - high.astype(F32)).astype(BF16)


def dot3(a, high, low):
    ahigh, alow = cut(a)
    return dot(ahigh, high) + dot(alow, high) + dot(ahigh, low)


def to_modes(b0, b1, xh_ref, xl_ref):
    return dot3(b0, xh_ref[0], xl_ref[0]) + dot3(b1, xh_ref[1], xl_ref[1])


def store_modes(out_ref, group, value, px, py):
    wide = value.shape[1] // px
    tall = value.shape[0] // py
    for i in range(px):
        for j in range(py):
            out_ref[i * py + j, group] = value[j * tall : (j + 1) * tall, i * wide : (i + 1) * wide]


def build_fields(spec_ref, xh_ref, xl_ref, gh_ref, px, py):
    modes = MY * MZ
    for g in range(spec_ref.shape[1]):
        rows = []
        for j in range(py):
            rows.append(jnp.concatenate([spec_ref[i * py + j, g] for i in range(px)], axis=1))
        value = jnp.concatenate(rows, axis=0)
        for t in range(2):
            high = dot3(value, xh_ref[t], xl_ref[t]).astype(BF16)
            half = high.shape[1] // 2
            for h in range(2):
                gh_ref[2 * g + h, t * modes : (t + 1) * modes] = high[:, h * half : (h + 1) * half]


def pair_of(ref, start):
    chans, _, nx = ref.shape
    first = ref[:, pl.ds(start, SUB), :].reshape(chans * SUB, nx)
    second = ref[:, pl.ds(start + SUB, SUB), :].reshape(chans * SUB, nx)
    return jnp.concatenate([first, second], axis=1)


def channel_mix(kron_ref, in_ref, out_ref):
    chans, rows, nx = in_ref.shape

    def body(q, carry):
        start = pl.multiple_of(q * 2 * SUB, 2 * SUB)
        value = dot(kron_ref[...], pair_of(in_ref, start))
        out_ref[:, pl.ds(start, SUB), :] = value[:, :nx].reshape(chans, SUB, nx)
        out_ref[:, pl.ds(start + SUB, SUB), :] = value[:, nx:].reshape(chans, SUB, nx)
        return carry

    lax.fori_loop(0, rows // (2 * SUB), body, 0)


def position(py):
    return lax.axis_index("px") * py + lax.axis_index("py")


def partner(px, py, offset):
    other = lax.rem(position(py) + offset, px * py)
    return other, {"px": lax.div(other, py), "py": lax.rem(other, py)}


def greet(px, py):
    barrier = pltpu.get_barrier_semaphore()
    for offset in range(1, px * py):
        pl.semaphore_signal(
            barrier, inc=1, device_id=partner(px, py, offset)[1], device_id_type=pl.DeviceIdType.MESH
        )
    pl.semaphore_wait(barrier, px * py - 1)


def scatter_copy(px, py, offset, group, part_ref, land_ref, send_sem, recv_sem):
    other, device = partner(px, py, offset)
    return pltpu.make_async_remote_copy(
        part_ref.at[other, group], land_ref.at[offset, group], send_sem.at[offset, group], recv_sem.at[offset, group],
        device_id=device, device_id_type=pl.DeviceIdType.MESH,
    )


def scatter_kernel(px, py, part_ref, out_ref, land_ref, send_sem, recv_sem):
    count = px * py
    greet(px, py)
    groups = part_ref.shape[1]
    for g in range(groups):
        for offset in range(1, count):
            scatter_copy(px, py, offset, g, part_ref, land_ref, send_sem, recv_sem).start()
    out_ref[...] = part_ref[position(py)]
    for g in range(groups):
        for offset in range(1, count):
            scatter_copy(px, py, offset, g, part_ref, land_ref, send_sem, recv_sem).wait()
            out_ref[g] += land_ref[offset, g]


def gather_kernel(px, py, own_ref, out_ref, land_ref, send_sem, recv_sem):
    count = px * py
    greet(px, py)
    copies = []
    for offset in range(1, count):
        copies.append(
            pltpu.make_async_remote_copy(
                own_ref, land_ref.at[offset], send_sem.at[offset], recv_sem.at[offset],
                device_id=partner(px, py, offset)[1], device_id_type=pl.DeviceIdType.MESH,
            )
        )
        copies[-1].start()
    here = position(py)
    out_ref[here] = own_ref[...]
    for offset in range(1, count):
        copies[offset - 1].wait()
        out_ref[lax.rem(here + count - offset, count)] = land_ref[offset]


def mix_kernel(s_ref, w_ref, out_ref):
    chans = s_ref.shape[1]
    real = jnp.zeros(out_ref.shape[1:], F32)
    imag = jnp.zeros(out_ref.shape[1:], F32)
    for c in range(chans):
        s_real, s_imag = s_ref[0, c : c + 1], s_ref[1, c : c + 1]
        w_real, w_imag = w_ref[0, c].astype(F32), w_ref[1, c].astype(F32)
        real += s_real * w_real - s_imag * w_imag
        imag += s_real * w_imag + s_imag * w_real
    out_ref[0] = real
    out_ref[1] = imag


def adjoint_kernel(b_ref, w_ref, out_ref):
    b_real, b_imag = b_ref[0], b_ref[1]
    for c in range(w_ref.shape[1]):
        w_real, w_imag = w_ref[0, c].astype(F32), w_ref[1, c].astype(F32)
        out_ref[0, c : c + 1] = jnp.sum(b_real * w_real + b_imag * w_imag, axis=0, keepdims=True)
        out_ref[1, c : c + 1] = jnp.sum(b_imag * w_real - b_real * w_imag, axis=0, keepdims=True)


def forward_kernel(
    px, py, v_ref, th_ref, xh_ref, xl_ref, out_ref, part_ref, land_ref, send_sem, recv_sem
):
    modes = MY * MZ
    parts = []
    for p in range(GROUP // 2):
        value = jnp.concatenate([v_ref[2 * p], v_ref[2 * p + 1]], axis=1)
        parts.append(dot(th_ref[...], value))
    b0 = jnp.concatenate([part[:modes] for part in parts], axis=1)
    b1 = jnp.concatenate([part[modes:] for part in parts], axis=1)
    step = pl.program_id(0)
    store_modes(part_ref, step, to_modes(b0, b1, xh_ref, xl_ref), px, py)
    count = px * py

    @pl.when(step == 0)
    def _():
        greet(px, py)

    for offset in range(1, count):
        scatter_copy(px, py, offset, step, part_ref, land_ref, send_sem, recv_sem).start()

    @pl.when(step == pl.num_programs(0) - 1)
    def _():
        out_ref[...] = part_ref[position(py)]
        for g in range(part_ref.shape[1]):
            for offset in range(1, count):
                scatter_copy(px, py, offset, g, part_ref, land_ref, send_sem, recv_sem).wait()
                out_ref[g] += land_ref[offset, g]


def middle_kernel(
    px, py, steps, spec_ref, vb_ref, va_ref, ca_ref, uh_ref, th_ref, xh_ref, xl_ref, fh_ref, fl_ref,
    kron_ref, ia_ref, sl_ref, back_ref, point_ref, gh_ref, acc_ref, mix_ref,
):
    step = pl.program_id(0)
    modes = MY * MZ
    nx = vb_ref.shape[2]
    chans, rows = vb_ref.shape[:2]

    @pl.when(step == 0)
    def _():
        build_fields(spec_ref, xh_ref, xl_ref, gh_ref, px, py)
        acc_ref[...] = jnp.zeros_like(acc_ref)
        point_ref[...] = jnp.zeros_like(point_ref)

    channel_mix(kron_ref, vb_ref, mix_ref)
    c0 = math.sqrt(2.0 / math.pi)

    def body(p, carry):
        field = dot(uh_ref[...], gh_ref[p])
        slopes = []
        for h in range(2):
            d = 2 * p + h
            v = field[:, h * nx : (h + 1) * nx] + mix_ref[d]
            v2 = v * v
            t = jnp.tanh(v * (c0 + (c0 * 0.044715) * v2))
            half = 0.5 + 0.5 * t
            ia_ref[d] = (va_ref[d].astype(F32) - v * half).astype(BF16)
            deriv = half + (0.5 * v) * (1.0 - t * t) * (c0 + (3.0 * c0 * 0.044715) * v2)
            slope = (ca_ref[d].astype(F32) * deriv).astype(BF16)
            sl_ref[d] = slope
            slopes.append(slope)
        both = jnp.concatenate(slopes, axis=1)
        acc_ref[p] += dot(th_ref[...], both)
        return carry

    lax.fori_loop(0, chans // 2, body, 0)

    def point_body(q, carry):
        start = pl.multiple_of(q * 2 * SUB, 2 * SUB)
        point_ref[...] += lax.dot_general(
            pair_of(vb_ref, start), pair_of(sl_ref, start), (((1,), (1,)), ((), ())), preferred_element_type=F32
        )
        return carry

    lax.fori_loop(0, rows // (2 * SUB), point_body, 0)

    @pl.when(step == steps - 1)
    def _():
        for g in range(chans // GROUP):
            parts = [acc_ref[2 * g + h] for h in range(2)]
            b0 = jnp.concatenate([part[:modes] for part in parts], axis=1)
            b1 = jnp.concatenate([part[modes:] for part in parts], axis=1)
            store_modes(back_ref, g, to_modes(b0, b1, fh_ref, fl_ref), px, py)


def last_kernel(
    px, py, spec_ref, sl_ref, cb_ref, uh_ref, xh_ref, xl_ref, kron_ref, out_ref, gh_ref, mix_ref
):
    nx = sl_ref.shape[2]

    @pl.when(pl.program_id(0) == 0)
    def _():
        build_fields(spec_ref, xh_ref, xl_ref, gh_ref, px, py)

    channel_mix(kron_ref, sl_ref, mix_ref)

    def body(p, carry):
        field = dot(uh_ref[...], gh_ref[p])
        for h in range(2):
            d = 2 * p + h
            value = cb_ref[d].astype(F32) + field[:, h * nx : (h + 1) * nx] + mix_ref[d]
            out_ref[d] = value.astype(BF16)
        return carry

    lax.fori_loop(0, sl_ref.shape[0] // 2, body, 0)


def whole(shape):
    return pl.BlockSpec(shape, lambda i: (0,) * len(shape), pipeline_mode=pl.Buffered(1))


def general_device(state_a, state_b, cotan_a, cotan_b, spectral_weight, point_weight):
    samples, px, py = (lax.axis_size(name) for name in ("dp", "px", "py"))
    _, chans, ys, zs, nx = state_b.shape
    ny, nz = ys * px, zs * py
    cells, modes = ys * zs, MY * MZ
    groups = chans // GROUP
    kk = MX // px
    tall, wide = modes // py, 2 * MX * GROUP // px
    own = tall * kk
    scale_f = 1.0 / math.sqrt(nx * ny * nz)
    scale_i = 1.0 / math.sqrt(MX * MY * MZ)
    grad_scale = math.sqrt(MX * MY * MZ / (samples * nx * ny * nz))
    point_scale = 1.0 / math.sqrt(samples * nx * ny * nz)
    shape = (ys, zs, ny, nz)
    th = analysis_table(shape).astype(BF16)
    uh = synthesis_table(shape).astype(BF16)
    xh, xl = x_tables(px, nx)
    fh, fl = (jnp.asarray(np.ascontiguousarray(table.transpose(0, 2, 1))) for table in (xh, xl))
    xh, xl = jnp.asarray(xh), jnp.asarray(xl)
    eye = jnp.eye(SUB, dtype=BF16)
    kron_f = (point_weight.T[:, None, :, None] * eye[None, :, None, :]).reshape(chans * SUB, chans * SUB)
    kron_b = (point_weight[:, None, :, None] * eye[None, :, None, :]).reshape(chans * SUB, chans * SUB)
    field_a, field_b, cot_a, cot_b = (
        value.reshape(chans, cells, nx) for value in (state_a, state_b, cotan_a, cotan_b)
    )
    part_shape = jax.ShapeDtypeStruct((px * py, groups, tall, wide), F32)
    params = pltpu.CompilerParams(vmem_limit_bytes=LIMIT)

    count = px * py
    own_shape = jax.ShapeDtypeStruct((groups, tall, wide), F32)
    exchange = [
        pltpu.VMEM(part_shape.shape, F32),
        pltpu.SemaphoreType.DMA((count, groups)),
        pltpu.SemaphoreType.DMA((count, groups)),
    ]

    def linked(number):
        return pltpu.CompilerParams(vmem_limit_bytes=LIMIT, collective_id=number, has_side_effects=True)

    def to_channels(value):
        value = value.reshape(groups, tall, GROUP, 2, kk).transpose(3, 0, 2, 1, 4)
        return value.reshape(2, chans, own)

    def gather(value, number):
        value = value.reshape(2, groups, GROUP, tall, kk).transpose(1, 3, 2, 0, 4)
        value = value.reshape(groups, tall, wide)
        return pl.pallas_call(
            lambda *refs: gather_kernel(px, py, *refs),
            in_specs=[pl.BlockSpec(memory_space=pltpu.VMEM)],
            out_specs=pl.BlockSpec(memory_space=pltpu.VMEM),
            out_shape=part_shape,
            scratch_shapes=[
                pltpu.VMEM(part_shape.shape, F32), pltpu.SemaphoreType.DMA((count,)), pltpu.SemaphoreType.DMA((count,)),
            ],
            compiler_params=linked(number),
            interpret=INTERPRET,
            name="gather",
        )(value)

    def mode_product(kernel, value, name):
        return pl.pallas_call(
            kernel,
            out_shape=jax.ShapeDtypeStruct((2, chans, own), F32),
            compiler_params=params,
            interpret=INTERPRET,
            name=name,
        )(value, weight)

    spectrum = pl.pallas_call(
        lambda *refs: forward_kernel(px, py, *refs),
        grid=(groups,),
        in_specs=[
            pl.BlockSpec((GROUP, cells, nx), lambda i: (i, 0, 0)),
            whole(th.shape), whole(fh.shape), whole(fl.shape),
        ],
        out_specs=whole(own_shape.shape),
        out_shape=own_shape,
        scratch_shapes=[pltpu.VMEM(part_shape.shape, F32)] + exchange,
        compiler_params=linked(0),
        interpret=INTERPRET,
        name="forward",
    )(field_b, th, fh, fl)
    weight = spectral_weight.transpose(3, 4, 5, 0, 1, 2).reshape(2, chans, chans, own)
    spectrum = to_channels(spectrum) * scale_f
    mixed = gather(mode_product(mix_kernel, spectrum, "mix") * scale_i, 1)

    rows = min(256, cells)
    steps = cells // rows
    block = pl.BlockSpec((chans, rows, nx), lambda i: (0, i, 0))
    u_block = pl.BlockSpec((rows, 2 * modes), lambda i: (i, 0))
    t_block = pl.BlockSpec((2 * modes, rows), lambda i: (0, i))
    field_shape = jax.ShapeDtypeStruct((chans, cells, nx), BF16)
    side = chans * SUB
    g_scratch = [pltpu.VMEM((chans // 2, 2 * modes, 2 * nx), BF16)]
    input_a, slope, back_part, point = pl.pallas_call(
        lambda *refs: middle_kernel(px, py, steps, *refs),
        grid=(steps,),
        in_specs=[
            whole(part_shape.shape), block, block, block, u_block, t_block,
            whole(xh.shape), whole(xl.shape), whole(fh.shape), whole(fl.shape), whole((side, side)),
        ],
        out_specs=[block, block, whole(part_shape.shape), whole((side, side))],
        out_shape=[field_shape, field_shape, part_shape, jax.ShapeDtypeStruct((side, side), F32)],
        scratch_shapes=g_scratch
        + [pltpu.VMEM((chans // 2, 2 * modes, 2 * nx), F32), pltpu.VMEM((chans, rows, nx), F32)],
        compiler_params=params,
        interpret=INTERPRET,
        name="middle",
    )(mixed, field_b, field_a, cot_a, uh, th, xh, xl, fh, fl, kron_f)

    back = pl.pallas_call(
        lambda *refs: scatter_kernel(px, py, *refs),
        in_specs=[pl.BlockSpec(memory_space=pltpu.VMEM)],
        out_specs=pl.BlockSpec(memory_space=pltpu.VMEM),
        out_shape=own_shape,
        scratch_shapes=exchange,
        compiler_params=linked(2),
        interpret=INTERPRET,
        name="scatter",
    )(back_part)
    back = to_channels(back) * scale_i
    grad_spec = gather(mode_product(adjoint_kernel, back, "adjoint") * scale_f, 3)
    grad_b = pl.pallas_call(
        lambda *refs: last_kernel(px, py, *refs),
        grid=(steps,),
        in_specs=[
            whole(part_shape.shape), block, block, u_block,
            whole(xh.shape), whole(xl.shape), whole((side, side)),
        ],
        out_specs=block,
        out_shape=field_shape,
        scratch_shapes=g_scratch + [pltpu.VMEM((chans, rows, nx), F32)],
        compiler_params=params,
        interpret=INTERPRET,
        name="last",
    )(grad_spec, slope, cot_b, uh, xh, xl, kron_b)

    share = chans // samples
    spec_all = lax.all_gather(spectrum, "dp", axis=0)
    back_all = lax.all_gather(back, "dp", axis=0)
    back_own = lax.dynamic_slice_in_dim(back_all, lax.axis_index("dp") * share, share, axis=2)
    p_real, p_imag = spec_all[:, 0, :, None], spec_all[:, 1, :, None]
    q_real, q_imag = back_own[:, 0, None], back_own[:, 1, None]
    grad_real = jnp.sum(p_real * q_real + p_imag * q_imag, axis=0)
    grad_imag = jnp.sum(p_real * q_imag - p_imag * q_real, axis=0)
    grad = jnp.stack([grad_real, grad_imag]) * grad_scale
    spectral_grad = grad.reshape(2, chans, share, tall // MZ, MZ, kk).transpose(3, 4, 5, 0, 1, 2)

    point = jnp.sum(point.reshape(chans, SUB, chans, SUB) * jnp.eye(SUB, dtype=F32)[None, :, None, :], axis=(1, 3))
    point_total = lax.psum(point, ("dp", "px", "py")) * point_scale
    full = state_b.shape
    return (input_a.reshape(full), grad_b.reshape(full), spectral_grad, point_total)


MESH = pl.DeviceIdType.MESH
CHUNK = 1024
FUSED_LIMIT = 62 * 1024 * 1024


def fused_fits(shape, local_samples, samples, px, py):
    _, chans, ys, zs, nx = shape
    kk = MX // px
    tall = MY * MZ // py
    return (
        local_samples == 1
        and 2 * kk * GROUP == 128
        and nx == 128
        and MZ == 8
        and tall // MZ == 128 // kk
        and samples * GROUP == chans
        and (ys * zs) % CHUNK == 0
    )


def base_tables(shape):
    ys, zs, ny, nz = shape
    fy = np.where(np.arange(MY) < MY // 2, np.arange(MY), ny - MY + np.arange(MY))
    fz = np.where(np.arange(MZ) < MZ // 2, np.arange(MZ), nz - MZ + np.arange(MZ))
    ay = 2.0 * np.pi / ny * (fy[:, None] * np.arange(ys) % ny)
    az = 2.0 * np.pi / nz * (fz[:, None] * np.arange(zs) % nz)
    both = ay[:, None, :, None] + az[None, :, None, :]
    table = np.stack([np.cos(both), -np.sin(both)]).reshape(2 * MY * MZ, ys * zs).astype(BF16)
    py = 2.0 * np.pi / ny * (fy[None] * (np.arange(ny // ys) * ys)[:, None] % ny)
    pz = 2.0 * np.pi / nz * (fz[None] * (np.arange(nz // zs) * zs)[:, None] % nz)
    turn = py[:, None, :, None] + pz[None, :, None, :]
    turn = np.stack([np.cos(turn), np.sin(turn)], axis=2).reshape(-1, 2, MY * MZ, 1)
    turn = np.broadcast_to(turn, turn.shape[:3] + (128,)).astype(np.float32)
    return table, np.ascontiguousarray(table.T), np.ascontiguousarray(turn)


def wide_tables(px, nx):
    high, low = x_tables(px, nx)
    inverse = [np.concatenate([t[0], t[1]], axis=1) for t in (high, low)]
    forward = [np.ascontiguousarray(t.T) for t in inverse]
    return forward, inverse


def flip(tiles):
    width = 128 // len(tiles)
    block = lax.broadcasted_iota(jnp.int32, tiles[0].shape, 1) // width
    out = []
    for q in range(len(tiles)):
        value = tiles[q]
        for i, tile in enumerate(tiles):
            if i != q:
                value = jnp.where(block == i, pltpu.roll(tile, (i - q) * width % 128, 1), value)
        out.append(value)
    return out


def gelu_pair(v, first, cotan):
    c0 = math.sqrt(2.0 / math.pi)
    v2 = v * v
    half = 0.5 + 0.5 * jnp.tanh(v * (c0 + (c0 * 0.044715) * v2))
    rebuilt = (first.astype(F32) - v * half).astype(BF16)
    inner = v * (2.0 * c0 + (6.0 * c0 * 0.044715) * v2)
    slope = (cotan.astype(F32) * (half + (half * (1.0 - half)) * inner)).astype(BF16)
    return rebuilt, slope


def fused_kernel(
    scales, sb_hbm, sa_hbm, ca_hbm, cb_hbm, th_hbm, uh_hbm, fh_hbm, fl_hbm, xh_hbm, xl_hbm, kf_hbm, kb_hbm, w_hbm,
    turn_hbm, ia_hbm, gb_hbm, sg_ref, pt_ref,
    sb, fa, fc, mix, th, uh, fh, fl, xh, xl, kf, kb, w, turn, part, land_x, land_y, gath, spec, spec_land, back,
    back_land, gf, acc, point, pt_src, pt_land,
    in_sem, sb_sem, sa_sem, ca_sem, cb_sem, ia_sem, gb_sem, rx_s, rx_r, ry_s, ry_r, gy_s, gy_r, gx_s, gx_r,
    dp_s, dp_r, pt_s, pt_r,
):
    scale_f, scale_i, grad_scale = scales
    groups = part.shape[2]
    py = part.shape[3]
    tall = part.shape[4]
    cells, nx = sb.shape[1:]
    samples = spec_land.shape[0] + 1
    modes = MY * MZ
    ix, iy, idp = lax.axis_index("px"), lax.axis_index("py"), lax.axis_index("dp")
    other_x = 1 - ix

    def near_y(offset):
        return lax.rem(iy + offset, py)

    def near_dp(offset):
        return lax.rem(idp + offset, samples)

    def chan(g):
        return pl.ds(g * GROUP, GROUP)

    def load(index, src, dst):
        return pltpu.make_async_copy(src, dst, in_sem.at[index])

    tables = [
        load(0, th_hbm, th), load(1, fh_hbm, fh), load(2, fl_hbm, fl),
        load(3, turn_hbm.at[ix * py + iy], turn), load(4, kf_hbm, kf), load(5, w_hbm, w), load(6, xh_hbm, xh),
        load(7, xl_hbm, xl), load(8, uh_hbm, uh), load(9, kb_hbm, kb),
    ]

    def field_load(src, dst, sem, g):
        return pltpu.make_async_copy(src.at[chan(g)], dst.at[chan(g)], sem.at[g])

    barrier = pltpu.get_barrier_semaphore()
    pl.semaphore_signal(barrier, inc=1, device_id={"px": other_x}, device_id_type=MESH)
    for offset in range(1, py):
        pl.semaphore_signal(barrier, inc=1, device_id={"py": near_y(offset)}, device_id_type=MESH)
    for offset in range(1, samples):
        pl.semaphore_signal(barrier, inc=1, device_id={"dp": near_dp(offset)}, device_id_type=MESH)

    field_load(sb_hbm, sb, sb_sem, 0).start()
    for i in range(4):
        tables[i].start()
    for g in range(1, groups):
        field_load(sb_hbm, sb, sb_sem, g).start()
    for i in range(4, len(tables)):
        tables[i].start()
    for g in range(groups):
        field_load(sa_hbm, fa, sa_sem, g).start()
        field_load(ca_hbm, fc, ca_sem, g).start()
    pl.semaphore_wait(barrier, 1 + (py - 1) + (samples - 1))

    def remote(src, dst, send, recv, device):
        return pltpu.make_async_remote_copy(src, dst, send, recv, device_id=device, device_id_type=MESH)

    def reduce_x(f, g):
        return remote(
            part.at[f, other_x, g], land_x.at[f, g], rx_s.at[f, g], rx_r.at[f, g], {"px": other_x}
        )

    def reduce_y(f, g, offset):
        to = near_y(offset)
        return remote(
            part.at[f, ix, g, to], land_y.at[f, offset - 1, g], ry_s.at[f, offset - 1, g], ry_r.at[f, offset - 1, g],
            {"py": to},
        )

    def gather_y(f, g, offset):
        block = gath.at[f, ix, iy, g]
        return remote(block, block, gy_s.at[f, offset - 1, g], gy_r.at[f, offset - 1, g], {"py": near_y(offset)})

    def gather_x(f, g, offset):
        block = gath.at[f, ix, lax.rem(iy + py - offset, py), g]
        return remote(block, block, gx_s.at[f, offset, g], gx_r.at[f, offset, g], {"px": other_x})

    def after_x(f, g):
        reduce_x(f, g).wait_recv()
        part[f, ix, g] += land_x[f, g]
        for offset in range(1, py):
            reduce_y(f, g, offset).start()

    def finish_reduce(f, g):
        for offset in range(1, py):
            reduce_y(f, g, offset).wait_recv()
        value = part[f, ix, g, iy]
        for offset in range(1, py):
            value = value + land_y[f, offset - 1, g]
        return flip([value[8 * i : 8 * i + 8] for i in range(tall // 8)])

    def end_reduce_sends(f):
        for g in range(groups):
            reduce_x(f, g).wait_send()
            for offset in range(1, py):
                reduce_y(f, g, offset).wait_send()

    def start_gather(f, g, tiles):
        for i, tile in enumerate(flip(tiles)):
            gath[f, ix, iy, g, 8 * i : 8 * i + 8] = tile
        for offset in range(1, py):
            gather_y(f, g, offset).start()
        gather_x(f, g, 0).start()

    def forward_gather(f, g):
        for offset in range(1, py):
            gather_y(f, g, offset).wait_recv()
            gather_x(f, g, offset).start()

    def finish_gather(f, g):
        for offset in range(py):
            gather_x(f, g, offset).wait_recv()

    def end_gather_sends(f):
        for g in range(groups):
            for offset in range(1, py):
                gather_y(f, g, offset).wait_send()
            for offset in range(py):
                gather_x(f, g, offset).wait_send()

    def turns():
        cosine = jnp.concatenate([turn[0]] * GROUP, axis=1)
        sine = jnp.concatenate([turn[1]] * GROUP, axis=1)
        return cosine, sine

    def analyse(src, first, slot):
        value = jnp.concatenate([src[first], src[first + 1]], axis=1)
        acc[slot] = dot(th[...], value)

    def to_part(f, g):
        cosine, sine = turns()
        b0 = jnp.concatenate([acc[0, :modes], acc[1, :modes]], axis=1)
        b1 = jnp.concatenate([acc[0, modes:], acc[1, modes:]], axis=1)
        both = jnp.concatenate([b0 * cosine + b1 * sine, b1 * cosine - b0 * sine], axis=1)
        value = dot3(both, fh[...], fl[...])
        for i in range(2):
            part[f, i, g] = value[:, i * 128 : (i + 1) * 128].reshape(py, tall, 128)

    def build(f, g):
        value = jnp.concatenate([gath[f, i, :, g].reshape(modes, 128) for i in range(2)], axis=1)
        high, low = cut(value)
        cosine, sine = turns()
        wide = GROUP * nx
        both = dot(high, xh[...]) + dot(low, xh[...]) + dot(high, xl[...])
        g0, g1 = both[:, :wide], both[:, wide:]
        for t, field in enumerate((g0 * cosine - g1 * sine, g1 * cosine + g0 * sine)):
            field = field.astype(BF16)
            for h in range(2):
                gf[h, t * modes : (t + 1) * modes] = field[:, h * 2 * nx : (h + 1) * 2 * nx]

    def mix_rows(table, src, lo, hi):
        def step(q, carry):
            start = pl.multiple_of(q * 2 * SUB, 2 * SUB)
            value = dot(table[...], pair_of(src, start))
            mix[:, pl.ds(start, SUB), :] = value[:, :nx].reshape(-1, SUB, nx)
            mix[:, pl.ds(start + SUB, SUB), :] = value[:, nx:].reshape(-1, SUB, nx)
            return carry

        lax.fori_loop(lo, hi, step, 0)

    steps = cells // (2 * SUB)

    for i in range(4):
        tables[i].wait()

    def forward(g, carry):
        field_load(sb_hbm, sb, sb_sem, g).wait()
        for p in range(2):
            analyse(sb, g * GROUP + 2 * p, p)
        to_part(0, g)
        reduce_x(0, g).start()

        @pl.when(g >= 1)
        def _():
            after_x(0, g - 1)

        return carry

    lax.fori_loop(0, groups, forward, 0)
    tables[4].wait()
    mix_rows(kf, sb, 0, steps // 2)
    after_x(0, groups - 1)
    mix_rows(kf, sb, steps // 2, steps)

    def take_spectrum(g, carry):
        tiles = finish_reduce(0, g)
        for q, tile in enumerate(tiles):
            spec[q % 2, g * GROUP + q // 2] = tile * scale_f
        return carry

    lax.fori_loop(0, groups, take_spectrum, 0)
    tables[5].wait()

    def blend(g, carry):
        real = jnp.zeros((GROUP, 8, 128), F32)
        imag = jnp.zeros((GROUP, 8, 128), F32)
        rows = pl.ds(pl.multiple_of(g * GROUP * 8, GROUP * 8), GROUP * 8)
        for c in range(spec.shape[1]):
            w_real = w[0, c, rows, :].astype(F32).reshape(GROUP, 8, 128)
            w_imag = w[1, c, rows, :].astype(F32).reshape(GROUP, 8, 128)
            s_real, s_imag = spec[0, c][None], spec[1, c][None]
            real += s_real * w_real - s_imag * w_imag
            imag += s_real * w_imag + s_imag * w_real
        tiles = []
        for q in range(2 * GROUP):
            tiles.append((imag if q % 2 else real)[q // 2] * scale_i)
        start_gather(0, g, tiles)
        return carry

    lax.fori_loop(0, groups, blend, 0)

    def send_spec(offset):
        return remote(
            spec, spec_land.at[offset - 1], dp_s.at[0, offset - 1], dp_r.at[0, offset - 1], {"dp": near_dp(offset)}
        )

    def send_back(offset):
        to = near_dp(offset)
        return remote(
            back.at[to], back_land.at[offset - 1], dp_s.at[1, offset - 1], dp_r.at[1, offset - 1], {"dp": to}
        )

    for offset in range(1, samples):
        send_spec(offset).start()
    end_reduce_sends(0)
    for i in range(6, len(tables)):
        tables[i].wait()
    forward_gather(0, 0)

    def middle(g, carry):
        @pl.when(g + 1 < groups)
        def _():
            forward_gather(0, g + 1)

        finish_gather(0, g)
        build(0, g)
        field_load(sa_hbm, fa, sa_sem, g).wait()
        field_load(ca_hbm, fc, ca_sem, g).wait()

        def pair(p, inner):
            first = g * GROUP + 2 * p

            def rows(r, deep):
                some = pl.ds(pl.multiple_of(r * CHUNK, CHUNK), CHUNK)
                field = dot(uh[some, :], gf[p])
                for h in range(2):
                    v = field[:, h * nx : (h + 1) * nx] + mix[first + h, some, :]
                    rebuilt, slope = gelu_pair(v, fa[first + h, some, :], fc[first + h, some, :])
                    fa[first + h, some, :] = rebuilt
                    fc[first + h, some, :] = slope
                return deep

            lax.fori_loop(0, cells // CHUNK, rows, 0)
            analyse(fc, first, p)
            return inner

        lax.fori_loop(0, 2, pair, 0)
        pltpu.make_async_copy(fa.at[chan(g)], ia_hbm.at[chan(g)], ia_sem.at[g]).start()
        to_part(1, g)
        reduce_x(1, g).start()

        @pl.when(g >= 1)
        def _():
            after_x(1, g - 1)

        return carry

    lax.fori_loop(0, groups, middle, 0)
    end_gather_sends(0)

    point[...] = jnp.zeros_like(point)

    def point_rows(lo, hi):
        def step(q, carry):
            start = pl.multiple_of(q * 4 * SUB, 4 * SUB)
            left = jnp.concatenate([pair_of(sb, start), pair_of(sb, start + 2 * SUB)], axis=1)
            right = jnp.concatenate([pair_of(fc, start), pair_of(fc, start + 2 * SUB)], axis=1)
            point[...] += lax.dot_general(left, right, (((1,), (1,)), ((), ())), preferred_element_type=F32)
            return carry

        lax.fori_loop(lo, hi, step, 0)

    point_rows(0, steps // 4)
    after_x(1, groups - 1)
    point_rows(steps // 4, steps // 2)
    row = lax.broadcasted_iota(jnp.int32, point.shape, 0)
    column = lax.broadcasted_iota(jnp.int32, point.shape, 1)
    diagonal = jnp.where(row % SUB == column % SUB, point[...], 0.0)
    pt_src[0] = jnp.sum(diagonal.reshape(-1, SUB, point.shape[1]), axis=1)

    def sum_x():
        return remote(pt_src.at[0], pt_land.at[0, 0], pt_s.at[0], pt_r.at[0], {"px": other_x})

    def sum_y(offset):
        return remote(
            pt_src.at[1], pt_land.at[1, iy], pt_s.at[offset], pt_r.at[offset], {"py": near_y(offset)}
        )

    def sum_dp(offset):
        return remote(
            pt_src.at[2], pt_land.at[2, idp], pt_s.at[py - 1 + offset], pt_r.at[py - 1 + offset],
            {"dp": near_dp(offset)},
        )

    sum_x().start()

    def take_back(g, carry):
        tiles = finish_reduce(1, g)
        for q, tile in enumerate(tiles):
            back[g, q % 2, q // 2] = tile * scale_i
        return carry

    lax.fori_loop(0, groups, take_back, 0)

    def adjoint(g, carry):
        tiles = []
        for c in range(GROUP):
            real = jnp.zeros((8, 128), F32)
            imag = jnp.zeros((8, 128), F32)
            w_real = w[0, g * GROUP + c].astype(F32).reshape(-1, 8, 128)
            w_imag = w[1, g * GROUP + c].astype(F32).reshape(-1, 8, 128)
            for s in range(back.shape[0]):
                for d in range(GROUP):
                    b_real, b_imag = back[s, 0, d], back[s, 1, d]
                    real += b_real * w_real[s * GROUP + d] + b_imag * w_imag[s * GROUP + d]
                    imag += b_imag * w_real[s * GROUP + d] - b_real * w_imag[s * GROUP + d]
            tiles += [real * scale_f, imag * scale_f]
        start_gather(1, g, tiles)
        return carry

    lax.fori_loop(0, groups, adjoint, 0)
    for offset in range(1, samples):
        send_back(offset).start()
    for g in range(groups):
        pltpu.make_async_copy(fa.at[chan(g)], ia_hbm.at[chan(g)], ia_sem.at[g]).wait()
        field_load(cb_hbm, fa, cb_sem, g).start()
    sum_x().wait()
    pt_src[1] = pt_src[0] + pt_land[0, 0]
    pt_land[1, iy] = pt_src[1]
    for offset in range(1, py):
        sum_y(offset).start()
    mix_rows(kb, fc, 0, steps // 2)
    forward_gather(1, 0)
    for offset in range(1, py):
        sum_y(offset).wait()
    pt_src[2] = sum(pt_land[1, i] for i in range(py))
    pt_land[2, idp] = pt_src[2]
    for offset in range(1, samples):
        sum_dp(offset).start()
    mix_rows(kb, fc, steps // 2, steps)

    def last(g, carry):
        @pl.when(g + 1 < groups)
        def _():
            forward_gather(1, g + 1)

        finish_gather(1, g)
        build(1, g)
        field_load(cb_hbm, fa, cb_sem, g).wait()

        def pair(p, inner):
            first = g * GROUP + 2 * p

            def rows(r, deep):
                some = pl.ds(pl.multiple_of(r * CHUNK, CHUNK), CHUNK)
                field = dot(uh[some, :], gf[p])
                for h in range(2):
                    value = fa[first + h, some, :].astype(F32) + field[:, h * nx : (h + 1) * nx]
                    fa[first + h, some, :] = (value + mix[first + h, some, :]).astype(BF16)
                return deep

            lax.fori_loop(0, cells // CHUNK, rows, 0)
            return inner

        lax.fori_loop(0, 2, pair, 0)
        pltpu.make_async_copy(fa.at[chan(g)], gb_hbm.at[chan(g)], gb_sem.at[g]).start()
        return carry

    lax.fori_loop(0, groups, last, 0)

    for offset in range(1, samples):
        send_spec(offset).wait()
        send_back(offset).wait()

    def outer(c, carry):
        for d in range(GROUP):
            real = jnp.zeros((8, 128), F32)
            imag = jnp.zeros((8, 128), F32)
            for s in range(samples):
                if s == 0:
                    p_real, p_imag = spec[0, c], spec[1, c]
                    q_real, q_imag = back[idp, 0, d], back[idp, 1, d]
                else:
                    p_real, p_imag = spec_land[s - 1, 0, c], spec_land[s - 1, 1, c]
                    q_real, q_imag = back_land[s - 1, 0, d], back_land[s - 1, 1, d]
                real += p_real * q_real + p_imag * q_imag
                imag += p_real * q_imag - p_imag * q_real
            sg_ref[0, c, d] = real * grad_scale
            sg_ref[1, c, d] = imag * grad_scale
        return carry

    lax.fori_loop(0, spec.shape[1], outer, 0)
    for offset in range(1, samples):
        sum_dp(offset).wait()
    pt_ref[...] = sum(pt_land[2, i] for i in range(samples))
    end_reduce_sends(1)
    end_gather_sends(1)
    for g in range(groups):
        pltpu.make_async_copy(fa.at[chan(g)], gb_hbm.at[chan(g)], gb_sem.at[g]).wait()


def fused_device(state_a, state_b, cotan_a, cotan_b, spectral_weight, point_weight):
    samples, px, py = (lax.axis_size(name) for name in ("dp", "px", "py"))
    _, chans, ys, zs, nx = state_b.shape
    ny, nz = ys * px, zs * py
    cells, modes = ys * zs, MY * MZ
    groups = chans // GROUP
    kk = MX // px
    tall = modes // py
    total = nx * ny * nz
    scales = (
        1.0 / math.sqrt(total), 1.0 / math.sqrt(MX * MY * MZ), math.sqrt(MX * MY * MZ / (samples * total)),
    )
    th, uh, turn = (jnp.asarray(t) for t in base_tables((ys, zs, ny, nz)))
    (fh, fl), (xh, xl) = wide_tables(px, nx)
    fh, fl, xh, xl = (jnp.asarray(t) for t in (fh, fl, xh, xl))
    eye = jnp.eye(SUB, dtype=BF16)
    side = chans * SUB
    kron_f = (point_weight.T[:, None, :, None] * eye[None, :, None, :]).reshape(side, side)
    kron_b = (point_weight[:, None, :, None] * eye[None, :, None, :]).reshape(side, side)
    weight = spectral_weight.transpose(3, 4, 5, 1, 0, 2).reshape(2, chans, chans * MZ, 128)
    fields = [value.reshape(chans, cells, nx) for value in (state_b, state_a, cotan_a, cotan_b)]
    field = jax.ShapeDtypeStruct((chans, cells, nx), BF16)
    any_spec = pl.BlockSpec(memory_space=pl.ANY)
    vmem_spec = pl.BlockSpec(memory_space=pltpu.VMEM)
    dma = pltpu.SemaphoreType.DMA
    near = py - 1
    input_a, grad_b, sg, point = pl.pallas_call(
        lambda *refs: fused_kernel(scales, *refs),
        in_specs=[any_spec] * 14,
        out_specs=[any_spec, any_spec, vmem_spec, vmem_spec],
        out_shape=[
            field, field, jax.ShapeDtypeStruct((2, chans, GROUP, MZ, 128), F32),
            jax.ShapeDtypeStruct((chans, side), F32),
        ],
        scratch_shapes=[
            pltpu.VMEM((chans, cells, nx), BF16), pltpu.VMEM((chans, cells, nx), BF16),
            pltpu.VMEM((chans, cells, nx), BF16), pltpu.VMEM((chans, cells, nx), F32),
            pltpu.VMEM(th.shape, BF16), pltpu.VMEM(uh.shape, BF16), pltpu.VMEM(fh.shape, BF16),
            pltpu.VMEM(fl.shape, BF16), pltpu.VMEM(xh.shape, BF16), pltpu.VMEM(xl.shape, BF16),
            pltpu.VMEM((side, side), BF16), pltpu.VMEM((side, side), BF16), pltpu.VMEM(weight.shape, BF16),
            pltpu.VMEM(turn.shape[1:], F32),
            pltpu.VMEM((2, px, groups, py, tall, 128), F32),
            pltpu.VMEM((2, groups, py, tall, 128), F32),
            pltpu.VMEM((2, near, groups, tall, 128), F32),
            pltpu.VMEM((2, px, py, groups, tall, 128), F32),
            pltpu.VMEM((2, chans, MZ, 128), F32),
            pltpu.VMEM((samples - 1, 2, chans, MZ, 128), F32),
            pltpu.VMEM((samples, 2, GROUP, MZ, 128), F32),
            pltpu.VMEM((samples - 1, 2, GROUP, MZ, 128), F32),
            pltpu.VMEM((2, 2 * modes, 2 * nx), BF16),
            pltpu.VMEM((2, 2 * modes, 2 * nx), F32),
            pltpu.VMEM((side, side), F32),
            pltpu.VMEM((3, chans, side), F32),
            pltpu.VMEM((3, max(py, samples), chans, side), F32),
            dma((10,)), dma((groups,)), dma((groups,)), dma((groups,)), dma((groups,)), dma((groups,)), dma((groups,)),
            dma((2, groups)), dma((2, groups)), dma((2, near, groups)), dma((2, near, groups)),
            dma((2, near, groups)), dma((2, near, groups)), dma((2, py, groups)), dma((2, py, groups)),
            dma((2, samples - 1)), dma((2, samples - 1)), dma((1 + near + samples - 1,)), dma((1 + near + samples - 1,)),
        ],
        compiler_params=pltpu.CompilerParams(
            vmem_limit_bytes=FUSED_LIMIT, collective_id=4, has_side_effects=True
        ),
        interpret=INTERPRET,
        name="fused",
    )(*fields, th, uh, fh, fl, xh, xl, kron_f, kron_b, weight, turn)
    spectral_grad = sg.reshape(2, chans, GROUP, MZ, tall // MZ, kk).transpose(4, 3, 5, 0, 1, 2)
    point_total = jnp.sum(point.reshape(chans, chans, SUB), axis=2) / math.sqrt(samples * total)
    full = state_b.shape
    return (input_a.reshape(full), grad_b.reshape(full), spectral_grad, point_total)


def solution(mesh):
    sizes = dict(mesh.shape)

    def body(*values):
        fits = fused_fits(values[1].shape, values[1].shape[0], sizes["dp"], sizes["px"], sizes["py"])
        return (fused_device if fits else general_device)(*values)

    return jax.shard_map(
        body,
        mesh=mesh,
        in_specs=(
            P("dp", None, "px", "py", None),
            P("dp", None, "px", "py", None),
            P("dp", None, "px", "py", None),
            P("dp", None, "px", "py", None),
            P("py", None, "px", None, None, None),
            P(),
        ),
        out_specs=(
            P("dp", None, "px", "py", None),
            P("dp", None, "px", "py", None),
            P("py", None, "px", None, None, "dp"),
            P(),
        ),
        check_vma=False,
    )
```

```python
import math

import jax
import jax.numpy as jnp
import numpy as np
from jax import lax
from jax.experimental import pallas as pl
from jax.experimental.pallas import tpu as pltpu
from jax.sharding import PartitionSpec as P

MX = 32
MY = 32
MZ = 8
GROUP = 4
SUB = 16
LIMIT = 56 * 1024 * 1024
INTERPRET = False
F32 = jnp.float32
BF16 = jnp.bfloat16


def kept(length_all, length_kept, position):
    return jnp.where(position < length_kept // 2, position, length_all - length_kept + position)


def angle(product, length_all):
    return (product % length_all).astype(F32) * (2.0 * math.pi / length_all)


def synthesis_table(shape):
    ys, zs, ny, nz = shape
    mode = lax.broadcasted_iota(jnp.int32, (1, MY * MZ), 1)
    fy = kept(ny, MY, mode // MZ)
    fz = kept(nz, MZ, mode % MZ)
    y = lax.axis_index("px") * ys + lax.broadcasted_iota(jnp.int32, (ys, 1), 0)
    z = lax.axis_index("py") * zs + lax.broadcasted_iota(jnp.int32, (zs, 1), 0)
    ay = angle(fy * y, ny)
    az = angle(fz * z, nz)
    cy, sy = jnp.cos(ay)[:, None, :], jnp.sin(ay)[:, None, :]
    cz, sz = jnp.cos(az)[None], jnp.sin(az)[None]
    table = jnp.concatenate([cy * cz - sy * sz, -(sy * cz + cy * sz)], axis=2)
    return table.reshape(ys * zs, 2 * MY * MZ)


def analysis_table(shape):
    ys, zs, ny, nz = shape
    cell = lax.broadcasted_iota(jnp.int32, (1, ys * zs), 1)
    y = lax.axis_index("px") * ys + cell // zs
    z = lax.axis_index("py") * zs + cell % zs
    fy = kept(ny, MY, lax.broadcasted_iota(jnp.int32, (MY, 1), 0))
    fz = kept(nz, MZ, lax.broadcasted_iota(jnp.int32, (MZ, 1), 0))
    ay = angle(fy * y, ny)
    az = angle(fz * z, nz)
    cy, sy = jnp.cos(ay)[:, None, :], jnp.sin(ay)[:, None, :]
    cz, sz = jnp.cos(az)[None], jnp.sin(az)[None]
    table = jnp.stack([cy * cz - sy * sz, -(sy * cz + cy * sz)])
    return table.reshape(2 * MY * MZ, ys * zs)


def x_tables(px, nx):
    kk = MX // px
    k = np.arange(MX).reshape(px, kk)
    phase = 2.0 * np.pi / nx * (k[:, :, None] * np.arange(nx) % nx)
    cosine, sine = np.cos(phase), np.sin(phase)
    table = np.zeros((2, px, GROUP, 2, kk, GROUP, nx))
    for c in range(GROUP):
        table[0, :, c, 0, :, c] = cosine
        table[0, :, c, 1, :, c] = -sine
        table[1, :, c, 0, :, c] = sine
        table[1, :, c, 1, :, c] = cosine
    table = table.reshape(2, 2 * MX * GROUP, GROUP * nx)
    high = table.astype(BF16)
    low = (table - high.astype(np.float64)).astype(BF16)
    return high, low


def dot(a, b):
    return jnp.dot(a, b, preferred_element_type=F32)


def cut(value):
    high = value.astype(BF16)
    return high, (value - high.astype(F32)).astype(BF16)


def dot3(a, high, low):
    ahigh, alow = cut(a)
    return dot(ahigh, high) + dot(alow, high) + dot(ahigh, low)


def to_modes(b0, b1, xh_ref, xl_ref):
    return dot3(b0, xh_ref[0], xl_ref[0]) + dot3(b1, xh_ref[1], xl_ref[1])


def store_modes(out_ref, group, value, px, py):
    wide = value.shape[1] // px
    tall = value.shape[0] // py
    for i in range(px):
        for j in range(py):
            out_ref[i * py + j, group] = value[j * tall : (j + 1) * tall, i * wide : (i + 1) * wide]


def build_fields(spec_ref, xh_ref, xl_ref, gh_ref, px, py):
    modes = MY * MZ
    for g in range(spec_ref.shape[1]):
        rows = []
        for j in range(py):
            rows.append(jnp.concatenate([spec_ref[i * py + j, g] for i in range(px)], axis=1))
        value = jnp.concatenate(rows, axis=0)
        for t in range(2):
            high = dot3(value, xh_ref[t], xl_ref[t]).astype(BF16)
            half = high.shape[1] // 2
            for h in range(2):
                gh_ref[2 * g + h, t * modes : (t + 1) * modes] = high[:, h * half : (h + 1) * half]


def pair_of(ref, start):
    chans, _, nx = ref.shape
    first = ref[:, pl.ds(start, SUB), :].reshape(chans * SUB, nx)
    second = ref[:, pl.ds(start + SUB, SUB), :].reshape(chans * SUB, nx)
    return jnp.concatenate([first, second], axis=1)


def channel_mix(kron_ref, in_ref, out_ref):
    chans, rows, nx = in_ref.shape

    def body(q, carry):
        start = pl.multiple_of(q * 2 * SUB, 2 * SUB)
        value = dot(kron_ref[...], pair_of(in_ref, start))
        out_ref[:, pl.ds(start, SUB), :] = value[:, :nx].reshape(chans, SUB, nx)
        out_ref[:, pl.ds(start + SUB, SUB), :] = value[:, nx:].reshape(chans, SUB, nx)
        return carry

    lax.fori_loop(0, rows // (2 * SUB), body, 0)


def position(py):
    return lax.axis_index("px") * py + lax.axis_index("py")


def partner(px, py, offset):
    other = lax.rem(position(py) + offset, px * py)
    return other, {"px": lax.div(other, py), "py": lax.rem(other, py)}


def greet(px, py):
    barrier = pltpu.get_barrier_semaphore()
    for offset in range(1, px * py):
        pl.semaphore_signal(
            barrier, inc=1, device_id=partner(px, py, offset)[1], device_id_type=pl.DeviceIdType.MESH
        )
    pl.semaphore_wait(barrier, px * py - 1)


def scatter_copy(px, py, offset, group, part_ref, land_ref, send_sem, recv_sem):
    other, device = partner(px, py, offset)
    return pltpu.make_async_remote_copy(
        part_ref.at[other, group], land_ref.at[offset, group], send_sem.at[offset, group], recv_sem.at[offset, group],
        device_id=device, device_id_type=pl.DeviceIdType.MESH,
    )


def scatter_kernel(px, py, part_ref, out_ref, land_ref, send_sem, recv_sem):
    count = px * py
    greet(px, py)
    groups = part_ref.shape[1]
    for g in range(groups):
        for offset in range(1, count):
            scatter_copy(px, py, offset, g, part_ref, land_ref, send_sem, recv_sem).start()
    out_ref[...] = part_ref[position(py)]
    for g in range(groups):
        for offset in range(1, count):
            scatter_copy(px, py, offset, g, part_ref, land_ref, send_sem, recv_sem).wait()
            out_ref[g] += land_ref[offset, g]


def gather_kernel(px, py, own_ref, out_ref, land_ref, send_sem, recv_sem):
    count = px * py
    greet(px, py)
    copies = []
    for offset in range(1, count):
        copies.append(
            pltpu.make_async_remote_copy(
                own_ref, land_ref.at[offset], send_sem.at[offset], recv_sem.at[offset],
                device_id=partner(px, py, offset)[1], device_id_type=pl.DeviceIdType.MESH,
            )
        )
        copies[-1].start()
    here = position(py)
    out_ref[here] = own_ref[...]
    for offset in range(1, count):
        copies[offset - 1].wait()
        out_ref[lax.rem(here + count - offset, count)] = land_ref[offset]


def mix_kernel(s_ref, w_ref, out_ref):
    chans = s_ref.shape[1]
    real = jnp.zeros(out_ref.shape[1:], F32)
    imag = jnp.zeros(out_ref.shape[1:], F32)
    for c in range(chans):
        s_real, s_imag = s_ref[0, c : c + 1], s_ref[1, c : c + 1]
        w_real, w_imag = w_ref[0, c].astype(F32), w_ref[1, c].astype(F32)
        real += s_real * w_real - s_imag * w_imag
        imag += s_real * w_imag + s_imag * w_real
    out_ref[0] = real
    out_ref[1] = imag


def adjoint_kernel(b_ref, w_ref, out_ref):
    b_real, b_imag = b_ref[0], b_ref[1]
    for c in range(w_ref.shape[1]):
        w_real, w_imag = w_ref[0, c].astype(F32), w_ref[1, c].astype(F32)
        out_ref[0, c : c + 1] = jnp.sum(b_real * w_real + b_imag * w_imag, axis=0, keepdims=True)
        out_ref[1, c : c + 1] = jnp.sum(b_imag * w_real - b_real * w_imag, axis=0, keepdims=True)


def forward_kernel(
    px, py, v_ref, th_ref, xh_ref, xl_ref, out_ref, part_ref, land_ref, send_sem, recv_sem
):
    modes = MY * MZ
    parts = []
    for p in range(GROUP // 2):
        value = jnp.concatenate([v_ref[2 * p], v_ref[2 * p + 1]], axis=1)
        parts.append(dot(th_ref[...], value))
    b0 = jnp.concatenate([part[:modes] for part in parts], axis=1)
    b1 = jnp.concatenate([part[modes:] for part in parts], axis=1)
    step = pl.program_id(0)
    store_modes(part_ref, step, to_modes(b0, b1, xh_ref, xl_ref), px, py)
    count = px * py

    @pl.when(step == 0)
    def _():
        greet(px, py)

    for offset in range(1, count):
        scatter_copy(px, py, offset, step, part_ref, land_ref, send_sem, recv_sem).start()

    @pl.when(step == pl.num_programs(0) - 1)
    def _():
        out_ref[...] = part_ref[position(py)]
        for g in range(part_ref.shape[1]):
            for offset in range(1, count):
                scatter_copy(px, py, offset, g, part_ref, land_ref, send_sem, recv_sem).wait()
                out_ref[g] += land_ref[offset, g]


def middle_kernel(
    px, py, steps, spec_ref, vb_ref, va_ref, ca_ref, uh_ref, th_ref, xh_ref, xl_ref, fh_ref, fl_ref,
    kron_ref, ia_ref, sl_ref, back_ref, point_ref, gh_ref, acc_ref, mix_ref,
):
    step = pl.program_id(0)
    modes = MY * MZ
    nx = vb_ref.shape[2]
    chans, rows = vb_ref.shape[:2]

    @pl.when(step == 0)
    def _():
        build_fields(spec_ref, xh_ref, xl_ref, gh_ref, px, py)
        acc_ref[...] = jnp.zeros_like(acc_ref)
        point_ref[...] = jnp.zeros_like(point_ref)

    channel_mix(kron_ref, vb_ref, mix_ref)
    c0 = math.sqrt(2.0 / math.pi)

    def body(p, carry):
        field = dot(uh_ref[...], gh_ref[p])
        slopes = []
        for h in range(2):
            d = 2 * p + h
            v = field[:, h * nx : (h + 1) * nx] + mix_ref[d]
            v2 = v * v
            t = jnp.tanh(v * (c0 + (c0 * 0.044715) * v2))
            half = 0.5 + 0.5 * t
            ia_ref[d] = (va_ref[d].astype(F32) - v * half).astype(BF16)
            deriv = half + (0.5 * v) * (1.0 - t * t) * (c0 + (3.0 * c0 * 0.044715) * v2)
            slope = (ca_ref[d].astype(F32) * deriv).astype(BF16)
            sl_ref[d] = slope
            slopes.append(slope)
        both = jnp.concatenate(slopes, axis=1)
        acc_ref[p] += dot(th_ref[...], both)
        return carry

    lax.fori_loop(0, chans // 2, body, 0)

    def point_body(q, carry):
        start = pl.multiple_of(q * 2 * SUB, 2 * SUB)
        point_ref[...] += lax.dot_general(
            pair_of(vb_ref, start), pair_of(sl_ref, start), (((1,), (1,)), ((), ())), preferred_element_type=F32
        )
        return carry

    lax.fori_loop(0, rows // (2 * SUB), point_body, 0)

    @pl.when(step == steps - 1)
    def _():
        for g in range(chans // GROUP):
            parts = [acc_ref[2 * g + h] for h in range(2)]
            b0 = jnp.concatenate([part[:modes] for part in parts], axis=1)
            b1 = jnp.concatenate([part[modes:] for part in parts], axis=1)
            store_modes(back_ref, g, to_modes(b0, b1, fh_ref, fl_ref), px, py)


def last_kernel(
    px, py, spec_ref, sl_ref, cb_ref, uh_ref, xh_ref, xl_ref, kron_ref, out_ref, gh_ref, mix_ref
):
    nx = sl_ref.shape[2]

    @pl.when(pl.program_id(0) == 0)
    def _():
        build_fields(spec_ref, xh_ref, xl_ref, gh_ref, px, py)

    channel_mix(kron_ref, sl_ref, mix_ref)

    def body(p, carry):
        field = dot(uh_ref[...], gh_ref[p])
        for h in range(2):
            d = 2 * p + h
            value = cb_ref[d].astype(F32) + field[:, h * nx : (h + 1) * nx] + mix_ref[d]
            out_ref[d] = value.astype(BF16)
        return carry

    lax.fori_loop(0, sl_ref.shape[0] // 2, body, 0)


def whole(shape):
    return pl.BlockSpec(shape, lambda i: (0,) * len(shape), pipeline_mode=pl.Buffered(1))


def general_device(state_a, state_b, cotan_a, cotan_b, spectral_weight, point_weight):
    samples, px, py = (lax.axis_size(name) for name in ("dp", "px", "py"))
    _, chans, ys, zs, nx = state_b.shape
    ny, nz = ys * px, zs * py
    cells, modes = ys * zs, MY * MZ
    groups = chans // GROUP
    kk = MX // px
    tall, wide = modes // py, 2 * MX * GROUP // px
    own = tall * kk
    scale_f = 1.0 / math.sqrt(nx * ny * nz)
    scale_i = 1.0 / math.sqrt(MX * MY * MZ)
    grad_scale = math.sqrt(MX * MY * MZ / (samples * nx * ny * nz))
    point_scale = 1.0 / math.sqrt(samples * nx * ny * nz)
    shape = (ys, zs, ny, nz)
    th = analysis_table(shape).astype(BF16)
    uh = synthesis_table(shape).astype(BF16)
    xh, xl = x_tables(px, nx)
    fh, fl = (jnp.asarray(np.ascontiguousarray(table.transpose(0, 2, 1))) for table in (xh, xl))
    xh, xl = jnp.asarray(xh), jnp.asarray(xl)
    eye = jnp.eye(SUB, dtype=BF16)
    kron_f = (point_weight.T[:, None, :, None] * eye[None, :, None, :]).reshape(chans * SUB, chans * SUB)
    kron_b = (point_weight[:, None, :, None] * eye[None, :, None, :]).reshape(chans * SUB, chans * SUB)
    field_a, field_b, cot_a, cot_b = (
        value.reshape(chans, cells, nx) for value in (state_a, state_b, cotan_a, cotan_b)
    )
    part_shape = jax.ShapeDtypeStruct((px * py, groups, tall, wide), F32)
    params = pltpu.CompilerParams(vmem_limit_bytes=LIMIT)

    count = px * py
    own_shape = jax.ShapeDtypeStruct((groups, tall, wide), F32)
    exchange = [
        pltpu.VMEM(part_shape.shape, F32),
        pltpu.SemaphoreType.DMA((count, groups)),
        pltpu.SemaphoreType.DMA((count, groups)),
    ]

    def linked(number):
        return pltpu.CompilerParams(vmem_limit_bytes=LIMIT, collective_id=number, has_side_effects=True)

    def to_channels(value):
        value = value.reshape(groups, tall, GROUP, 2, kk).transpose(3, 0, 2, 1, 4)
        return value.reshape(2, chans, own)

    def gather(value, number):
        value = value.reshape(2, groups, GROUP, tall, kk).transpose(1, 3, 2, 0, 4)
        value = value.reshape(groups, tall, wide)
        return pl.pallas_call(
            lambda *refs: gather_kernel(px, py, *refs),
            in_specs=[pl.BlockSpec(memory_space=pltpu.VMEM)],
            out_specs=pl.BlockSpec(memory_space=pltpu.VMEM),
            out_shape=part_shape,
            scratch_shapes=[
                pltpu.VMEM(part_shape.shape, F32), pltpu.SemaphoreType.DMA((count,)), pltpu.SemaphoreType.DMA((count,)),
            ],
            compiler_params=linked(number),
            interpret=INTERPRET,
            name="gather",
        )(value)

    def mode_product(kernel, value, name):
        return pl.pallas_call(
            kernel,
            out_shape=jax.ShapeDtypeStruct((2, chans, own), F32),
            compiler_params=params,
            interpret=INTERPRET,
            name=name,
        )(value, weight)

    spectrum = pl.pallas_call(
        lambda *refs: forward_kernel(px, py, *refs),
        grid=(groups,),
        in_specs=[
            pl.BlockSpec((GROUP, cells, nx), lambda i: (i, 0, 0)),
            whole(th.shape), whole(fh.shape), whole(fl.shape),
        ],
        out_specs=whole(own_shape.shape),
        out_shape=own_shape,
        scratch_shapes=[pltpu.VMEM(part_shape.shape, F32)] + exchange,
        compiler_params=linked(0),
        interpret=INTERPRET,
        name="forward",
    )(field_b, th, fh, fl)
    weight = spectral_weight.transpose(3, 4, 5, 0, 1, 2).reshape(2, chans, chans, own)
    spectrum = to_channels(spectrum) * scale_f
    mixed = gather(mode_product(mix_kernel, spectrum, "mix") * scale_i, 1)

    rows = min(256, cells)
    steps = cells // rows
    block = pl.BlockSpec((chans, rows, nx), lambda i: (0, i, 0))
    u_block = pl.BlockSpec((rows, 2 * modes), lambda i: (i, 0))
    t_block = pl.BlockSpec((2 * modes, rows), lambda i: (0, i))
    field_shape = jax.ShapeDtypeStruct((chans, cells, nx), BF16)
    side = chans * SUB
    g_scratch = [pltpu.VMEM((chans // 2, 2 * modes, 2 * nx), BF16)]
    input_a, slope, back_part, point = pl.pallas_call(
        lambda *refs: middle_kernel(px, py, steps, *refs),
        grid=(steps,),
        in_specs=[
            whole(part_shape.shape), block, block, block, u_block, t_block,
            whole(xh.shape), whole(xl.shape), whole(fh.shape), whole(fl.shape), whole((side, side)),
        ],
        out_specs=[block, block, whole(part_shape.shape), whole((side, side))],
        out_shape=[field_shape, field_shape, part_shape, jax.ShapeDtypeStruct((side, side), F32)],
        scratch_shapes=g_scratch
        + [pltpu.VMEM((chans // 2, 2 * modes, 2 * nx), F32), pltpu.VMEM((chans, rows, nx), F32)],
        compiler_params=params,
        interpret=INTERPRET,
        name="middle",
    )(mixed, field_b, field_a, cot_a, uh, th, xh, xl, fh, fl, kron_f)

    back = pl.pallas_call(
        lambda *refs: scatter_kernel(px, py, *refs),
        in_specs=[pl.BlockSpec(memory_space=pltpu.VMEM)],
        out_specs=pl.BlockSpec(memory_space=pltpu.VMEM),
        out_shape=own_shape,
        scratch_shapes=exchange,
        compiler_params=linked(2),
        interpret=INTERPRET,
        name="scatter",
    )(back_part)
    back = to_channels(back) * scale_i
    grad_spec = gather(mode_product(adjoint_kernel, back, "adjoint") * scale_f, 3)
    grad_b = pl.pallas_call(
        lambda *refs: last_kernel(px, py, *refs),
        grid=(steps,),
        in_specs=[
            whole(part_shape.shape), block, block, u_block,
            whole(xh.shape), whole(xl.shape), whole((side, side)),
        ],
        out_specs=block,
        out_shape=field_shape,
        scratch_shapes=g_scratch + [pltpu.VMEM((chans, rows, nx), F32)],
        compiler_params=params,
        interpret=INTERPRET,
        name="last",
    )(grad_spec, slope, cot_b, uh, xh, xl, kron_b)

    share = chans // samples
    spec_all = lax.all_gather(spectrum, "dp", axis=0)
    back_all = lax.all_gather(back, "dp", axis=0)
    back_own = lax.dynamic_slice_in_dim(back_all, lax.axis_index("dp") * share, share, axis=2)
    p_real, p_imag = spec_all[:, 0, :, None], spec_all[:, 1, :, None]
    q_real, q_imag = back_own[:, 0, None], back_own[:, 1, None]
    grad_real = jnp.sum(p_real * q_real + p_imag * q_imag, axis=0)
    grad_imag = jnp.sum(p_real * q_imag - p_imag * q_real, axis=0)
    grad = jnp.stack([grad_real, grad_imag]) * grad_scale
    spectral_grad = grad.reshape(2, chans, share, tall // MZ, MZ, kk).transpose(3, 4, 5, 0, 1, 2)

    point = jnp.sum(point.reshape(chans, SUB, chans, SUB) * jnp.eye(SUB, dtype=F32)[None, :, None, :], axis=(1, 3))
    point_total = lax.psum(point, ("dp", "px", "py")) * point_scale
    full = state_b.shape
    return (input_a.reshape(full), grad_b.reshape(full), spectral_grad, point_total)


MESH = pl.DeviceIdType.MESH
CHUNK = 1024
FUSED_LIMIT = 62 * 1024 * 1024


def fused_fits(shape, local_samples, samples, px, py):
    _, chans, ys, zs, nx = shape
    kk = MX // px
    tall = MY * MZ // py
    return (
        local_samples == 1
        and 2 * kk * GROUP == 128
        and nx == 128
        and MZ == 8
        and tall // MZ == 128 // kk
        and samples * GROUP == chans
        and (ys * zs) % CHUNK == 0
    )


def base_tables(shape):
    ys, zs, ny, nz = shape
    fy = np.where(np.arange(MY) < MY // 2, np.arange(MY), ny - MY + np.arange(MY))
    fz = np.where(np.arange(MZ) < MZ // 2, np.arange(MZ), nz - MZ + np.arange(MZ))
    ay = 2.0 * np.pi / ny * (fy[:, None] * np.arange(ys) % ny)
    az = 2.0 * np.pi / nz * (fz[:, None] * np.arange(zs) % nz)
    both = ay[:, None, :, None] + az[None, :, None, :]
    table = np.stack([np.cos(both), -np.sin(both)]).reshape(2 * MY * MZ, ys * zs).astype(BF16)
    py = 2.0 * np.pi / ny * (fy[None] * (np.arange(ny // ys) * ys)[:, None] % ny)
    pz = 2.0 * np.pi / nz * (fz[None] * (np.arange(nz // zs) * zs)[:, None] % nz)
    turn = py[:, None, :, None] + pz[None, :, None, :]
    turn = np.stack([np.cos(turn), np.sin(turn)], axis=2).reshape(-1, 2, MY * MZ, 1)
    turn = np.broadcast_to(turn, turn.shape[:3] + (128,)).astype(np.float32)
    return table, np.ascontiguousarray(table.T), np.ascontiguousarray(turn)


def wide_tables(px, nx):
    high, low = x_tables(px, nx)
    inverse = [np.concatenate([t[0], t[1]], axis=1) for t in (high, low)]
    forward = [np.ascontiguousarray(t.T) for t in inverse]
    return forward, inverse


def flip(tiles):
    width = 128 // len(tiles)
    block = lax.broadcasted_iota(jnp.int32, tiles[0].shape, 1) // width
    out = []
    for q in range(len(tiles)):
        value = tiles[q]
        for i, tile in enumerate(tiles):
            if i != q:
                value = jnp.where(block == i, pltpu.roll(tile, (i - q) * width % 128, 1), value)
        out.append(value)
    return out


def gelu_pair(v, first, cotan):
    c0 = math.sqrt(2.0 / math.pi)
    v2 = v * v
    half = 0.5 + 0.5 * jnp.tanh(v * (c0 + (c0 * 0.044715) * v2))
    rebuilt = (first.astype(F32) - v * half).astype(BF16)
    inner = v * (2.0 * c0 + (6.0 * c0 * 0.044715) * v2)
    slope = (cotan.astype(F32) * (half + (half * (1.0 - half)) * inner)).astype(BF16)
    return rebuilt, slope


def fused_kernel(
    scales, sb_hbm, sa_hbm, ca_hbm, cb_hbm, th_hbm, uh_hbm, fh_hbm, fl_hbm, xh_hbm, xl_hbm, w_hbm, turn_hbm, pw_ref,
    ia_hbm, gb_hbm, sg_ref, pt_ref,
    sb, fa, fc, mix, th, uh, fh, fl, xh, xl, kf, kb, w_raw, w, turn, part, land_x, land_y, gath, spec, spec_land, mode, back,
    back_land, grad, gf, acc, point, pt_src, pt_land,
    in_sem, w_sem, sb_sem, sa_sem, ca_sem, cb_sem, ia_sem, gb_sem, rx_s, rx_r, ry_s, ry_r, gy_s, gy_r, gx_s, gx_r,
    dp_s, dp_r, pt_s, pt_r,
):
    scale_f, scale_i, grad_scale = scales
    groups = part.shape[1]
    py = part.shape[2]
    tall = part.shape[3]
    cells, nx = sb.shape[1:]
    samples = spec_land.shape[0] + 1
    modes = MY * MZ
    ix, iy, idp = lax.axis_index("px"), lax.axis_index("py"), lax.axis_index("dp")
    other_x = 1 - ix

    def near_y(offset):
        return lax.rem(iy + offset, py)

    def near_dp(offset):
        return lax.rem(idp + offset, samples)

    def chan(g):
        return pl.ds(g * GROUP, GROUP)

    def load(index, src, dst):
        return pltpu.make_async_copy(src, dst, in_sem.at[index])

    tables = [
        load(0, th_hbm, th), load(1, fh_hbm, fh), load(2, fl_hbm, fl),
        load(3, turn_hbm.at[ix * py + iy], turn), load(4, xh_hbm, xh), load(5, xl_hbm, xl), load(6, uh_hbm, uh),
    ]

    def load_weight(l):
        slot = lax.rem(l, 2)
        return pltpu.make_async_copy(w_hbm.at[:, l], w_raw.at[slot], w_sem.at[slot])

    def field_load(src, dst, sem, g):
        return pltpu.make_async_copy(src.at[chan(g)], dst.at[chan(g)], sem.at[g])

    barrier = pltpu.get_barrier_semaphore()
    pl.semaphore_signal(barrier, inc=1, device_id={"px": other_x}, device_id_type=MESH)
    for offset in range(1, py):
        pl.semaphore_signal(barrier, inc=1, device_id={"py": near_y(offset)}, device_id_type=MESH)
    for offset in range(1, samples):
        pl.semaphore_signal(barrier, inc=1, device_id={"dp": near_dp(offset)}, device_id_type=MESH)

    field_load(sb_hbm, sb, sb_sem, 0).start()
    for i in range(4):
        tables[i].start()
    for g in range(1, groups):
        field_load(sb_hbm, sb, sb_sem, g).start()
    load_weight(0).start()
    for i in range(4, len(tables)):
        tables[i].start()
    for g in range(groups):
        field_load(sa_hbm, fa, sa_sem, g).start()
        field_load(ca_hbm, fc, ca_sem, g).start()
    pl.semaphore_wait(barrier, 1 + (py - 1) + (samples - 1))

    def remote(src, dst, send, recv, device):
        return pltpu.make_async_remote_copy(src, dst, send, recv, device_id=device, device_id_type=MESH)

    def reduce_x(f, g):
        return remote(
            part.at[other_x, g], land_x.at[f, g], rx_s.at[f, g], rx_r.at[f, g], {"px": other_x}
        )

    def reduce_y(f, g, offset):
        to = near_y(offset)
        return remote(
            part.at[ix, g, to], land_y.at[f, offset - 1, g], ry_s.at[f, offset - 1, g], ry_r.at[f, offset - 1, g],
            {"py": to},
        )

    def gather_y(f, g, offset):
        block = gath.at[f, ix, iy, g]
        return remote(block, block, gy_s.at[f, offset - 1, g], gy_r.at[f, offset - 1, g], {"py": near_y(offset)})

    def gather_x(f, g, offset):
        block = gath.at[f, ix, lax.rem(iy + py - offset, py), g]
        return remote(block, block, gx_s.at[f, offset, g], gx_r.at[f, offset, g], {"px": other_x})

    def after_x(f, g):
        reduce_x(f, g).wait_recv()
        part[ix, g] += land_x[f, g]
        for offset in range(1, py):
            reduce_y(f, g, offset).start()

    def finish_reduce(f, g):
        for offset in range(1, py):
            reduce_y(f, g, offset).wait_recv()
        value = part[ix, g, iy]
        for offset in range(1, py):
            value = value + land_y[f, offset - 1, g]
        return flip([value[8 * i : 8 * i + 8] for i in range(tall // 8)])

    def end_reduce_sends(f):
        for g in range(groups):
            reduce_x(f, g).wait_send()
            for offset in range(1, py):
                reduce_y(f, g, offset).wait_send()

    def start_gather(f, g, tiles):
        for i, tile in enumerate(flip(tiles)):
            gath[f, ix, iy, g, 8 * i : 8 * i + 8] = tile
        for offset in range(1, py):
            gather_y(f, g, offset).start()
        gather_x(f, g, 0).start()

    def forward_gather(f, g):
        for offset in range(1, py):
            gather_y(f, g, offset).wait_recv()
            gather_x(f, g, offset).start()

    def finish_gather(f, g):
        for offset in range(py):
            gather_x(f, g, offset).wait_recv()

    def end_gather_sends(f):
        for g in range(groups):
            for offset in range(1, py):
                gather_y(f, g, offset).wait_send()
            for offset in range(py):
                gather_x(f, g, offset).wait_send()

    def turns():
        cosine = jnp.concatenate([turn[0]] * GROUP, axis=1)
        sine = jnp.concatenate([turn[1]] * GROUP, axis=1)
        return cosine, sine

    def analyse(src, first, slot):
        value = jnp.concatenate([src[first], src[first + 1]], axis=1)
        acc[slot] = dot(th[...], value)

    def to_part(g):
        cosine, sine = turns()
        b0 = jnp.concatenate([acc[0, :modes], acc[1, :modes]], axis=1)
        b1 = jnp.concatenate([acc[0, modes:], acc[1, modes:]], axis=1)
        both = jnp.concatenate([b0 * cosine + b1 * sine, b1 * cosine - b0 * sine], axis=1)
        value = dot3(both, fh[...], fl[...])
        for i in range(2):
            part[i, g] = value[:, i * 128 : (i + 1) * 128].reshape(py, tall, 128)

    def build(f, g):
        value = jnp.concatenate([gath[f, i, :, g].reshape(modes, 128) for i in range(2)], axis=1)
        high, low = cut(value)
        cosine, sine = turns()
        wide = GROUP * nx
        both = dot(high, xh[...]) + dot(low, xh[...]) + dot(high, xl[...])
        g0, g1 = both[:, :wide], both[:, wide:]
        for t, field in enumerate((g0 * cosine - g1 * sine, g1 * cosine + g0 * sine)):
            field = field.astype(BF16)
            for h in range(2):
                gf[h, t * modes : (t + 1) * modes] = field[:, h * 2 * nx : (h + 1) * 2 * nx]

    def mix_rows(table, src, lo, hi):
        def step(q, carry):
            start = pl.multiple_of(q * 2 * SUB, 2 * SUB)
            value = dot(table[...], pair_of(src, start))
            mix[:, pl.ds(start, SUB), :] = value[:, :nx].reshape(-1, SUB, nx)
            mix[:, pl.ds(start + SUB, SUB), :] = value[:, nx:].reshape(-1, SUB, nx)
            return carry

        lax.fori_loop(lo, hi, step, 0)

    steps = cells // (2 * SUB)
    side = point.shape[0]
    row = lax.broadcasted_iota(jnp.int32, (side, side), 0)
    column = lax.broadcasted_iota(jnp.int32, (side, side), 1)
    same = row % SUB == column % SUB

    for i in range(4):
        tables[i].wait()

    def forward(g, carry):
        field_load(sb_hbm, sb, sb_sem, g).wait()
        for p in range(2):
            analyse(sb, g * GROUP + 2 * p, p)
        to_part(g)
        reduce_x(0, g).start()

        @pl.when(g >= 1)
        def _():
            after_x(0, g - 1)

        return carry

    lax.fori_loop(0, groups, forward, 0)

    def turn_weight(l, carry):
        @pl.when(l + 1 < MZ)
        def _():
            load_weight(l + 1).start()

        load_weight(l).wait()
        half = w_raw.shape[1] // 2
        for h in range(2):
            raw = w_raw[lax.rem(l, 2), h * half : (h + 1) * half].astype(F32)
            mix[h, : half * raw.shape[1], : raw.shape[2]] = raw.reshape(-1, raw.shape[2])
        inner = 2 * spec.shape[1]
        for r in range(inner):
            rows = [mix[h, pl.ds(r, half * raw.shape[1] // inner, stride=inner), : raw.shape[2]] for h in range(2)]
            w[r // spec.shape[1], r % spec.shape[1], l] = jnp.concatenate(rows, axis=0).T.astype(BF16)
        return carry

    lax.fori_loop(0, MZ, turn_weight, 0)
    spread = (row // SUB == column)[:, :SUB].astype(BF16)
    gathered = (lax.broadcasted_iota(jnp.int32, (SUB, side), 1) // SUB
                == lax.broadcasted_iota(jnp.int32, (SUB, side), 0)).astype(BF16)
    turned = lax.dot_general(spread, pw_ref[...], (((1,), (1,)), ((), ())), preferred_element_type=F32)
    kf[...] = jnp.where(same, dot(turned.astype(BF16), gathered), 0.0).astype(BF16)
    kb[...] = jnp.where(same, dot(dot(spread, pw_ref[...]).astype(BF16), gathered), 0.0).astype(BF16)
    mix_rows(kf, sb, 0, steps // 2)
    after_x(0, groups - 1)
    mix_rows(kf, sb, steps // 2, steps)

    def take_spectrum(g, carry):
        tiles = finish_reduce(0, g)
        for q, tile in enumerate(tiles):
            spec[q % 2, g * GROUP + q // 2] = tile * scale_f
        return carry

    lax.fori_loop(0, groups, take_spectrum, 0)

    def blend(l, carry):
        real = jnp.zeros(w.shape[3:], F32)
        imag = jnp.zeros(w.shape[3:], F32)
        for c in range(spec.shape[1]):
            w_real, w_imag = w[0, c, l].astype(F32), w[1, c, l].astype(F32)
            s_real, s_imag = spec[0, c, pl.ds(l, 1), :], spec[1, c, pl.ds(l, 1), :]
            real += s_real * w_real - s_imag * w_imag
            imag += s_real * w_imag + s_imag * w_real
        mode[0, pl.ds(l, real.shape[0], stride=MZ), :] = real * scale_i
        mode[1, pl.ds(l, real.shape[0], stride=MZ), :] = imag * scale_i
        return carry

    lax.fori_loop(0, MZ, blend, 0)
    for g in range(groups):
        start_gather(0, g, [mode[q % 2, (g * GROUP + q // 2) * MZ :][:MZ] for q in range(2 * GROUP)])

    def send_spec(offset):
        return remote(
            spec, spec_land.at[offset - 1], dp_s.at[0, offset - 1], dp_r.at[0, offset - 1], {"dp": near_dp(offset)}
        )

    def send_back(offset):
        to = near_dp(offset)
        return remote(
            back.at[to], back_land.at[offset - 1], dp_s.at[1, offset - 1], dp_r.at[1, offset - 1], {"dp": to}
        )

    for offset in range(1, samples):
        send_spec(offset).start()
    end_reduce_sends(0)
    for i in range(4, len(tables)):
        tables[i].wait()
    forward_gather(0, 0)

    def middle(g, carry):
        @pl.when(g + 1 < groups)
        def _():
            forward_gather(0, g + 1)

        finish_gather(0, g)
        build(0, g)
        field_load(sa_hbm, fa, sa_sem, g).wait()
        field_load(ca_hbm, fc, ca_sem, g).wait()

        def pair(p, inner):
            first = g * GROUP + 2 * p

            def rows(r, deep):
                some = pl.ds(pl.multiple_of(r * CHUNK, CHUNK), CHUNK)
                field = dot(uh[some, :], gf[p])
                for h in range(2):
                    v = field[:, h * nx : (h + 1) * nx] + mix[first + h, some, :]
                    rebuilt, slope = gelu_pair(v, fa[first + h, some, :], fc[first + h, some, :])
                    fa[first + h, some, :] = rebuilt
                    fc[first + h, some, :] = slope
                return deep

            lax.fori_loop(0, cells // CHUNK, rows, 0)
            analyse(fc, first, p)
            return inner

        lax.fori_loop(0, 2, pair, 0)
        pltpu.make_async_copy(fa.at[chan(g)], ia_hbm.at[chan(g)], ia_sem.at[g]).start()
        to_part(g)
        reduce_x(1, g).start()

        @pl.when(g >= 1)
        def _():
            after_x(1, g - 1)

        return carry

    lax.fori_loop(0, groups, middle, 0)
    end_gather_sends(0)

    point[...] = jnp.zeros_like(point)

    def point_rows(lo, hi):
        def step(q, carry):
            start = pl.multiple_of(q * 4 * SUB, 4 * SUB)
            left = jnp.concatenate([pair_of(sb, start), pair_of(sb, start + 2 * SUB)], axis=1)
            right = jnp.concatenate([pair_of(fc, start), pair_of(fc, start + 2 * SUB)], axis=1)
            point[...] += lax.dot_general(left, right, (((1,), (1,)), ((), ())), preferred_element_type=F32)
            return carry

        lax.fori_loop(lo, hi, step, 0)

    point_rows(0, steps // 4)
    after_x(1, groups - 1)
    point_rows(steps // 4, steps // 2)
    diagonal = jnp.where(same, point[...], 0.0)
    pt_src[0] = jnp.sum(diagonal.reshape(-1, SUB, point.shape[1]), axis=1)

    def sum_x():
        return remote(pt_src.at[0], pt_land.at[0, 0], pt_s.at[0], pt_r.at[0], {"px": other_x})

    def sum_y(offset):
        return remote(
            pt_src.at[1], pt_land.at[1, iy], pt_s.at[offset], pt_r.at[offset], {"py": near_y(offset)}
        )

    def sum_dp(offset):
        return remote(
            pt_src.at[2], pt_land.at[2, idp], pt_s.at[py - 1 + offset], pt_r.at[py - 1 + offset],
            {"dp": near_dp(offset)},
        )

    sum_x().start()

    def take_back(g, carry):
        tiles = finish_reduce(1, g)
        for q, tile in enumerate(tiles):
            back[g, q % 2, q // 2] = tile * scale_i
            mode[q % 2, pl.ds(pl.multiple_of((g * GROUP + q // 2) * MZ, MZ), MZ), :] = tile * scale_i
        return carry

    lax.fori_loop(0, groups, take_back, 0)

    def adjoint(g, carry):
        for l in range(MZ):
            b_real, b_imag = (mode[i, pl.ds(l, w.shape[3], stride=MZ), :] for i in range(2))
            for c in range(GROUP):
                w_real, w_imag = w[0, g * GROUP + c, l].astype(F32), w[1, g * GROUP + c, l].astype(F32)
                real = jnp.sum(b_real * w_real + b_imag * w_imag, axis=0, keepdims=True)
                imag = jnp.sum(b_imag * w_real - b_real * w_imag, axis=0, keepdims=True)
                grad[2 * c, l : l + 1] = real * scale_f
                grad[2 * c + 1, l : l + 1] = imag * scale_f
        start_gather(1, g, [grad[q] for q in range(2 * GROUP)])
        return carry

    lax.fori_loop(0, groups, adjoint, 0)
    for offset in range(1, samples):
        send_back(offset).start()
    for g in range(groups):
        pltpu.make_async_copy(fa.at[chan(g)], ia_hbm.at[chan(g)], ia_sem.at[g]).wait()
        field_load(cb_hbm, fa, cb_sem, g).start()
    sum_x().wait()
    pt_src[1] = pt_src[0] + pt_land[0, 0]
    pt_land[1, iy] = pt_src[1]
    for offset in range(1, py):
        sum_y(offset).start()
    mix_rows(kb, fc, 0, steps // 2)
    forward_gather(1, 0)
    for offset in range(1, py):
        sum_y(offset).wait()
    pt_src[2] = sum(pt_land[1, i] for i in range(py))
    pt_land[2, idp] = pt_src[2]
    for offset in range(1, samples):
        sum_dp(offset).start()
    mix_rows(kb, fc, steps // 2, steps)

    def last(g, carry):
        @pl.when(g + 1 < groups)
        def _():
            forward_gather(1, g + 1)

        finish_gather(1, g)
        build(1, g)
        field_load(cb_hbm, fa, cb_sem, g).wait()

        def pair(p, inner):
            first = g * GROUP + 2 * p

            def rows(r, deep):
                some = pl.ds(pl.multiple_of(r * CHUNK, CHUNK), CHUNK)
                field = dot(uh[some, :], gf[p])
                for h in range(2):
                    value = fa[first + h, some, :].astype(F32) + field[:, h * nx : (h + 1) * nx]
                    fa[first + h, some, :] = (value + mix[first + h, some, :]).astype(BF16)
                return deep

            lax.fori_loop(0, cells // CHUNK, rows, 0)
            return inner

        lax.fori_loop(0, 2, pair, 0)
        pltpu.make_async_copy(fa.at[chan(g)], gb_hbm.at[chan(g)], gb_sem.at[g]).start()
        return carry

    lax.fori_loop(0, groups, last, 0)

    for offset in range(1, samples):
        send_spec(offset).wait()
        send_back(offset).wait()

    def outer(c, carry):
        for d in range(GROUP):
            real = jnp.zeros((8, 128), F32)
            imag = jnp.zeros((8, 128), F32)
            for s in range(samples):
                if s == 0:
                    p_real, p_imag = spec[0, c], spec[1, c]
                    q_real, q_imag = back[idp, 0, d], back[idp, 1, d]
                else:
                    p_real, p_imag = spec_land[s - 1, 0, c], spec_land[s - 1, 1, c]
                    q_real, q_imag = back_land[s - 1, 0, d], back_land[s - 1, 1, d]
                real += p_real * q_real + p_imag * q_imag
                imag += p_real * q_imag - p_imag * q_real
            sg_ref[0, d, pl.ds(pl.multiple_of(c * MZ, MZ), MZ), :] = real * grad_scale
            sg_ref[1, d, pl.ds(pl.multiple_of(c * MZ, MZ), MZ), :] = imag * grad_scale
        return carry

    lax.fori_loop(0, spec.shape[1], outer, 0)
    for offset in range(1, samples):
        sum_dp(offset).wait()
    pt_ref[...] = sum(pt_land[2, i] for i in range(samples))
    end_reduce_sends(1)
    end_gather_sends(1)
    for g in range(groups):
        pltpu.make_async_copy(fa.at[chan(g)], gb_hbm.at[chan(g)], gb_sem.at[g]).wait()


def finish_kernel(ia_raw, gb_raw, sg_ref, ia_hbm, gb_hbm, out_hbm, hold, out, in_sem, copy_sem, out_sem):
    slots, each = hold.shape[:2]
    jj, rows, chans = out.shape[1:]
    inner = 2 * GROUP
    kk = rows // inner
    jobs = [(a, b, i) for i in range(ia_raw.shape[0] // each) for a, b in ((ia_raw, ia_hbm), (gb_raw, gb_hbm))]

    def fetch(t):
        src, _, i = jobs[t]
        return pltpu.make_async_copy(src.at[pl.ds(i * each, each)], hold.at[t % slots], in_sem.at[t % slots])

    def write(t):
        _, dst, i = jobs[t]
        return pltpu.make_async_copy(hold.at[t % slots], dst.at[pl.ds(i * each, each)], copy_sem.at[t % slots])

    def store(l):
        return pltpu.make_async_copy(out.at[l % 2], out_hbm.at[:, l], out_sem.at[l % 2])

    def spread(l):
        if l >= 2:
            store(l - 2).wait()
        for r in range(inner):
            value = sg_ref[r // GROUP, r % GROUP, pl.ds(l, chans, stride=MZ), :].T
            for j in range(jj):
                out[l % 2, j, pl.ds(r, kk, stride=inner), :] = value[j * kk : (j + 1) * kk]
        store(l).start()

    ahead = min(slots, len(jobs))
    for t in range(ahead):
        fetch(t).start()
    written = 0
    for t in range(len(jobs)):
        fetch(t).wait()
        write(t).start()
        if t * MZ // len(jobs) != (t + 1) * MZ // len(jobs):
            spread(t * MZ // len(jobs))
        if t >= 2 and ahead < len(jobs):
            write(t - 2).wait()
            written = t - 1
            fetch(ahead).start()
            ahead += 1
    for t in range(written, len(jobs)):
        write(t).wait()
    store(MZ - 2).wait()
    store(MZ - 1).wait()


def fused_device(state_a, state_b, cotan_a, cotan_b, spectral_weight, point_weight):
    samples, px, py = (lax.axis_size(name) for name in ("dp", "px", "py"))
    _, chans, ys, zs, nx = state_b.shape
    ny, nz = ys * px, zs * py
    cells, modes = ys * zs, MY * MZ
    groups = chans // GROUP
    kk = MX // px
    tall = modes // py
    total = nx * ny * nz
    scales = (
        1.0 / math.sqrt(total), 1.0 / math.sqrt(MX * MY * MZ), math.sqrt(MX * MY * MZ / (samples * total)),
    )
    th, uh, turn = (jnp.asarray(t) for t in base_tables((ys, zs, ny, nz)))
    (fh, fl), (xh, xl) = wide_tables(px, nx)
    fh, fl, xh, xl = (jnp.asarray(t) for t in (fh, fl, xh, xl))
    side = chans * SUB
    jj, ll = tall // MZ, MZ
    weight = spectral_weight.reshape(jj, ll, kk * 2 * chans, chans)
    fields = [value.reshape(chans, cells, nx) for value in (state_b, state_a, cotan_a, cotan_b)]
    field = jax.ShapeDtypeStruct((chans, cells, nx), BF16)
    any_spec = pl.BlockSpec(memory_space=pl.ANY)
    vmem_spec = pl.BlockSpec(memory_space=pltpu.VMEM)
    dma = pltpu.SemaphoreType.DMA
    near = py - 1
    input_a, grad_b, sg, point = pl.pallas_call(
        lambda *refs: fused_kernel(scales, *refs),
        in_specs=[any_spec] * 12 + [vmem_spec],
        out_specs=[any_spec, any_spec, vmem_spec, vmem_spec],
        out_shape=[
            field, field, jax.ShapeDtypeStruct((2, GROUP, chans * MZ, 128), F32),
            jax.ShapeDtypeStruct((chans, side), F32),
        ],
        scratch_shapes=[
            pltpu.VMEM((chans, cells, nx), BF16), pltpu.VMEM((chans, cells, nx), BF16),
            pltpu.VMEM((chans, cells, nx), BF16), pltpu.VMEM((chans, cells, nx), F32),
            pltpu.VMEM(th.shape, BF16), pltpu.VMEM(uh.shape, BF16), pltpu.VMEM(fh.shape, BF16),
            pltpu.VMEM(fl.shape, BF16), pltpu.VMEM(xh.shape, BF16), pltpu.VMEM(xl.shape, BF16),
            pltpu.VMEM((side, side), BF16), pltpu.VMEM((side, side), BF16),
            pltpu.VMEM((2, jj) + weight.shape[2:], BF16), pltpu.VMEM((2, chans, MZ, chans, 128), BF16),
            pltpu.VMEM(turn.shape[1:], F32),
            pltpu.VMEM((px, groups, py, tall, 128), F32),
            pltpu.VMEM((2, groups, py, tall, 128), F32),
            pltpu.VMEM((2, near, groups, tall, 128), F32),
            pltpu.VMEM((2, px, py, groups, tall, 128), F32),
            pltpu.VMEM((2, chans, MZ, 128), F32),
            pltpu.VMEM((samples - 1, 2, chans, MZ, 128), F32),
            pltpu.VMEM((2, chans * MZ, 128), F32),
            pltpu.VMEM((samples, 2, GROUP, MZ, 128), F32),
            pltpu.VMEM((samples - 1, 2, GROUP, MZ, 128), F32),
            pltpu.VMEM((2 * GROUP, MZ, 128), F32),
            pltpu.VMEM((2, 2 * modes, 2 * nx), BF16),
            pltpu.VMEM((2, 2 * modes, 2 * nx), F32),
            pltpu.VMEM((side, side), F32),
            pltpu.VMEM((3, chans, side), F32),
            pltpu.VMEM((3, max(py, samples), chans, side), F32),
            dma((7,)), dma((2,)), dma((groups,)), dma((groups,)), dma((groups,)), dma((groups,)), dma((groups,)), dma((groups,)),
            dma((2, groups)), dma((2, groups)), dma((2, near, groups)), dma((2, near, groups)),
            dma((2, near, groups)), dma((2, near, groups)), dma((2, py, groups)), dma((2, py, groups)),
            dma((2, samples - 1)), dma((2, samples - 1)), dma((1 + near + samples - 1,)), dma((1 + near + samples - 1,)),
        ],
        compiler_params=pltpu.CompilerParams(
            vmem_limit_bytes=FUSED_LIMIT, collective_id=4, has_side_effects=True
        ),
        interpret=INTERPRET,
        name="fused",
    )(*fields, th, uh, fh, fl, xh, xl, weight, turn, point_weight)
    spread = (jj, ll, kk * 2 * GROUP, chans)
    slots, each = 6, 2
    input_a, grad_b, spectral_grad = pl.pallas_call(
        finish_kernel,
        in_specs=[any_spec, any_spec, vmem_spec],
        out_specs=[any_spec] * 3,
        out_shape=[field, field, jax.ShapeDtypeStruct(spread, F32)],
        scratch_shapes=[
            pltpu.VMEM((slots, each, cells, nx), BF16), pltpu.VMEM((2, jj) + spread[2:], F32),
            dma((slots,)), dma((slots,)), dma((2,)),
        ],
        compiler_params=pltpu.CompilerParams(vmem_limit_bytes=LIMIT),
        interpret=INTERPRET,
        name="finish",
    )(input_a, grad_b, sg)
    spectral_grad = spectral_grad.reshape(jj, ll, kk, 2, GROUP, chans).transpose(0, 1, 2, 3, 5, 4)
    point_total = jnp.sum(point.reshape(chans, chans, SUB), axis=2) / math.sqrt(samples * total)
    full = state_b.shape
    return (input_a.reshape(full), grad_b.reshape(full), spectral_grad, point_total)


def solution(mesh):
    sizes = dict(mesh.shape)

    def body(*values):
        fits = fused_fits(values[1].shape, values[1].shape[0], sizes["dp"], sizes["px"], sizes["py"])
        return (fused_device if fits else general_device)(*values)

    return jax.shard_map(
        body,
        mesh=mesh,
        in_specs=(
            P("dp", None, "px", "py", None),
            P("dp", None, "px", "py", None),
            P("dp", None, "px", "py", None),
            P("dp", None, "px", "py", None),
            P("py", None, "px", None, None, None),
            P(),
        ),
        out_specs=(
            P("dp", None, "px", "py", None),
            P("dp", None, "px", "py", None),
            P("py", None, "px", None, None, "dp"),
            P(),
        ),
        check_vma=False,
    )
```

```python
import math

import jax
import jax.numpy as jnp
import numpy as np
from jax import lax
from jax.experimental import pallas as pl
from jax.experimental.pallas import tpu as pltpu
from jax.sharding import PartitionSpec as P

MX = 32
MY = 32
MZ = 8
GROUP = 4
SUB = 16
LIMIT = 56 * 1024 * 1024
INTERPRET = False
F32 = jnp.float32
BF16 = jnp.bfloat16


def kept(length_all, length_kept, position):
    return jnp.where(position < length_kept // 2, position, length_all - length_kept + position)


def angle(product, length_all):
    return (product % length_all).astype(F32) * (2.0 * math.pi / length_all)


def synthesis_table(shape):
    ys, zs, ny, nz = shape
    mode = lax.broadcasted_iota(jnp.int32, (1, MY * MZ), 1)
    fy = kept(ny, MY, mode // MZ)
    fz = kept(nz, MZ, mode % MZ)
    y = lax.axis_index("px") * ys + lax.broadcasted_iota(jnp.int32, (ys, 1), 0)
    z = lax.axis_index("py") * zs + lax.broadcasted_iota(jnp.int32, (zs, 1), 0)
    ay = angle(fy * y, ny)
    az = angle(fz * z, nz)
    cy, sy = jnp.cos(ay)[:, None, :], jnp.sin(ay)[:, None, :]
    cz, sz = jnp.cos(az)[None], jnp.sin(az)[None]
    table = jnp.concatenate([cy * cz - sy * sz, -(sy * cz + cy * sz)], axis=2)
    return table.reshape(ys * zs, 2 * MY * MZ)


def analysis_table(shape):
    ys, zs, ny, nz = shape
    cell = lax.broadcasted_iota(jnp.int32, (1, ys * zs), 1)
    y = lax.axis_index("px") * ys + cell // zs
    z = lax.axis_index("py") * zs + cell % zs
    fy = kept(ny, MY, lax.broadcasted_iota(jnp.int32, (MY, 1), 0))
    fz = kept(nz, MZ, lax.broadcasted_iota(jnp.int32, (MZ, 1), 0))
    ay = angle(fy * y, ny)
    az = angle(fz * z, nz)
    cy, sy = jnp.cos(ay)[:, None, :], jnp.sin(ay)[:, None, :]
    cz, sz = jnp.cos(az)[None], jnp.sin(az)[None]
    table = jnp.stack([cy * cz - sy * sz, -(sy * cz + cy * sz)])
    return table.reshape(2 * MY * MZ, ys * zs)


def x_tables(px, nx):
    kk = MX // px
    k = np.arange(MX).reshape(px, kk)
    phase = 2.0 * np.pi / nx * (k[:, :, None] * np.arange(nx) % nx)
    cosine, sine = np.cos(phase), np.sin(phase)
    table = np.zeros((2, px, GROUP, 2, kk, GROUP, nx))
    for c in range(GROUP):
        table[0, :, c, 0, :, c] = cosine
        table[0, :, c, 1, :, c] = -sine
        table[1, :, c, 0, :, c] = sine
        table[1, :, c, 1, :, c] = cosine
    table = table.reshape(2, 2 * MX * GROUP, GROUP * nx)
    high = table.astype(BF16)
    low = (table - high.astype(np.float64)).astype(BF16)
    return high, low


def dot(a, b):
    return jnp.dot(a, b, preferred_element_type=F32)


def cut(value):
    high = value.astype(BF16)
    return high, (value - high.astype(F32)).astype(BF16)


def dot3(a, high, low):
    ahigh, alow = cut(a)
    return dot(ahigh, high) + dot(alow, high) + dot(ahigh, low)


def to_modes(b0, b1, xh_ref, xl_ref):
    return dot3(b0, xh_ref[0], xl_ref[0]) + dot3(b1, xh_ref[1], xl_ref[1])


def store_modes(out_ref, group, value, px, py):
    wide = value.shape[1] // px
    tall = value.shape[0] // py
    for i in range(px):
        for j in range(py):
            out_ref[i * py + j, group] = value[j * tall : (j + 1) * tall, i * wide : (i + 1) * wide]


def build_fields(spec_ref, xh_ref, xl_ref, gh_ref, px, py):
    modes = MY * MZ
    for g in range(spec_ref.shape[1]):
        rows = []
        for j in range(py):
            rows.append(jnp.concatenate([spec_ref[i * py + j, g] for i in range(px)], axis=1))
        value = jnp.concatenate(rows, axis=0)
        for t in range(2):
            high = dot3(value, xh_ref[t], xl_ref[t]).astype(BF16)
            half = high.shape[1] // 2
            for h in range(2):
                gh_ref[2 * g + h, t * modes : (t + 1) * modes] = high[:, h * half : (h + 1) * half]


def pair_of(ref, start):
    chans, _, nx = ref.shape
    first = ref[:, pl.ds(start, SUB), :].reshape(chans * SUB, nx)
    second = ref[:, pl.ds(start + SUB, SUB), :].reshape(chans * SUB, nx)
    return jnp.concatenate([first, second], axis=1)


def channel_mix(kron_ref, in_ref, out_ref):
    chans, rows, nx = in_ref.shape

    def body(q, carry):
        start = pl.multiple_of(q * 2 * SUB, 2 * SUB)
        value = dot(kron_ref[...], pair_of(in_ref, start))
        out_ref[:, pl.ds(start, SUB), :] = value[:, :nx].reshape(chans, SUB, nx)
        out_ref[:, pl.ds(start + SUB, SUB), :] = value[:, nx:].reshape(chans, SUB, nx)
        return carry

    lax.fori_loop(0, rows // (2 * SUB), body, 0)


def position(py):
    return lax.axis_index("px") * py + lax.axis_index("py")


def partner(px, py, offset):
    other = lax.rem(position(py) + offset, px * py)
    return other, {"px": lax.div(other, py), "py": lax.rem(other, py)}


def greet(px, py):
    barrier = pltpu.get_barrier_semaphore()
    for offset in range(1, px * py):
        pl.semaphore_signal(
            barrier, inc=1, device_id=partner(px, py, offset)[1], device_id_type=pl.DeviceIdType.MESH
        )
    pl.semaphore_wait(barrier, px * py - 1)


def scatter_copy(px, py, offset, group, part_ref, land_ref, send_sem, recv_sem):
    other, device = partner(px, py, offset)
    return pltpu.make_async_remote_copy(
        part_ref.at[other, group], land_ref.at[offset, group], send_sem.at[offset, group], recv_sem.at[offset, group],
        device_id=device, device_id_type=pl.DeviceIdType.MESH,
    )


def scatter_kernel(px, py, part_ref, out_ref, land_ref, send_sem, recv_sem):
    count = px * py
    greet(px, py)
    groups = part_ref.shape[1]
    for g in range(groups):
        for offset in range(1, count):
            scatter_copy(px, py, offset, g, part_ref, land_ref, send_sem, recv_sem).start()
    out_ref[...] = part_ref[position(py)]
    for g in range(groups):
        for offset in range(1, count):
            scatter_copy(px, py, offset, g, part_ref, land_ref, send_sem, recv_sem).wait()
            out_ref[g] += land_ref[offset, g]


def gather_kernel(px, py, own_ref, out_ref, land_ref, send_sem, recv_sem):
    count = px * py
    greet(px, py)
    copies = []
    for offset in range(1, count):
        copies.append(
            pltpu.make_async_remote_copy(
                own_ref, land_ref.at[offset], send_sem.at[offset], recv_sem.at[offset],
                device_id=partner(px, py, offset)[1], device_id_type=pl.DeviceIdType.MESH,
            )
        )
        copies[-1].start()
    here = position(py)
    out_ref[here] = own_ref[...]
    for offset in range(1, count):
        copies[offset - 1].wait()
        out_ref[lax.rem(here + count - offset, count)] = land_ref[offset]


def mix_kernel(s_ref, w_ref, out_ref):
    chans = s_ref.shape[1]
    real = jnp.zeros(out_ref.shape[1:], F32)
    imag = jnp.zeros(out_ref.shape[1:], F32)
    for c in range(chans):
        s_real, s_imag = s_ref[0, c : c + 1], s_ref[1, c : c + 1]
        w_real, w_imag = w_ref[0, c].astype(F32), w_ref[1, c].astype(F32)
        real += s_real * w_real - s_imag * w_imag
        imag += s_real * w_imag + s_imag * w_real
    out_ref[0] = real
    out_ref[1] = imag


def adjoint_kernel(b_ref, w_ref, out_ref):
    b_real, b_imag = b_ref[0], b_ref[1]
    for c in range(w_ref.shape[1]):
        w_real, w_imag = w_ref[0, c].astype(F32), w_ref[1, c].astype(F32)
        out_ref[0, c : c + 1] = jnp.sum(b_real * w_real + b_imag * w_imag, axis=0, keepdims=True)
        out_ref[1, c : c + 1] = jnp.sum(b_imag * w_real - b_real * w_imag, axis=0, keepdims=True)


def forward_kernel(
    px, py, v_ref, th_ref, xh_ref, xl_ref, out_ref, part_ref, land_ref, send_sem, recv_sem
):
    modes = MY * MZ
    parts = []
    for p in range(GROUP // 2):
        value = jnp.concatenate([v_ref[2 * p], v_ref[2 * p + 1]], axis=1)
        parts.append(dot(th_ref[...], value))
    b0 = jnp.concatenate([part[:modes] for part in parts], axis=1)
    b1 = jnp.concatenate([part[modes:] for part in parts], axis=1)
    step = pl.program_id(0)
    store_modes(part_ref, step, to_modes(b0, b1, xh_ref, xl_ref), px, py)
    count = px * py

    @pl.when(step == 0)
    def _():
        greet(px, py)

    for offset in range(1, count):
        scatter_copy(px, py, offset, step, part_ref, land_ref, send_sem, recv_sem).start()

    @pl.when(step == pl.num_programs(0) - 1)
    def _():
        out_ref[...] = part_ref[position(py)]
        for g in range(part_ref.shape[1]):
            for offset in range(1, count):
                scatter_copy(px, py, offset, g, part_ref, land_ref, send_sem, recv_sem).wait()
                out_ref[g] += land_ref[offset, g]


def middle_kernel(
    px, py, steps, spec_ref, vb_ref, va_ref, ca_ref, uh_ref, th_ref, xh_ref, xl_ref, fh_ref, fl_ref,
    kron_ref, ia_ref, sl_ref, back_ref, point_ref, gh_ref, acc_ref, mix_ref,
):
    step = pl.program_id(0)
    modes = MY * MZ
    nx = vb_ref.shape[2]
    chans, rows = vb_ref.shape[:2]

    @pl.when(step == 0)
    def _():
        build_fields(spec_ref, xh_ref, xl_ref, gh_ref, px, py)
        acc_ref[...] = jnp.zeros_like(acc_ref)
        point_ref[...] = jnp.zeros_like(point_ref)

    channel_mix(kron_ref, vb_ref, mix_ref)
    c0 = math.sqrt(2.0 / math.pi)

    def body(p, carry):
        field = dot(uh_ref[...], gh_ref[p])
        slopes = []
        for h in range(2):
            d = 2 * p + h
            v = field[:, h * nx : (h + 1) * nx] + mix_ref[d]
            v2 = v * v
            t = jnp.tanh(v * (c0 + (c0 * 0.044715) * v2))
            half = 0.5 + 0.5 * t
            ia_ref[d] = (va_ref[d].astype(F32) - v * half).astype(BF16)
            deriv = half + (0.5 * v) * (1.0 - t * t) * (c0 + (3.0 * c0 * 0.044715) * v2)
            slope = (ca_ref[d].astype(F32) * deriv).astype(BF16)
            sl_ref[d] = slope
            slopes.append(slope)
        both = jnp.concatenate(slopes, axis=1)
        acc_ref[p] += dot(th_ref[...], both)
        return carry

    lax.fori_loop(0, chans // 2, body, 0)

    def point_body(q, carry):
        start = pl.multiple_of(q * 2 * SUB, 2 * SUB)
        point_ref[...] += lax.dot_general(
            pair_of(vb_ref, start), pair_of(sl_ref, start), (((1,), (1,)), ((), ())), preferred_element_type=F32
        )
        return carry

    lax.fori_loop(0, rows // (2 * SUB), point_body, 0)

    @pl.when(step == steps - 1)
    def _():
        for g in range(chans // GROUP):
            parts = [acc_ref[2 * g + h] for h in range(2)]
            b0 = jnp.concatenate([part[:modes] for part in parts], axis=1)
            b1 = jnp.concatenate([part[modes:] for part in parts], axis=1)
            store_modes(back_ref, g, to_modes(b0, b1, fh_ref, fl_ref), px, py)


def last_kernel(
    px, py, spec_ref, sl_ref, cb_ref, uh_ref, xh_ref, xl_ref, kron_ref, out_ref, gh_ref, mix_ref
):
    nx = sl_ref.shape[2]

    @pl.when(pl.program_id(0) == 0)
    def _():
        build_fields(spec_ref, xh_ref, xl_ref, gh_ref, px, py)

    channel_mix(kron_ref, sl_ref, mix_ref)

    def body(p, carry):
        field = dot(uh_ref[...], gh_ref[p])
        for h in range(2):
            d = 2 * p + h
            value = cb_ref[d].astype(F32) + field[:, h * nx : (h + 1) * nx] + mix_ref[d]
            out_ref[d] = value.astype(BF16)
        return carry

    lax.fori_loop(0, sl_ref.shape[0] // 2, body, 0)


def whole(shape):
    return pl.BlockSpec(shape, lambda i: (0,) * len(shape), pipeline_mode=pl.Buffered(1))


def general_device(state_a, state_b, cotan_a, cotan_b, spectral_weight, point_weight):
    samples, px, py = (lax.axis_size(name) for name in ("dp", "px", "py"))
    _, chans, ys, zs, nx = state_b.shape
    ny, nz = ys * px, zs * py
    cells, modes = ys * zs, MY * MZ
    groups = chans // GROUP
    kk = MX // px
    tall, wide = modes // py, 2 * MX * GROUP // px
    own = tall * kk
    scale_f = 1.0 / math.sqrt(nx * ny * nz)
    scale_i = 1.0 / math.sqrt(MX * MY * MZ)
    grad_scale = math.sqrt(MX * MY * MZ / (samples * nx * ny * nz))
    point_scale = 1.0 / math.sqrt(samples * nx * ny * nz)
    shape = (ys, zs, ny, nz)
    th = analysis_table(shape).astype(BF16)
    uh = synthesis_table(shape).astype(BF16)
    xh, xl = x_tables(px, nx)
    fh, fl = (jnp.asarray(np.ascontiguousarray(table.transpose(0, 2, 1))) for table in (xh, xl))
    xh, xl = jnp.asarray(xh), jnp.asarray(xl)
    eye = jnp.eye(SUB, dtype=BF16)
    kron_f = (point_weight.T[:, None, :, None] * eye[None, :, None, :]).reshape(chans * SUB, chans * SUB)
    kron_b = (point_weight[:, None, :, None] * eye[None, :, None, :]).reshape(chans * SUB, chans * SUB)
    field_a, field_b, cot_a, cot_b = (
        value.reshape(chans, cells, nx) for value in (state_a, state_b, cotan_a, cotan_b)
    )
    part_shape = jax.ShapeDtypeStruct((px * py, groups, tall, wide), F32)
    params = pltpu.CompilerParams(vmem_limit_bytes=LIMIT)

    count = px * py
    own_shape = jax.ShapeDtypeStruct((groups, tall, wide), F32)
    exchange = [
        pltpu.VMEM(part_shape.shape, F32),
        pltpu.SemaphoreType.DMA((count, groups)),
        pltpu.SemaphoreType.DMA((count, groups)),
    ]

    def linked(number):
        return pltpu.CompilerParams(vmem_limit_bytes=LIMIT, collective_id=number, has_side_effects=True)

    def to_channels(value):
        value = value.reshape(groups, tall, GROUP, 2, kk).transpose(3, 0, 2, 1, 4)
        return value.reshape(2, chans, own)

    def gather(value, number):
        value = value.reshape(2, groups, GROUP, tall, kk).transpose(1, 3, 2, 0, 4)
        value = value.reshape(groups, tall, wide)
        return pl.pallas_call(
            lambda *refs: gather_kernel(px, py, *refs),
            in_specs=[pl.BlockSpec(memory_space=pltpu.VMEM)],
            out_specs=pl.BlockSpec(memory_space=pltpu.VMEM),
            out_shape=part_shape,
            scratch_shapes=[
                pltpu.VMEM(part_shape.shape, F32), pltpu.SemaphoreType.DMA((count,)), pltpu.SemaphoreType.DMA((count,)),
            ],
            compiler_params=linked(number),
            interpret=INTERPRET,
            name="gather",
        )(value)

    def mode_product(kernel, value, name):
        return pl.pallas_call(
            kernel,
            out_shape=jax.ShapeDtypeStruct((2, chans, own), F32),
            compiler_params=params,
            interpret=INTERPRET,
            name=name,
        )(value, weight)

    spectrum = pl.pallas_call(
        lambda *refs: forward_kernel(px, py, *refs),
        grid=(groups,),
        in_specs=[
            pl.BlockSpec((GROUP, cells, nx), lambda i: (i, 0, 0)),
            whole(th.shape), whole(fh.shape), whole(fl.shape),
        ],
        out_specs=whole(own_shape.shape),
        out_shape=own_shape,
        scratch_shapes=[pltpu.VMEM(part_shape.shape, F32)] + exchange,
        compiler_params=linked(0),
        interpret=INTERPRET,
        name="forward",
    )(field_b, th, fh, fl)
    weight = spectral_weight.transpose(3, 4, 5, 0, 1, 2).reshape(2, chans, chans, own)
    spectrum = to_channels(spectrum) * scale_f
    mixed = gather(mode_product(mix_kernel, spectrum, "mix") * scale_i, 1)

    rows = min(256, cells)
    steps = cells // rows
    block = pl.BlockSpec((chans, rows, nx), lambda i: (0, i, 0))
    u_block = pl.BlockSpec((rows, 2 * modes), lambda i: (i, 0))
    t_block = pl.BlockSpec((2 * modes, rows), lambda i: (0, i))
    field_shape = jax.ShapeDtypeStruct((chans, cells, nx), BF16)
    side = chans * SUB
    g_scratch = [pltpu.VMEM((chans // 2, 2 * modes, 2 * nx), BF16)]
    input_a, slope, back_part, point = pl.pallas_call(
        lambda *refs: middle_kernel(px, py, steps, *refs),
        grid=(steps,),
        in_specs=[
            whole(part_shape.shape), block, block, block, u_block, t_block,
            whole(xh.shape), whole(xl.shape), whole(fh.shape), whole(fl.shape), whole((side, side)),
        ],
        out_specs=[block, block, whole(part_shape.shape), whole((side, side))],
        out_shape=[field_shape, field_shape, part_shape, jax.ShapeDtypeStruct((side, side), F32)],
        scratch_shapes=g_scratch
        + [pltpu.VMEM((chans // 2, 2 * modes, 2 * nx), F32), pltpu.VMEM((chans, rows, nx), F32)],
        compiler_params=params,
        interpret=INTERPRET,
        name="middle",
    )(mixed, field_b, field_a, cot_a, uh, th, xh, xl, fh, fl, kron_f)

    back = pl.pallas_call(
        lambda *refs: scatter_kernel(px, py, *refs),
        in_specs=[pl.BlockSpec(memory_space=pltpu.VMEM)],
        out_specs=pl.BlockSpec(memory_space=pltpu.VMEM),
        out_shape=own_shape,
        scratch_shapes=exchange,
        compiler_params=linked(2),
        interpret=INTERPRET,
        name="scatter",
    )(back_part)
    back = to_channels(back) * scale_i
    grad_spec = gather(mode_product(adjoint_kernel, back, "adjoint") * scale_f, 3)
    grad_b = pl.pallas_call(
        lambda *refs: last_kernel(px, py, *refs),
        grid=(steps,),
        in_specs=[
            whole(part_shape.shape), block, block, u_block,
            whole(xh.shape), whole(xl.shape), whole((side, side)),
        ],
        out_specs=block,
        out_shape=field_shape,
        scratch_shapes=g_scratch + [pltpu.VMEM((chans, rows, nx), F32)],
        compiler_params=params,
        interpret=INTERPRET,
        name="last",
    )(grad_spec, slope, cot_b, uh, xh, xl, kron_b)

    share = chans // samples
    spec_all = lax.all_gather(spectrum, "dp", axis=0)
    back_all = lax.all_gather(back, "dp", axis=0)
    back_own = lax.dynamic_slice_in_dim(back_all, lax.axis_index("dp") * share, share, axis=2)
    p_real, p_imag = spec_all[:, 0, :, None], spec_all[:, 1, :, None]
    q_real, q_imag = back_own[:, 0, None], back_own[:, 1, None]
    grad_real = jnp.sum(p_real * q_real + p_imag * q_imag, axis=0)
    grad_imag = jnp.sum(p_real * q_imag - p_imag * q_real, axis=0)
    grad = jnp.stack([grad_real, grad_imag]) * grad_scale
    spectral_grad = grad.reshape(2, chans, share, tall // MZ, MZ, kk).transpose(3, 4, 5, 0, 1, 2)

    point = jnp.sum(point.reshape(chans, SUB, chans, SUB) * jnp.eye(SUB, dtype=F32)[None, :, None, :], axis=(1, 3))
    point_total = lax.psum(point, ("dp", "px", "py")) * point_scale
    full = state_b.shape
    return (input_a.reshape(full), grad_b.reshape(full), spectral_grad, point_total)


MESH = pl.DeviceIdType.MESH
CHUNK = 1024
TALL = 512
FUSED_LIMIT = 46 * 1024 * 1024
FINISH_LIMIT = 16 * 1024 * 1024


def fused_fits(shape, local_samples, samples, px, py):
    _, chans, ys, zs, nx = shape
    kk = MX // px
    tall = MY * MZ // py
    return (
        local_samples == 1
        and 2 * kk * GROUP == 128
        and nx == 128
        and MZ == 8
        and tall // MZ == 128 // kk
        and samples * GROUP == chans
        and (ys * zs) % CHUNK == 0
    )


def base_tables(shape):
    ys, zs, ny, nz = shape
    fy = np.where(np.arange(MY) < MY // 2, np.arange(MY), ny - MY + np.arange(MY))
    fz = np.where(np.arange(MZ) < MZ // 2, np.arange(MZ), nz - MZ + np.arange(MZ))
    ay = 2.0 * np.pi / ny * (fy[:, None] * np.arange(ys) % ny)
    az = 2.0 * np.pi / nz * (fz[:, None] * np.arange(zs) % nz)
    both = ay[:, None, :, None] + az[None, :, None, :]
    table = np.stack([np.cos(both), -np.sin(both)]).reshape(2 * MY * MZ, ys * zs).astype(BF16)
    py = 2.0 * np.pi / ny * (fy[None] * (np.arange(ny // ys) * ys)[:, None] % ny)
    pz = 2.0 * np.pi / nz * (fz[None] * (np.arange(nz // zs) * zs)[:, None] % nz)
    turn = py[:, None, :, None] + pz[None, :, None, :]
    turn = np.stack([np.cos(turn), np.sin(turn)], axis=2).reshape(-1, 2, MY * MZ, 1)
    turn = np.broadcast_to(turn, turn.shape[:3] + (128,)).astype(np.float32)
    return table, np.ascontiguousarray(table.T), np.ascontiguousarray(turn)


def wide_tables(px, nx):
    high, low = x_tables(px, nx)
    inverse = [np.concatenate([t[0], t[1]], axis=1) for t in (high, low)]
    forward = [np.ascontiguousarray(t.T) for t in inverse]
    return forward, inverse


def swap_bits(tiles, first):
    lane = lax.broadcasted_iota(jnp.int32, tiles[0].shape, 1)
    tiles = list(tiles)
    for i in range(len(tiles).bit_length() - 1):
        shift = 1 << (first + i)
        upper = lane // shift % 2 == 1
        for t in range(len(tiles)):
            if not t >> i & 1:
                u = t | 1 << i
                low, high = tiles[t], tiles[u]
                tiles[t] = jnp.where(upper, pltpu.roll(high, shift, 1), low)
                tiles[u] = jnp.where(upper, high, pltpu.roll(low, 128 - shift, 1))
    return tiles


def flip(tiles):
    return swap_bits(tiles, 7 - (len(tiles).bit_length() - 1))


def rows_of(ref, start):
    chans, _, nx = ref.shape
    parts = [ref[:, pl.ds(start + u * SUB, SUB), :].reshape(chans * SUB, nx) for u in range(TALL // SUB)]
    return jnp.concatenate(parts, axis=1)


def gelu_pair(v, first, cotan):
    c0 = math.sqrt(2.0 / math.pi)
    v2 = v * v
    half = 0.5 + 0.5 * jnp.tanh(v * (c0 + (c0 * 0.044715) * v2))
    rebuilt = (first.astype(F32) - v * half).astype(BF16)
    inner = v * (2.0 * c0 + (6.0 * c0 * 0.044715) * v2)
    slope = (cotan.astype(F32) * (half + (half * (1.0 - half)) * inner)).astype(BF16)
    return rebuilt, slope


def fused_kernel(
    scales, sb_hbm, sa_hbm, ca_hbm, cb_hbm, th_hbm, uh_hbm, fh_hbm, fl_hbm, xh_hbm, xl_hbm, w_hbm, turn_hbm, pw_ref,
    fa, sb, sg_ref, pt_ref, fc, mix, th, uh, fh, fl, xh, xl, kf, kb, w_raw, w, turn, part, land_x, land_y, gath, spec, spec_land, mode, back,
    back_land, grad, gf, acc, point, pt_src, pt_land,
    in_sem, w_sem, sb_sem, sa_sem, ca_sem, cb_sem, rx_s, rx_r, ry_s, ry_r, gy_s, gy_r, gx_s, gx_r,
    dp_s, dp_r, pt_s, pt_r,
):
    scale_f, scale_i, grad_scale = scales
    groups = part.shape[1]
    py = part.shape[2]
    tall = part.shape[3]
    cells, nx = sb.shape[1:]
    samples = spec_land.shape[0] + 1
    modes = MY * MZ
    ix, iy, idp = lax.axis_index("px"), lax.axis_index("py"), lax.axis_index("dp")
    other_x = 1 - ix

    def near_y(offset):
        return lax.rem(iy + offset, py)

    def near_dp(offset):
        return lax.rem(idp + offset, samples)

    def chan(g):
        return pl.ds(g * GROUP, GROUP)

    def load(index, src, dst):
        return pltpu.make_async_copy(src, dst, in_sem.at[index])

    tables = [
        load(0, th_hbm, th), load(1, fh_hbm, fh), load(2, fl_hbm, fl),
        load(3, turn_hbm.at[ix * py + iy], turn), load(4, xh_hbm, xh), load(5, xl_hbm, xl), load(6, uh_hbm, uh),
    ]

    def load_weight(l):
        slot = lax.rem(l, 2)
        return pltpu.make_async_copy(w_hbm.at[:, l], w_raw.at[slot], w_sem.at[slot])

    def field_load(src, dst, sem, g):
        return pltpu.make_async_copy(src.at[chan(g)], dst.at[chan(g)], sem.at[g])

    barrier = pltpu.get_barrier_semaphore()
    pl.semaphore_signal(barrier, inc=1, device_id={"px": other_x}, device_id_type=MESH)
    for offset in range(1, py):
        pl.semaphore_signal(barrier, inc=1, device_id={"py": near_y(offset)}, device_id_type=MESH)
    for offset in range(1, samples):
        pl.semaphore_signal(barrier, inc=1, device_id={"dp": near_dp(offset)}, device_id_type=MESH)

    field_load(sb_hbm, sb, sb_sem, 0).start()
    for i in range(4):
        tables[i].start()
    for g in range(1, groups):
        field_load(sb_hbm, sb, sb_sem, g).start()
    load_weight(0).start()
    for i in range(4, len(tables)):
        tables[i].start()
    for g in range(groups):
        field_load(sa_hbm, fa, sa_sem, g).start()
        field_load(ca_hbm, fc, ca_sem, g).start()
    pl.semaphore_wait(barrier, 1 + (py - 1) + (samples - 1))

    def remote(src, dst, send, recv, device):
        return pltpu.make_async_remote_copy(src, dst, send, recv, device_id=device, device_id_type=MESH)

    def reduce_x(f, g):
        return remote(
            part.at[other_x, g], land_x.at[f, g], rx_s.at[f, g], rx_r.at[f, g], {"px": other_x}
        )

    def reduce_y(f, g, offset):
        to = near_y(offset)
        return remote(
            part.at[ix, g, to], land_y.at[f, offset - 1, g], ry_s.at[f, offset - 1, g], ry_r.at[f, offset - 1, g],
            {"py": to},
        )

    def gather_y(f, g, offset):
        block = gath.at[f, ix, iy, g]
        return remote(block, block, gy_s.at[f, offset - 1, g], gy_r.at[f, offset - 1, g], {"py": near_y(offset)})

    def gather_x(f, g, offset):
        block = gath.at[f, ix, lax.rem(iy + py - offset, py), g]
        return remote(block, block, gx_s.at[f, offset, g], gx_r.at[f, offset, g], {"px": other_x})

    def after_x(f, g):
        reduce_x(f, g).wait_recv()
        part[ix, g] += land_x[f, g]
        for offset in range(1, py):
            reduce_y(f, g, offset).start()

    def finish_reduce(f, g):
        for offset in range(1, py):
            reduce_y(f, g, offset).wait_recv()
        value = part[ix, g, iy]
        for offset in range(1, py):
            value = value + land_y[f, offset - 1, g]
        return flip([value[8 * i : 8 * i + 8] for i in range(tall // 8)])

    def end_reduce_sends(f):
        for g in range(groups):
            reduce_x(f, g).wait_send()
            for offset in range(1, py):
                reduce_y(f, g, offset).wait_send()

    def start_gather(f, g, tiles):
        for i, tile in enumerate(flip(tiles)):
            gath[f, ix, iy, g, 8 * i : 8 * i + 8] = tile
        for offset in range(1, py):
            gather_y(f, g, offset).start()
        gather_x(f, g, 0).start()

    def forward_gather(f, g):
        for offset in range(1, py):
            gather_y(f, g, offset).wait_recv()
            gather_x(f, g, offset).start()

    def finish_gather(f, g):
        for offset in range(py):
            gather_x(f, g, offset).wait_recv()

    def end_gather_sends(f):
        for g in range(groups):
            for offset in range(1, py):
                gather_y(f, g, offset).wait_send()
            for offset in range(py):
                gather_x(f, g, offset).wait_send()

    def turns():
        cosine = jnp.concatenate([turn[0]] * GROUP, axis=1)
        sine = jnp.concatenate([turn[1]] * GROUP, axis=1)
        return cosine, sine

    def analyse(src, first, slot):
        value = jnp.concatenate([src[first], src[first + 1]], axis=1)
        acc[slot] = dot(th[...], value)

    def to_part(g):
        cosine, sine = turns()
        b0 = jnp.concatenate([acc[0, :modes], acc[1, :modes]], axis=1)
        b1 = jnp.concatenate([acc[0, modes:], acc[1, modes:]], axis=1)
        both = jnp.concatenate([b0 * cosine + b1 * sine, b1 * cosine - b0 * sine], axis=1)
        value = dot3(both, fh[...], fl[...])
        for i in range(2):
            part[i, g] = value[:, i * 128 : (i + 1) * 128].reshape(py, tall, 128)

    def build(f, g):
        value = jnp.concatenate([gath[f, i, :, g].reshape(modes, 128) for i in range(2)], axis=1)
        high, low = cut(value)
        cosine, sine = turns()
        wide = GROUP * nx
        both = dot(high, xh[...]) + dot(low, xh[...]) + dot(high, xl[...])
        g0, g1 = both[:, :wide], both[:, wide:]
        for t, field in enumerate((g0 * cosine - g1 * sine, g1 * cosine + g0 * sine)):
            field = field.astype(BF16)
            for h in range(2):
                gf[h, t * modes : (t + 1) * modes] = field[:, h * 2 * nx : (h + 1) * 2 * nx]

    def mix_rows(table, src, lo, hi):
        def step(q, carry):
            start = pl.multiple_of(q * TALL, TALL)
            value = dot(table[...], rows_of(src, start))
            for u in range(TALL // SUB):
                mix[:, pl.ds(start + u * SUB, SUB), :] = value[:, u * nx : (u + 1) * nx].reshape(-1, SUB, nx)
            return carry

        lax.fori_loop(lo, hi, step, 0)

    steps = cells // TALL
    side = point.shape[0]
    row = lax.broadcasted_iota(jnp.int32, (side, side), 0)
    column = lax.broadcasted_iota(jnp.int32, (side, side), 1)
    same = row % SUB == column % SUB

    for i in range(4):
        tables[i].wait()

    def forward(g, carry):
        field_load(sb_hbm, sb, sb_sem, g).wait()
        for p in range(2):
            analyse(sb, g * GROUP + 2 * p, p)
        to_part(g)
        reduce_x(0, g).start()

        @pl.when(g >= 1)
        def _():
            after_x(0, g - 1)

        return carry

    lax.fori_loop(0, groups, forward, 0)

    def turn_weight(l, carry):
        @pl.when(l + 1 < MZ)
        def _():
            load_weight(l + 1).start()

        load_weight(l).wait()
        slot = lax.rem(l, 2)
        chans = spec.shape[1]
        inner = 2 * chans
        kk = w_raw.shape[2] // inner
        tiles = []
        for t in range(inner):
            low, k = t // kk, t % kk
            some = range(low, w_raw.shape[1], inner // kk)
            rows = [w_raw[slot, j, k * inner : (k + 1) * inner, :] for j in some]
            tiles.append(jnp.concatenate(rows, axis=0).astype(F32).T)
        for r, tile in enumerate(swap_bits(tiles, 0)):
            w[r // chans, r % chans, l] = tile.astype(BF16)
        return carry

    lax.fori_loop(0, MZ, turn_weight, 0)
    spread = (row // SUB == column)[:, :SUB].astype(BF16)
    gathered = (lax.broadcasted_iota(jnp.int32, (SUB, side), 1) // SUB
                == lax.broadcasted_iota(jnp.int32, (SUB, side), 0)).astype(BF16)
    turned = lax.dot_general(spread, pw_ref[...], (((1,), (1,)), ((), ())), preferred_element_type=F32)
    kf[...] = jnp.where(same, dot(turned.astype(BF16), gathered), 0.0).astype(BF16)
    kb[...] = jnp.where(same, dot(dot(spread, pw_ref[...]).astype(BF16), gathered), 0.0).astype(BF16)
    mix_rows(kf, sb, 0, steps // 2)
    after_x(0, groups - 1)
    mix_rows(kf, sb, steps // 2, steps)

    def take_spectrum(g, carry):
        tiles = finish_reduce(0, g)
        for q, tile in enumerate(tiles):
            spec[q % 2, g * GROUP + q // 2] = tile * scale_f
        return carry

    lax.fori_loop(0, groups, take_spectrum, 0)

    def blend(l, carry):
        real = jnp.zeros(w.shape[3:], F32)
        imag = jnp.zeros(w.shape[3:], F32)
        for c in range(spec.shape[1]):
            w_real, w_imag = w[0, c, l].astype(F32), w[1, c, l].astype(F32)
            s_real, s_imag = spec[0, c, pl.ds(l, 1), :], spec[1, c, pl.ds(l, 1), :]
            real += s_real * w_real - s_imag * w_imag
            imag += s_real * w_imag + s_imag * w_real
        mode[0, pl.ds(l, real.shape[0], stride=MZ), :] = real * scale_i
        mode[1, pl.ds(l, real.shape[0], stride=MZ), :] = imag * scale_i
        return carry

    lax.fori_loop(0, MZ, blend, 0)
    for g in range(groups):
        start_gather(0, g, [mode[q % 2, (g * GROUP + q // 2) * MZ :][:MZ] for q in range(2 * GROUP)])

    def send_spec(offset):
        return remote(
            spec, spec_land.at[offset - 1], dp_s.at[0, offset - 1], dp_r.at[0, offset - 1], {"dp": near_dp(offset)}
        )

    def send_back(offset):
        to = near_dp(offset)
        return remote(
            back.at[to], back_land.at[offset - 1], dp_s.at[1, offset - 1], dp_r.at[1, offset - 1], {"dp": to}
        )

    for offset in range(1, samples):
        send_spec(offset).start()
    end_reduce_sends(0)
    for i in range(4, len(tables)):
        tables[i].wait()
    forward_gather(0, 0)

    def middle(g, carry):
        @pl.when(g + 1 < groups)
        def _():
            forward_gather(0, g + 1)

        finish_gather(0, g)
        build(0, g)
        field_load(sa_hbm, fa, sa_sem, g).wait()
        field_load(ca_hbm, fc, ca_sem, g).wait()

        def pair(p, inner):
            first = g * GROUP + 2 * p

            def rows(r, deep):
                some = pl.ds(pl.multiple_of(r * CHUNK, CHUNK), CHUNK)
                field = dot(uh[some, :], gf[p])
                for h in range(2):
                    v = field[:, h * nx : (h + 1) * nx] + mix[first + h, some, :]
                    rebuilt, slope = gelu_pair(v, fa[first + h, some, :], fc[first + h, some, :])
                    fa[first + h, some, :] = rebuilt
                    fc[first + h, some, :] = slope
                return deep

            lax.fori_loop(0, cells // CHUNK, rows, 0)
            analyse(fc, first, p)
            return inner

        lax.fori_loop(0, 2, pair, 0)
        to_part(g)
        reduce_x(1, g).start()

        @pl.when(g >= 1)
        def _():
            after_x(1, g - 1)

        return carry

    lax.fori_loop(0, groups, middle, 0)
    end_gather_sends(0)

    point[...] = jnp.zeros_like(point)

    def point_rows(lo, hi):
        def step(q, carry):
            start = pl.multiple_of(q * TALL, TALL)
            left, right = rows_of(sb, start), rows_of(fc, start)
            point[...] += lax.dot_general(left, right, (((1,), (1,)), ((), ())), preferred_element_type=F32)
            return carry

        lax.fori_loop(lo, hi, step, 0)

    point_rows(0, steps // 2)
    after_x(1, groups - 1)
    point_rows(steps // 2, steps)
    diagonal = jnp.where(same, point[...], 0.0)
    pt_src[0] = jnp.sum(diagonal.reshape(-1, SUB, point.shape[1]), axis=1)

    def sum_x():
        return remote(pt_src.at[0], pt_land.at[0, 0], pt_s.at[0], pt_r.at[0], {"px": other_x})

    def sum_y(offset):
        return remote(
            pt_src.at[1], pt_land.at[1, iy], pt_s.at[offset], pt_r.at[offset], {"py": near_y(offset)}
        )

    def sum_dp(offset):
        return remote(
            pt_src.at[2], pt_land.at[2, idp], pt_s.at[py - 1 + offset], pt_r.at[py - 1 + offset],
            {"dp": near_dp(offset)},
        )

    sum_x().start()

    def take_back(g, carry):
        tiles = finish_reduce(1, g)
        for q, tile in enumerate(tiles):
            back[g, q % 2, q // 2] = tile * scale_i
            mode[q % 2, pl.ds(pl.multiple_of((g * GROUP + q // 2) * MZ, MZ), MZ), :] = tile * scale_i
        return carry

    lax.fori_loop(0, groups, take_back, 0)

    def adjoint(g, carry):
        for l in range(MZ):
            b_real, b_imag = (mode[i, pl.ds(l, w.shape[3], stride=MZ), :] for i in range(2))
            for c in range(GROUP):
                w_real, w_imag = w[0, g * GROUP + c, l].astype(F32), w[1, g * GROUP + c, l].astype(F32)
                real = jnp.sum(b_real * w_real + b_imag * w_imag, axis=0, keepdims=True)
                imag = jnp.sum(b_imag * w_real - b_real * w_imag, axis=0, keepdims=True)
                grad[2 * c, l : l + 1] = real * scale_f
                grad[2 * c + 1, l : l + 1] = imag * scale_f
        start_gather(1, g, [grad[q] for q in range(2 * GROUP)])
        return carry

    lax.fori_loop(0, groups, adjoint, 0)
    for offset in range(1, samples):
        send_back(offset).start()
    for g in range(groups):
        field_load(cb_hbm, sb, cb_sem, g).start()
    sum_x().wait()
    pt_src[1] = pt_src[0] + pt_land[0, 0]
    pt_land[1, iy] = pt_src[1]
    for offset in range(1, py):
        sum_y(offset).start()
    mix_rows(kb, fc, 0, steps // 2)
    forward_gather(1, 0)
    for offset in range(1, py):
        sum_y(offset).wait()
    pt_src[2] = sum(pt_land[1, i] for i in range(py))
    pt_land[2, idp] = pt_src[2]
    for offset in range(1, samples):
        sum_dp(offset).start()
    mix_rows(kb, fc, steps // 2, steps)

    def last(g, carry):
        @pl.when(g + 1 < groups)
        def _():
            forward_gather(1, g + 1)

        finish_gather(1, g)
        build(1, g)
        field_load(cb_hbm, sb, cb_sem, g).wait()

        def pair(p, inner):
            first = g * GROUP + 2 * p

            def rows(r, deep):
                some = pl.ds(pl.multiple_of(r * CHUNK, CHUNK), CHUNK)
                field = dot(uh[some, :], gf[p])
                for h in range(2):
                    value = sb[first + h, some, :].astype(F32) + field[:, h * nx : (h + 1) * nx]
                    sb[first + h, some, :] = (value + mix[first + h, some, :]).astype(BF16)
                return deep

            lax.fori_loop(0, cells // CHUNK, rows, 0)
            return inner

        lax.fori_loop(0, 2, pair, 0)
        return carry

    lax.fori_loop(0, groups, last, 0)

    for offset in range(1, samples):
        send_spec(offset).wait()
        send_back(offset).wait()

    def outer(c, carry):
        for d in range(GROUP):
            real = jnp.zeros((8, 128), F32)
            imag = jnp.zeros((8, 128), F32)
            for s in range(samples):
                if s == 0:
                    p_real, p_imag = spec[0, c], spec[1, c]
                    q_real, q_imag = back[idp, 0, d], back[idp, 1, d]
                else:
                    p_real, p_imag = spec_land[s - 1, 0, c], spec_land[s - 1, 1, c]
                    q_real, q_imag = back_land[s - 1, 0, d], back_land[s - 1, 1, d]
                real += p_real * q_real + p_imag * q_imag
                imag += p_real * q_imag - p_imag * q_real
            sg_ref[0, d, pl.ds(pl.multiple_of(c * MZ, MZ), MZ), :] = real * grad_scale
            sg_ref[1, d, pl.ds(pl.multiple_of(c * MZ, MZ), MZ), :] = imag * grad_scale
        return carry

    lax.fori_loop(0, spec.shape[1], outer, 0)
    for offset in range(1, samples):
        sum_dp(offset).wait()
    pt_ref[...] = sum(pt_land[2, i] for i in range(samples))
    end_reduce_sends(1)
    end_gather_sends(1)


def finish_kernel(point_scale, ia_ref, gb_ref, sg_ref, pt_ref, ia_hbm, gb_hbm, out_hbm, point_ref, out, copy_sem, out_sem):
    parts = copy_sem.shape[1]
    each = ia_ref.shape[0] // parts
    jj, rows, chans = out.shape[1:]
    inner = 2 * GROUP
    kk = rows // inner

    def field_copy(which, i):
        some = pl.ds(i * each, each)
        src, dst = ((ia_ref, ia_hbm), (gb_ref, gb_hbm))[which]
        return pltpu.make_async_copy(src.at[some], dst.at[some], copy_sem.at[which, i])

    def store(l):
        slot = lax.rem(l, 2)
        return pltpu.make_async_copy(out.at[slot], out_hbm.at[:, l], out_sem.at[slot])

    for i in range(parts):
        for which in range(2):
            field_copy(which, i).start()

    def spread(l, carry):
        @pl.when(l >= 2)
        def _():
            store(l - 2).wait()

        for r in range(inner):
            value = sg_ref[r // GROUP, r % GROUP, pl.ds(l, chans, stride=MZ), :].T
            for j in range(jj):
                out[lax.rem(l, 2), j, pl.ds(r, kk, stride=inner), :] = value[j * kk : (j + 1) * kk]
        store(l).start()
        return carry

    lax.fori_loop(0, MZ, spread, 0)
    value = pt_ref[...]
    row = lax.broadcasted_iota(jnp.int32, (value.shape[1], chans), 0)
    column = lax.broadcasted_iota(jnp.int32, (value.shape[1], chans), 1)
    ones = (row // SUB == column).astype(BF16)
    total = jnp.zeros(point_ref.shape, F32)
    for _ in range(3):
        part = value.astype(BF16)
        total += dot(part, ones)
        value -= part.astype(F32)
    point_ref[...] = total * point_scale
    store(MZ - 2).wait()
    store(MZ - 1).wait()
    for i in range(parts):
        for which in range(2):
            field_copy(which, i).wait()


def fused_device(state_a, state_b, cotan_a, cotan_b, spectral_weight, point_weight):
    samples, px, py = (lax.axis_size(name) for name in ("dp", "px", "py"))
    _, chans, ys, zs, nx = state_b.shape
    ny, nz = ys * px, zs * py
    cells, modes = ys * zs, MY * MZ
    groups = chans // GROUP
    kk = MX // px
    tall = modes // py
    total = nx * ny * nz
    scales = (
        1.0 / math.sqrt(total), 1.0 / math.sqrt(MX * MY * MZ), math.sqrt(MX * MY * MZ / (samples * total)),
    )
    th, uh, turn = (jnp.asarray(t) for t in base_tables((ys, zs, ny, nz)))
    (fh, fl), (xh, xl) = wide_tables(px, nx)
    fh, fl, xh, xl = (jnp.asarray(t) for t in (fh, fl, xh, xl))
    side = chans * SUB
    jj, ll = tall // MZ, MZ
    weight = spectral_weight.reshape(jj, ll, kk * 2 * chans, chans)
    fields = [value.reshape(chans, cells, nx) for value in (state_b, state_a, cotan_a, cotan_b)]
    field = jax.ShapeDtypeStruct((chans, cells, nx), BF16)
    any_spec = pl.BlockSpec(memory_space=pl.ANY)
    vmem_spec = pl.BlockSpec(memory_space=pltpu.VMEM)
    dma = pltpu.SemaphoreType.DMA
    near = py - 1
    input_a, grad_b, sg, point = pl.pallas_call(
        lambda *refs: fused_kernel(scales, *refs),
        in_specs=[any_spec] * 12 + [vmem_spec],
        out_specs=[vmem_spec] * 4,
        out_shape=[
            pltpu.VMEM(field.shape, BF16), pltpu.VMEM(field.shape, BF16),
            pltpu.VMEM((2, GROUP, chans * MZ, 128), F32), pltpu.VMEM((chans, side), F32),
        ],
        scratch_shapes=[
            pltpu.VMEM((chans, cells, nx), BF16), pltpu.VMEM((chans, cells, nx), F32),
            pltpu.VMEM(th.shape, BF16), pltpu.VMEM(uh.shape, BF16), pltpu.VMEM(fh.shape, BF16),
            pltpu.VMEM(fl.shape, BF16), pltpu.VMEM(xh.shape, BF16), pltpu.VMEM(xl.shape, BF16),
            pltpu.VMEM((side, side), BF16), pltpu.VMEM((side, side), BF16),
            pltpu.VMEM((2, jj) + weight.shape[2:], BF16), pltpu.VMEM((2, chans, MZ, chans, 128), BF16),
            pltpu.VMEM(turn.shape[1:], F32),
            pltpu.VMEM((px, groups, py, tall, 128), F32),
            pltpu.VMEM((2, groups, py, tall, 128), F32),
            pltpu.VMEM((2, near, groups, tall, 128), F32),
            pltpu.VMEM((2, px, py, groups, tall, 128), F32),
            pltpu.VMEM((2, chans, MZ, 128), F32),
            pltpu.VMEM((samples - 1, 2, chans, MZ, 128), F32),
            pltpu.VMEM((2, chans * MZ, 128), F32),
            pltpu.VMEM((samples, 2, GROUP, MZ, 128), F32),
            pltpu.VMEM((samples - 1, 2, GROUP, MZ, 128), F32),
            pltpu.VMEM((2 * GROUP, MZ, 128), F32),
            pltpu.VMEM((2, 2 * modes, 2 * nx), BF16),
            pltpu.VMEM((2, 2 * modes, 2 * nx), F32),
            pltpu.VMEM((side, side), F32),
            pltpu.VMEM((3, chans, side), F32),
            pltpu.VMEM((3, max(py, samples), chans, side), F32),
            dma((7,)), dma((2,)), dma((groups,)), dma((groups,)), dma((groups,)), dma((groups,)),
            dma((2, groups)), dma((2, groups)), dma((2, near, groups)), dma((2, near, groups)),
            dma((2, near, groups)), dma((2, near, groups)), dma((2, py, groups)), dma((2, py, groups)),
            dma((2, samples - 1)), dma((2, samples - 1)), dma((1 + near + samples - 1,)), dma((1 + near + samples - 1,)),
        ],
        compiler_params=pltpu.CompilerParams(
            vmem_limit_bytes=FUSED_LIMIT, collective_id=4, has_side_effects=True
        ),
        interpret=INTERPRET,
        name="fused",
    )(*fields, th, uh, fh, fl, xh, xl, weight, turn, point_weight)
    spread = (jj, ll, kk * 2 * GROUP, chans)
    point_scale = 1.0 / math.sqrt(samples * total)
    input_a, grad_b, spectral_grad, point_total = pl.pallas_call(
        lambda *refs: finish_kernel(point_scale, *refs),
        in_specs=[vmem_spec] * 4,
        out_specs=[any_spec] * 3 + [vmem_spec],
        out_shape=[
            field, field, jax.ShapeDtypeStruct(spread, F32), jax.ShapeDtypeStruct((chans, chans), F32),
        ],
        scratch_shapes=[pltpu.VMEM((2, jj) + spread[2:], F32), dma((2, groups)), dma((2,))],
        compiler_params=pltpu.CompilerParams(vmem_limit_bytes=FINISH_LIMIT),
        interpret=INTERPRET,
        name="finish",
    )(input_a, grad_b, sg, point)
    spectral_grad = spectral_grad.reshape(jj, ll, kk, 2, GROUP, chans).transpose(0, 1, 2, 3, 5, 4)
    full = state_b.shape
    return (input_a.reshape(full), grad_b.reshape(full), spectral_grad, point_total)


def solution(mesh):
    sizes = dict(mesh.shape)

    def body(*values):
        fits = fused_fits(values[1].shape, values[1].shape[0], sizes["dp"], sizes["px"], sizes["py"])
        return (fused_device if fits else general_device)(*values)

    return jax.shard_map(
        body,
        mesh=mesh,
        in_specs=(
            P("dp", None, "px", "py", None),
            P("dp", None, "px", "py", None),
            P("dp", None, "px", "py", None),
            P("dp", None, "px", "py", None),
            P("py", None, "px", None, None, None),
            P(),
        ),
        out_specs=(
            P("dp", None, "px", "py", None),
            P("dp", None, "px", "py", None),
            P("py", None, "px", None, None, "dp"),
            P(),
        ),
        check_vma=False,
    )
```

```python
import math

import jax
import jax.numpy as jnp
import numpy as np
from jax import lax
from jax.experimental import pallas as pl
from jax.experimental.pallas import tpu as pltpu
from jax.sharding import PartitionSpec as P

MX = 32
MY = 32
MZ = 8
GROUP = 4
SUB = 16
LIMIT = 56 * 1024 * 1024
INTERPRET = False
F32 = jnp.float32
BF16 = jnp.bfloat16


def kept(length_all, length_kept, position):
    return jnp.where(position < length_kept // 2, position, length_all - length_kept + position)


def angle(product, length_all):
    return (product % length_all).astype(F32) * (2.0 * math.pi / length_all)


def synthesis_table(shape):
    ys, zs, ny, nz = shape
    mode = lax.broadcasted_iota(jnp.int32, (1, MY * MZ), 1)
    fy = kept(ny, MY, mode // MZ)
    fz = kept(nz, MZ, mode % MZ)
    y = lax.axis_index("px") * ys + lax.broadcasted_iota(jnp.int32, (ys, 1), 0)
    z = lax.axis_index("py") * zs + lax.broadcasted_iota(jnp.int32, (zs, 1), 0)
    ay = angle(fy * y, ny)
    az = angle(fz * z, nz)
    cy, sy = jnp.cos(ay)[:, None, :], jnp.sin(ay)[:, None, :]
    cz, sz = jnp.cos(az)[None], jnp.sin(az)[None]
    table = jnp.concatenate([cy * cz - sy * sz, -(sy * cz + cy * sz)], axis=2)
    return table.reshape(ys * zs, 2 * MY * MZ)


def analysis_table(shape):
    ys, zs, ny, nz = shape
    cell = lax.broadcasted_iota(jnp.int32, (1, ys * zs), 1)
    y = lax.axis_index("px") * ys + cell // zs
    z = lax.axis_index("py") * zs + cell % zs
    fy = kept(ny, MY, lax.broadcasted_iota(jnp.int32, (MY, 1), 0))
    fz = kept(nz, MZ, lax.broadcasted_iota(jnp.int32, (MZ, 1), 0))
    ay = angle(fy * y, ny)
    az = angle(fz * z, nz)
    cy, sy = jnp.cos(ay)[:, None, :], jnp.sin(ay)[:, None, :]
    cz, sz = jnp.cos(az)[None], jnp.sin(az)[None]
    table = jnp.stack([cy * cz - sy * sz, -(sy * cz + cy * sz)])
    return table.reshape(2 * MY * MZ, ys * zs)


def x_tables(px, nx):
    kk = MX // px
    k = np.arange(MX).reshape(px, kk)
    phase = 2.0 * np.pi / nx * (k[:, :, None] * np.arange(nx) % nx)
    cosine, sine = np.cos(phase), np.sin(phase)
    table = np.zeros((2, px, GROUP, 2, kk, GROUP, nx))
    for c in range(GROUP):
        table[0, :, c, 0, :, c] = cosine
        table[0, :, c, 1, :, c] = -sine
        table[1, :, c, 0, :, c] = sine
        table[1, :, c, 1, :, c] = cosine
    table = table.reshape(2, 2 * MX * GROUP, GROUP * nx)
    high = table.astype(BF16)
    low = (table - high.astype(np.float64)).astype(BF16)
    return high, low


def dot(a, b):
    return jnp.dot(a, b, preferred_element_type=F32)


def cut(value):
    high = value.astype(BF16)
    return high, (value - high.astype(F32)).astype(BF16)


def dot3(a, high, low):
    ahigh, alow = cut(a)
    return dot(ahigh, high) + dot(alow, high) + dot(ahigh, low)


def to_modes(b0, b1, xh_ref, xl_ref):
    return dot3(b0, xh_ref[0], xl_ref[0]) + dot3(b1, xh_ref[1], xl_ref[1])


def store_modes(out_ref, group, value, px, py):
    wide = value.shape[1] // px
    tall = value.shape[0] // py
    for i in range(px):
        for j in range(py):
            out_ref[i * py + j, group] = value[j * tall : (j + 1) * tall, i * wide : (i + 1) * wide]


def build_fields(spec_ref, xh_ref, xl_ref, gh_ref, px, py):
    modes = MY * MZ
    for g in range(spec_ref.shape[1]):
        rows = []
        for j in range(py):
            rows.append(jnp.concatenate([spec_ref[i * py + j, g] for i in range(px)], axis=1))
        value = jnp.concatenate(rows, axis=0)
        for t in range(2):
            high = dot3(value, xh_ref[t], xl_ref[t]).astype(BF16)
            half = high.shape[1] // 2
            for h in range(2):
                gh_ref[2 * g + h, t * modes : (t + 1) * modes] = high[:, h * half : (h + 1) * half]


def pair_of(ref, start):
    chans, _, nx = ref.shape
    first = ref[:, pl.ds(start, SUB), :].reshape(chans * SUB, nx)
    second = ref[:, pl.ds(start + SUB, SUB), :].reshape(chans * SUB, nx)
    return jnp.concatenate([first, second], axis=1)


def channel_mix(kron_ref, in_ref, out_ref):
    chans, rows, nx = in_ref.shape

    def body(q, carry):
        start = pl.multiple_of(q * 2 * SUB, 2 * SUB)
        value = dot(kron_ref[...], pair_of(in_ref, start))
        out_ref[:, pl.ds(start, SUB), :] = value[:, :nx].reshape(chans, SUB, nx)
        out_ref[:, pl.ds(start + SUB, SUB), :] = value[:, nx:].reshape(chans, SUB, nx)
        return carry

    lax.fori_loop(0, rows // (2 * SUB), body, 0)


def position(py):
    return lax.axis_index("px") * py + lax.axis_index("py")


def partner(px, py, offset):
    other = lax.rem(position(py) + offset, px * py)
    return other, {"px": lax.div(other, py), "py": lax.rem(other, py)}


def greet(px, py):
    barrier = pltpu.get_barrier_semaphore()
    for offset in range(1, px * py):
        pl.semaphore_signal(
            barrier, inc=1, device_id=partner(px, py, offset)[1], device_id_type=pl.DeviceIdType.MESH
        )
    pl.semaphore_wait(barrier, px * py - 1)


def scatter_copy(px, py, offset, group, part_ref, land_ref, send_sem, recv_sem):
    other, device = partner(px, py, offset)
    return pltpu.make_async_remote_copy(
        part_ref.at[other, group], land_ref.at[offset, group], send_sem.at[offset, group], recv_sem.at[offset, group],
        device_id=device, device_id_type=pl.DeviceIdType.MESH,
    )


def scatter_kernel(px, py, part_ref, out_ref, land_ref, send_sem, recv_sem):
    count = px * py
    greet(px, py)
    groups = part_ref.shape[1]
    for g in range(groups):
        for offset in range(1, count):
            scatter_copy(px, py, offset, g, part_ref, land_ref, send_sem, recv_sem).start()
    out_ref[...] = part_ref[position(py)]
    for g in range(groups):
        for offset in range(1, count):
            scatter_copy(px, py, offset, g, part_ref, land_ref, send_sem, recv_sem).wait()
            out_ref[g] += land_ref[offset, g]


def gather_kernel(px, py, own_ref, out_ref, land_ref, send_sem, recv_sem):
    count = px * py
    greet(px, py)
    copies = []
    for offset in range(1, count):
        copies.append(
            pltpu.make_async_remote_copy(
                own_ref, land_ref.at[offset], send_sem.at[offset], recv_sem.at[offset],
                device_id=partner(px, py, offset)[1], device_id_type=pl.DeviceIdType.MESH,
            )
        )
        copies[-1].start()
    here = position(py)
    out_ref[here] = own_ref[...]
    for offset in range(1, count):
        copies[offset - 1].wait()
        out_ref[lax.rem(here + count - offset, count)] = land_ref[offset]


def mix_kernel(s_ref, w_ref, out_ref):
    chans = s_ref.shape[1]
    real = jnp.zeros(out_ref.shape[1:], F32)
    imag = jnp.zeros(out_ref.shape[1:], F32)
    for c in range(chans):
        s_real, s_imag = s_ref[0, c : c + 1], s_ref[1, c : c + 1]
        w_real, w_imag = w_ref[0, c].astype(F32), w_ref[1, c].astype(F32)
        real += s_real * w_real - s_imag * w_imag
        imag += s_real * w_imag + s_imag * w_real
    out_ref[0] = real
    out_ref[1] = imag


def adjoint_kernel(b_ref, w_ref, out_ref):
    b_real, b_imag = b_ref[0], b_ref[1]
    for c in range(w_ref.shape[1]):
        w_real, w_imag = w_ref[0, c].astype(F32), w_ref[1, c].astype(F32)
        out_ref[0, c : c + 1] = jnp.sum(b_real * w_real + b_imag * w_imag, axis=0, keepdims=True)
        out_ref[1, c : c + 1] = jnp.sum(b_imag * w_real - b_real * w_imag, axis=0, keepdims=True)


def forward_kernel(
    px, py, v_ref, th_ref, xh_ref, xl_ref, out_ref, part_ref, land_ref, send_sem, recv_sem
):
    modes = MY * MZ
    parts = []
    for p in range(GROUP // 2):
        value = jnp.concatenate([v_ref[2 * p], v_ref[2 * p + 1]], axis=1)
        parts.append(dot(th_ref[...], value))
    b0 = jnp.concatenate([part[:modes] for part in parts], axis=1)
    b1 = jnp.concatenate([part[modes:] for part in parts], axis=1)
    step = pl.program_id(0)
    store_modes(part_ref, step, to_modes(b0, b1, xh_ref, xl_ref), px, py)
    count = px * py

    @pl.when(step == 0)
    def _():
        greet(px, py)

    for offset in range(1, count):
        scatter_copy(px, py, offset, step, part_ref, land_ref, send_sem, recv_sem).start()

    @pl.when(step == pl.num_programs(0) - 1)
    def _():
        out_ref[...] = part_ref[position(py)]
        for g in range(part_ref.shape[1]):
            for offset in range(1, count):
                scatter_copy(px, py, offset, g, part_ref, land_ref, send_sem, recv_sem).wait()
                out_ref[g] += land_ref[offset, g]


def middle_kernel(
    px, py, steps, spec_ref, vb_ref, va_ref, ca_ref, uh_ref, th_ref, xh_ref, xl_ref, fh_ref, fl_ref,
    kron_ref, ia_ref, sl_ref, back_ref, point_ref, gh_ref, acc_ref, mix_ref,
):
    step = pl.program_id(0)
    modes = MY * MZ
    nx = vb_ref.shape[2]
    chans, rows = vb_ref.shape[:2]

    @pl.when(step == 0)
    def _():
        build_fields(spec_ref, xh_ref, xl_ref, gh_ref, px, py)
        acc_ref[...] = jnp.zeros_like(acc_ref)
        point_ref[...] = jnp.zeros_like(point_ref)

    channel_mix(kron_ref, vb_ref, mix_ref)
    c0 = math.sqrt(2.0 / math.pi)

    def body(p, carry):
        field = dot(uh_ref[...], gh_ref[p])
        slopes = []
        for h in range(2):
            d = 2 * p + h
            v = field[:, h * nx : (h + 1) * nx] + mix_ref[d]
            v2 = v * v
            t = jnp.tanh(v * (c0 + (c0 * 0.044715) * v2))
            half = 0.5 + 0.5 * t
            ia_ref[d] = (va_ref[d].astype(F32) - v * half).astype(BF16)
            deriv = half + (0.5 * v) * (1.0 - t * t) * (c0 + (3.0 * c0 * 0.044715) * v2)
            slope = (ca_ref[d].astype(F32) * deriv).astype(BF16)
            sl_ref[d] = slope
            slopes.append(slope)
        both = jnp.concatenate(slopes, axis=1)
        acc_ref[p] += dot(th_ref[...], both)
        return carry

    lax.fori_loop(0, chans // 2, body, 0)

    def point_body(q, carry):
        start = pl.multiple_of(q * 2 * SUB, 2 * SUB)
        point_ref[...] += lax.dot_general(
            pair_of(vb_ref, start), pair_of(sl_ref, start), (((1,), (1,)), ((), ())), preferred_element_type=F32
        )
        return carry

    lax.fori_loop(0, rows // (2 * SUB), point_body, 0)

    @pl.when(step == steps - 1)
    def _():
        for g in range(chans // GROUP):
            parts = [acc_ref[2 * g + h] for h in range(2)]
            b0 = jnp.concatenate([part[:modes] for part in parts], axis=1)
            b1 = jnp.concatenate([part[modes:] for part in parts], axis=1)
            store_modes(back_ref, g, to_modes(b0, b1, fh_ref, fl_ref), px, py)


def last_kernel(
    px, py, spec_ref, sl_ref, cb_ref, uh_ref, xh_ref, xl_ref, kron_ref, out_ref, gh_ref, mix_ref
):
    nx = sl_ref.shape[2]

    @pl.when(pl.program_id(0) == 0)
    def _():
        build_fields(spec_ref, xh_ref, xl_ref, gh_ref, px, py)

    channel_mix(kron_ref, sl_ref, mix_ref)

    def body(p, carry):
        field = dot(uh_ref[...], gh_ref[p])
        for h in range(2):
            d = 2 * p + h
            value = cb_ref[d].astype(F32) + field[:, h * nx : (h + 1) * nx] + mix_ref[d]
            out_ref[d] = value.astype(BF16)
        return carry

    lax.fori_loop(0, sl_ref.shape[0] // 2, body, 0)


def whole(shape):
    return pl.BlockSpec(shape, lambda i: (0,) * len(shape), pipeline_mode=pl.Buffered(1))


def general_device(state_a, state_b, cotan_a, cotan_b, spectral_weight, point_weight):
    samples, px, py = (lax.axis_size(name) for name in ("dp", "px", "py"))
    _, chans, ys, zs, nx = state_b.shape
    ny, nz = ys * px, zs * py
    cells, modes = ys * zs, MY * MZ
    groups = chans // GROUP
    kk = MX // px
    tall, wide = modes // py, 2 * MX * GROUP // px
    own = tall * kk
    scale_f = 1.0 / math.sqrt(nx * ny * nz)
    scale_i = 1.0 / math.sqrt(MX * MY * MZ)
    grad_scale = math.sqrt(MX * MY * MZ / (samples * nx * ny * nz))
    point_scale = 1.0 / math.sqrt(samples * nx * ny * nz)
    shape = (ys, zs, ny, nz)
    th = analysis_table(shape).astype(BF16)
    uh = synthesis_table(shape).astype(BF16)
    xh, xl = x_tables(px, nx)
    fh, fl = (jnp.asarray(np.ascontiguousarray(table.transpose(0, 2, 1))) for table in (xh, xl))
    xh, xl = jnp.asarray(xh), jnp.asarray(xl)
    eye = jnp.eye(SUB, dtype=BF16)
    kron_f = (point_weight.T[:, None, :, None] * eye[None, :, None, :]).reshape(chans * SUB, chans * SUB)
    kron_b = (point_weight[:, None, :, None] * eye[None, :, None, :]).reshape(chans * SUB, chans * SUB)
    field_a, field_b, cot_a, cot_b = (
        value.reshape(chans, cells, nx) for value in (state_a, state_b, cotan_a, cotan_b)
    )
    part_shape = jax.ShapeDtypeStruct((px * py, groups, tall, wide), F32)
    params = pltpu.CompilerParams(vmem_limit_bytes=LIMIT)

    count = px * py
    own_shape = jax.ShapeDtypeStruct((groups, tall, wide), F32)
    exchange = [
        pltpu.VMEM(part_shape.shape, F32),
        pltpu.SemaphoreType.DMA((count, groups)),
        pltpu.SemaphoreType.DMA((count, groups)),
    ]

    def linked(number):
        return pltpu.CompilerParams(vmem_limit_bytes=LIMIT, collective_id=number, has_side_effects=True)

    def to_channels(value):
        value = value.reshape(groups, tall, GROUP, 2, kk).transpose(3, 0, 2, 1, 4)
        return value.reshape(2, chans, own)

    def gather(value, number):
        value = value.reshape(2, groups, GROUP, tall, kk).transpose(1, 3, 2, 0, 4)
        value = value.reshape(groups, tall, wide)
        return pl.pallas_call(
            lambda *refs: gather_kernel(px, py, *refs),
            in_specs=[pl.BlockSpec(memory_space=pltpu.VMEM)],
            out_specs=pl.BlockSpec(memory_space=pltpu.VMEM),
            out_shape=part_shape,
            scratch_shapes=[
                pltpu.VMEM(part_shape.shape, F32), pltpu.SemaphoreType.DMA((count,)), pltpu.SemaphoreType.DMA((count,)),
            ],
            compiler_params=linked(number),
            interpret=INTERPRET,
            name="gather",
        )(value)

    def mode_product(kernel, value, name):
        return pl.pallas_call(
            kernel,
            out_shape=jax.ShapeDtypeStruct((2, chans, own), F32),
            compiler_params=params,
            interpret=INTERPRET,
            name=name,
        )(value, weight)

    spectrum = pl.pallas_call(
        lambda *refs: forward_kernel(px, py, *refs),
        grid=(groups,),
        in_specs=[
            pl.BlockSpec((GROUP, cells, nx), lambda i: (i, 0, 0)),
            whole(th.shape), whole(fh.shape), whole(fl.shape),
        ],
        out_specs=whole(own_shape.shape),
        out_shape=own_shape,
        scratch_shapes=[pltpu.VMEM(part_shape.shape, F32)] + exchange,
        compiler_params=linked(0),
        interpret=INTERPRET,
        name="forward",
    )(field_b, th, fh, fl)
    weight = spectral_weight.transpose(3, 4, 5, 0, 1, 2).reshape(2, chans, chans, own)
    spectrum = to_channels(spectrum) * scale_f
    mixed = gather(mode_product(mix_kernel, spectrum, "mix") * scale_i, 1)

    rows = min(256, cells)
    steps = cells // rows
    block = pl.BlockSpec((chans, rows, nx), lambda i: (0, i, 0))
    u_block = pl.BlockSpec((rows, 2 * modes), lambda i: (i, 0))
    t_block = pl.BlockSpec((2 * modes, rows), lambda i: (0, i))
    field_shape = jax.ShapeDtypeStruct((chans, cells, nx), BF16)
    side = chans * SUB
    g_scratch = [pltpu.VMEM((chans // 2, 2 * modes, 2 * nx), BF16)]
    input_a, slope, back_part, point = pl.pallas_call(
        lambda *refs: middle_kernel(px, py, steps, *refs),
        grid=(steps,),
        in_specs=[
            whole(part_shape.shape), block, block, block, u_block, t_block,
            whole(xh.shape), whole(xl.shape), whole(fh.shape), whole(fl.shape), whole((side, side)),
        ],
        out_specs=[block, block, whole(part_shape.shape), whole((side, side))],
        out_shape=[field_shape, field_shape, part_shape, jax.ShapeDtypeStruct((side, side), F32)],
        scratch_shapes=g_scratch
        + [pltpu.VMEM((chans // 2, 2 * modes, 2 * nx), F32), pltpu.VMEM((chans, rows, nx), F32)],
        compiler_params=params,
        interpret=INTERPRET,
        name="middle",
    )(mixed, field_b, field_a, cot_a, uh, th, xh, xl, fh, fl, kron_f)

    back = pl.pallas_call(
        lambda *refs: scatter_kernel(px, py, *refs),
        in_specs=[pl.BlockSpec(memory_space=pltpu.VMEM)],
        out_specs=pl.BlockSpec(memory_space=pltpu.VMEM),
        out_shape=own_shape,
        scratch_shapes=exchange,
        compiler_params=linked(2),
        interpret=INTERPRET,
        name="scatter",
    )(back_part)
    back = to_channels(back) * scale_i
    grad_spec = gather(mode_product(adjoint_kernel, back, "adjoint") * scale_f, 3)
    grad_b = pl.pallas_call(
        lambda *refs: last_kernel(px, py, *refs),
        grid=(steps,),
        in_specs=[
            whole(part_shape.shape), block, block, u_block,
            whole(xh.shape), whole(xl.shape), whole((side, side)),
        ],
        out_specs=block,
        out_shape=field_shape,
        scratch_shapes=g_scratch + [pltpu.VMEM((chans, rows, nx), F32)],
        compiler_params=params,
        interpret=INTERPRET,
        name="last",
    )(grad_spec, slope, cot_b, uh, xh, xl, kron_b)

    share = chans // samples
    spec_all = lax.all_gather(spectrum, "dp", axis=0)
    back_all = lax.all_gather(back, "dp", axis=0)
    back_own = lax.dynamic_slice_in_dim(back_all, lax.axis_index("dp") * share, share, axis=2)
    p_real, p_imag = spec_all[:, 0, :, None], spec_all[:, 1, :, None]
    q_real, q_imag = back_own[:, 0, None], back_own[:, 1, None]
    grad_real = jnp.sum(p_real * q_real + p_imag * q_imag, axis=0)
    grad_imag = jnp.sum(p_real * q_imag - p_imag * q_real, axis=0)
    grad = jnp.stack([grad_real, grad_imag]) * grad_scale
    spectral_grad = grad.reshape(2, chans, share, tall // MZ, MZ, kk).transpose(3, 4, 5, 0, 1, 2)

    point = jnp.sum(point.reshape(chans, SUB, chans, SUB) * jnp.eye(SUB, dtype=F32)[None, :, None, :], axis=(1, 3))
    point_total = lax.psum(point, ("dp", "px", "py")) * point_scale
    full = state_b.shape
    return (input_a.reshape(full), grad_b.reshape(full), spectral_grad, point_total)


MESH = pl.DeviceIdType.MESH
CHUNK = 1024
TALL = 512
FINE = 512
WEIGHT_SLOTS = 2
FUSED_LIMIT = 44900 * 1024
FINISH_LIMIT = 8 * 1024 * 1024


def fused_fits(shape, local_samples, samples, px, py):
    _, chans, ys, zs, nx = shape
    kk = MX // px
    tall = MY * MZ // py
    return (
        local_samples == 1
        and 2 * kk * GROUP == 128
        and nx == 128
        and MZ == 8
        and tall // MZ == 128 // kk
        and samples * GROUP == chans
        and (ys * zs) % CHUNK == 0
    )


def base_tables(shape):
    ys, zs, ny, nz = shape
    fy = np.where(np.arange(MY) < MY // 2, np.arange(MY), ny - MY + np.arange(MY))
    fz = np.where(np.arange(MZ) < MZ // 2, np.arange(MZ), nz - MZ + np.arange(MZ))
    ay = 2.0 * np.pi / ny * (fy[:, None] * np.arange(ys) % ny)
    az = 2.0 * np.pi / nz * (fz[:, None] * np.arange(zs) % nz)
    both = ay[:, None, :, None] + az[None, :, None, :]
    table = np.stack([np.cos(both), -np.sin(both)]).reshape(2 * MY * MZ, ys * zs).astype(BF16)
    py = 2.0 * np.pi / ny * (fy[None] * (np.arange(ny // ys) * ys)[:, None] % ny)
    pz = 2.0 * np.pi / nz * (fz[None] * (np.arange(nz // zs) * zs)[:, None] % nz)
    turn = py[:, None, :, None] + pz[None, :, None, :]
    turn = np.stack([np.cos(turn), np.sin(turn)], axis=2).reshape(-1, 2, MY * MZ, 1)
    turn = np.broadcast_to(turn, turn.shape[:3] + (128,)).astype(np.float32)
    return table, np.ascontiguousarray(table.T), np.ascontiguousarray(turn)


def wide_tables(px, nx):
    high, low = x_tables(px, nx)
    inverse = [np.concatenate([t[0], t[1]], axis=1) for t in (high, low)]
    forward = [np.ascontiguousarray(t.T) for t in inverse]
    return forward, inverse


def swap_bits(tiles, first):
    lane = lax.broadcasted_iota(jnp.int32, tiles[0].shape, 1)
    tiles = list(tiles)
    for i in range(len(tiles).bit_length() - 1):
        shift = 1 << (first + i)
        upper = lane // shift % 2 == 1
        for t in range(len(tiles)):
            if not t >> i & 1:
                u = t | 1 << i
                low, high = tiles[t], tiles[u]
                tiles[t] = jnp.where(upper, pltpu.roll(high, shift, 1), low)
                tiles[u] = jnp.where(upper, high, pltpu.roll(low, 128 - shift, 1))
    return tiles


def flip(tiles):
    return swap_bits(tiles, 7 - (len(tiles).bit_length() - 1))


def rows_of(ref, start):
    chans, _, nx = ref.shape
    parts = [ref[:, pl.ds(start + u * SUB, SUB), :].reshape(chans * SUB, nx) for u in range(TALL // SUB)]
    return jnp.concatenate(parts, axis=1)


def gelu_pair(v, first, cotan):
    c0 = math.sqrt(2.0 / math.pi)
    v2 = v * v
    half = 0.5 + 0.5 * jnp.tanh(v * (c0 + (c0 * 0.044715) * v2))
    rebuilt = (first.astype(F32) - v * half).astype(BF16)
    inner = v * (2.0 * c0 + (6.0 * c0 * 0.044715) * v2)
    slope = (cotan.astype(F32) * (half + (half * (1.0 - half)) * inner)).astype(BF16)
    return rebuilt, slope


def fused_kernel(
    scales, sb_hbm, sa_hbm, ca_hbm, cb_hbm, th_hbm, uh_hbm, fh_hbm, fl_hbm, xh_hbm, xl_hbm, w_hbm, turn_hbm, pw_ref,
    fa, sb, sg_ref, pt_ref, fc, mix, th, uh, fh, fl, xh, xl, kron, w_raw, w, turn, part, land_x, land_y, gath, spec, spec_land, mode, back,
    back_land, grad, gf, acc, point, sg, pt_src, pt_land,
    in_sem, w_sem, sb_sem, sa_sem, ca_sem, cb_sem, rx_s, rx_r, ry_s, ry_r, gy_s, gy_r, gx_s, gx_r,
    dp_s, dp_r, pt_s, pt_r,
):
    scale_f, scale_i, grad_scale = scales
    groups = part.shape[1]
    py = part.shape[2]
    tall = part.shape[3]
    cells, nx = sb.shape[1:]
    samples = spec_land.shape[0] + 1
    modes = MY * MZ
    ix, iy, idp = lax.axis_index("px"), lax.axis_index("py"), lax.axis_index("dp")
    other_x = 1 - ix

    def near_y(offset):
        return lax.rem(iy + offset, py)

    def near_dp(offset):
        return lax.rem(idp + offset, samples)

    def chan(g):
        return pl.ds(g * GROUP, GROUP)

    def load(index, src, dst):
        return pltpu.make_async_copy(src, dst, in_sem.at[index])

    tables = [
        load(0, th_hbm, th), load(1, fh_hbm, fh), load(2, fl_hbm, fl),
        load(3, turn_hbm.at[ix * py + iy], turn), load(4, xh_hbm, xh), load(5, xl_hbm, xl), load(6, uh_hbm, uh),
    ]

    def load_weight(l):
        slot = lax.rem(l, WEIGHT_SLOTS)
        return pltpu.make_async_copy(w_hbm.at[:, l], w_raw.at[slot], w_sem.at[slot])

    def field_load(src, dst, sem, g):
        return pltpu.make_async_copy(src.at[chan(g)], dst.at[chan(g)], sem.at[g])

    barrier = pltpu.get_barrier_semaphore()
    pl.semaphore_signal(barrier, inc=1, device_id={"px": other_x}, device_id_type=MESH)
    for offset in range(1, py):
        pl.semaphore_signal(barrier, inc=1, device_id={"py": near_y(offset)}, device_id_type=MESH)
    for offset in range(1, samples):
        pl.semaphore_signal(barrier, inc=1, device_id={"dp": near_dp(offset)}, device_id_type=MESH)

    field_load(sb_hbm, sb, sb_sem, 0).start()
    for i in range(4):
        tables[i].start()
    for g in range(1, groups):
        field_load(sb_hbm, sb, sb_sem, g).start()
    for l in range(WEIGHT_SLOTS - 1):
        load_weight(l).start()
    for i in range(4, len(tables)):
        tables[i].start()
    for g in range(groups):
        field_load(sa_hbm, fa, sa_sem, g).start()
        field_load(ca_hbm, fc, ca_sem, g).start()
    pl.semaphore_wait(barrier, 1 + (py - 1) + (samples - 1))

    def remote(src, dst, send, recv, device):
        return pltpu.make_async_remote_copy(src, dst, send, recv, device_id=device, device_id_type=MESH)

    def reduce_x(f, g):
        return remote(
            part.at[other_x, g], land_x.at[g], rx_s.at[f, g], rx_r.at[f, g], {"px": other_x}
        )

    def reduce_y(f, g, offset):
        to = near_y(offset)
        return remote(
            part.at[ix, g, to], land_y.at[offset - 1, g], ry_s.at[f, offset - 1, g], ry_r.at[f, offset - 1, g],
            {"py": to},
        )

    def gather_y(f, g, offset):
        block = gath.at[ix, iy, g]
        return remote(block, block, gy_s.at[f, offset - 1, g], gy_r.at[f, offset - 1, g], {"py": near_y(offset)})

    def gather_x(f, g, offset):
        block = gath.at[ix, lax.rem(iy + py - offset, py), g]
        return remote(block, block, gx_s.at[f, offset, g], gx_r.at[f, offset, g], {"px": other_x})

    def after_x(f, g):
        reduce_x(f, g).wait_recv()
        part[ix, g] += land_x[g]
        for offset in range(1, py):
            reduce_y(f, g, offset).start()

    def finish_reduce(f, g):
        for offset in range(1, py):
            reduce_y(f, g, offset).wait_recv()
        value = part[ix, g, iy]
        for offset in range(1, py):
            value = value + land_y[offset - 1, g]
        return flip([value[8 * i : 8 * i + 8] for i in range(tall // 8)])

    def end_reduce_sends(f):
        for g in range(groups):
            reduce_x(f, g).wait_send()
            for offset in range(1, py):
                reduce_y(f, g, offset).wait_send()

    def start_gather(f, g, tiles):
        for i, tile in enumerate(flip(tiles)):
            gath[ix, iy, g, 8 * i : 8 * i + 8] = tile
        for offset in range(1, py):
            gather_y(f, g, offset).start()
        gather_x(f, g, 0).start()

    def forward_gather(f, g):
        for offset in range(1, py):
            gather_y(f, g, offset).wait_recv()
            gather_x(f, g, offset).start()

    def finish_gather(f, g):
        for offset in range(py):
            gather_x(f, g, offset).wait_recv()

    def end_gather_sends(f):
        for g in range(groups):
            for offset in range(1, py):
                gather_y(f, g, offset).wait_send()
            for offset in range(py):
                gather_x(f, g, offset).wait_send()

    def turns():
        cosine = jnp.concatenate([turn[0]] * GROUP, axis=1)
        sine = jnp.concatenate([turn[1]] * GROUP, axis=1)
        return cosine, sine

    def analyse(src, first, slot):
        value = jnp.concatenate([src[first], src[first + 1]], axis=1)
        acc[slot] = dot(th[...], value)

    def to_part(g):
        cosine, sine = turns()
        b0 = jnp.concatenate([acc[0, :modes], acc[1, :modes]], axis=1)
        b1 = jnp.concatenate([acc[0, modes:], acc[1, modes:]], axis=1)
        both = jnp.concatenate([b0 * cosine + b1 * sine, b1 * cosine - b0 * sine], axis=1)
        value = dot3(both, fh[...], fl[...])
        for i in range(2):
            part[i, g] = value[:, i * 128 : (i + 1) * 128].reshape(py, tall, 128)

    def build(g):
        value = jnp.concatenate([gath[i, :, g].reshape(modes, 128) for i in range(2)], axis=1)
        high, low = cut(value)
        cosine, sine = turns()
        wide = GROUP * nx
        both = dot(high, xh[...]) + dot(low, xh[...]) + dot(high, xl[...])
        g0, g1 = both[:, :wide], both[:, wide:]
        for t, field in enumerate((g0 * cosine - g1 * sine, g1 * cosine + g0 * sine)):
            field = field.astype(BF16)
            for h in range(2):
                gf[h, t * modes : (t + 1) * modes] = field[:, h * 2 * nx : (h + 1) * 2 * nx]

    def mix_rows(table, src, lo, hi):
        def step(q, carry):
            start = pl.multiple_of(q * TALL, TALL)
            value = dot(table[...], rows_of(src, start))
            for u in range(TALL // SUB):
                mix[:, pl.ds(start + u * SUB, SUB), :] = value[:, u * nx : (u + 1) * nx].reshape(-1, SUB, nx)
            return carry

        lax.fori_loop(lo, hi, step, 0)

    steps = cells // TALL
    side = point.shape[0]
    row = lax.broadcasted_iota(jnp.int32, (side, side), 0)
    column = lax.broadcasted_iota(jnp.int32, (side, side), 1)
    same = row % SUB == column % SUB

    for i in range(4):
        tables[i].wait()

    def forward(g, carry):
        field_load(sb_hbm, sb, sb_sem, g).wait()
        for p in range(2):
            analyse(sb, g * GROUP + 2 * p, p)
        to_part(g)
        reduce_x(0, g).start()

        @pl.when(g >= 1)
        def _():
            after_x(0, g - 1)

        return carry

    lax.fori_loop(0, groups, forward, 0)

    def turn_weight(l, carry):
        ahead = l + WEIGHT_SLOTS - 1

        @pl.when(ahead < MZ)
        def _():
            load_weight(ahead).start()

        load_weight(l).wait()
        slot = lax.rem(l, WEIGHT_SLOTS)
        chans = spec.shape[1]
        inner = 2 * chans
        kk = w_raw.shape[2] // inner
        tiles = []
        for t in range(inner):
            low, k = t // kk, t % kk
            some = range(low, w_raw.shape[1], inner // kk)
            rows = [w_raw[slot, j, k * inner : (k + 1) * inner, :] for j in some]
            tiles.append(jnp.concatenate(rows, axis=0).astype(F32).T)
        for r, tile in enumerate(swap_bits(tiles, 0)):
            w[r // chans, r % chans, l] = tile.astype(BF16)
        return carry

    lax.fori_loop(0, MZ // 2, turn_weight, 0)
    after_x(0, groups - 1)
    lax.fori_loop(MZ // 2, MZ, turn_weight, 0)
    spread = (row // SUB == column)[:, :SUB].astype(BF16)
    gathered = (lax.broadcasted_iota(jnp.int32, (SUB, side), 1) // SUB
                == lax.broadcasted_iota(jnp.int32, (SUB, side), 0)).astype(BF16)
    turned = lax.dot_general(spread, pw_ref[...], (((1,), (1,)), ((), ())), preferred_element_type=F32)
    kron[...] = jnp.where(same, dot(turned.astype(BF16), gathered), 0.0).astype(BF16)

    def take_spectrum(g, carry):
        tiles = finish_reduce(0, g)
        for q, tile in enumerate(tiles):
            spec[q % 2, g * GROUP + q // 2] = tile * scale_f
        return carry

    lax.fori_loop(0, groups, take_spectrum, 0)

    def blend(l, carry):
        real = jnp.zeros(w.shape[3:], F32)
        imag = jnp.zeros(w.shape[3:], F32)
        for c in range(spec.shape[1]):
            w_real, w_imag = w[0, c, l].astype(F32), w[1, c, l].astype(F32)
            s_real, s_imag = spec[0, c, pl.ds(l, 1), :], spec[1, c, pl.ds(l, 1), :]
            real += s_real * w_real - s_imag * w_imag
            imag += s_real * w_imag + s_imag * w_real
        mode[0, pl.ds(l, real.shape[0], stride=MZ), :] = real * scale_i
        mode[1, pl.ds(l, real.shape[0], stride=MZ), :] = imag * scale_i
        return carry

    lax.fori_loop(0, MZ, blend, 0)
    for g in range(groups):
        start_gather(0, g, [mode[q % 2, (g * GROUP + q // 2) * MZ :][:MZ] for q in range(2 * GROUP)])

    def send_spec(offset):
        return remote(
            spec, spec_land.at[offset - 1], dp_s.at[0, offset - 1], dp_r.at[0, offset - 1], {"dp": near_dp(offset)}
        )

    def send_back(offset):
        to = near_dp(offset)
        return remote(
            back.at[to], back_land.at[offset - 1], dp_s.at[1, offset - 1], dp_r.at[1, offset - 1], {"dp": to}
        )

    for offset in range(1, samples):
        send_spec(offset).start()
    end_reduce_sends(0)
    for i in range(4, len(tables)):
        tables[i].wait()
    mix_rows(kron, sb, 0, steps)
    forward_gather(0, 0)

    def middle(g, carry):
        @pl.when(g + 1 < groups)
        def _():
            forward_gather(0, g + 1)

        finish_gather(0, g)
        build(g)
        field_load(sa_hbm, fa, sa_sem, g).wait()
        field_load(ca_hbm, fc, ca_sem, g).wait()

        def pair(p, inner):
            first = g * GROUP + 2 * p

            total = None
            for start in range(0, cells, FINE):
                some = slice(start, start + FINE)
                field = dot(uh[some], gf[p])
                slopes = []
                for h in range(2):
                    v = field[:, h * nx : (h + 1) * nx] + mix[first + h, some]
                    rebuilt, slope = gelu_pair(v, fa[first + h, some], fc[first + h, some])
                    fa[first + h, some] = rebuilt
                    fc[first + h, some] = slope
                    slopes.append(slope)
                piece = dot(th[:, some], jnp.concatenate(slopes, axis=1))
                total = piece if total is None else total + piece
            acc[p] = total
            return inner

        lax.fori_loop(0, 2, pair, 0)
        to_part(g)
        reduce_x(1, g).start()

        @pl.when(g >= 1)
        def _():
            after_x(1, g - 1)

        return carry

    lax.fori_loop(0, groups, middle, 0)
    end_gather_sends(0)

    point[...] = jnp.zeros_like(point)

    def point_rows(lo, hi):
        def step(q, carry):
            start = pl.multiple_of(q * TALL, TALL)
            left, right = rows_of(sb, start), rows_of(fc, start)
            point[...] += lax.dot_general(left, right, (((1,), (1,)), ((), ())), preferred_element_type=F32)
            return carry

        lax.fori_loop(lo, hi, step, 0)

    point_rows(0, steps)
    after_x(1, groups - 1)
    for g in range(groups):
        field_load(cb_hbm, sb, cb_sem, g).start()
    kron[...] = jnp.where(same, dot(dot(spread, pw_ref[...]).astype(BF16), gathered), 0.0).astype(BF16)
    mix_rows(kron, fc, 0, steps)
    diagonal = jnp.where(same, point[...], 0.0)
    pt_src[0] = jnp.sum(diagonal.reshape(-1, SUB, point.shape[1]), axis=1)

    def sum_x():
        return remote(pt_src.at[0], pt_land.at[0, 0], pt_s.at[0], pt_r.at[0], {"px": other_x})

    def sum_y(offset):
        return remote(
            pt_src.at[1], pt_land.at[1, iy], pt_s.at[offset], pt_r.at[offset], {"py": near_y(offset)}
        )

    def sum_dp(offset):
        return remote(
            pt_src.at[2], pt_land.at[2, idp], pt_s.at[py - 1 + offset], pt_r.at[py - 1 + offset],
            {"dp": near_dp(offset)},
        )

    sum_x().start()

    def take_back(g, carry):
        tiles = finish_reduce(1, g)
        for q, tile in enumerate(tiles):
            back[g, q % 2, q // 2] = tile * scale_i
            mode[q % 2, pl.ds(pl.multiple_of((g * GROUP + q // 2) * MZ, MZ), MZ), :] = tile * scale_i
        return carry

    lax.fori_loop(0, groups, take_back, 0)

    def adjoint(g, carry):
        for l in range(MZ):
            b_real, b_imag = (mode[i, pl.ds(l, w.shape[3], stride=MZ), :] for i in range(2))
            for c in range(GROUP):
                w_real, w_imag = w[0, g * GROUP + c, l].astype(F32), w[1, g * GROUP + c, l].astype(F32)
                real = jnp.sum(b_real * w_real + b_imag * w_imag, axis=0, keepdims=True)
                imag = jnp.sum(b_imag * w_real - b_real * w_imag, axis=0, keepdims=True)
                grad[2 * c, l : l + 1] = real * scale_f
                grad[2 * c + 1, l : l + 1] = imag * scale_f
        start_gather(1, g, [grad[q] for q in range(2 * GROUP)])
        return carry

    lax.fori_loop(0, groups, adjoint, 0)
    for offset in range(1, samples):
        send_back(offset).start()
    sum_x().wait()
    pt_src[1] = pt_src[0] + pt_land[0, 0]
    pt_land[1, iy] = pt_src[1]
    for offset in range(1, py):
        sum_y(offset).start()
    forward_gather(1, 0)

    for offset in range(1, samples):
        send_spec(offset).wait()
        send_back(offset).wait()

    def outer(c, carry):
        for d in range(GROUP):
            real = jnp.zeros((8, 128), F32)
            imag = jnp.zeros((8, 128), F32)
            for s in range(samples):
                if s == 0:
                    p_real, p_imag = spec[0, c], spec[1, c]
                    q_real, q_imag = back[idp, 0, d], back[idp, 1, d]
                else:
                    p_real, p_imag = spec_land[s - 1, 0, c], spec_land[s - 1, 1, c]
                    q_real, q_imag = back_land[s - 1, 0, d], back_land[s - 1, 1, d]
                real += p_real * q_real + p_imag * q_imag
                imag += p_real * q_imag - p_imag * q_real
            sg[0, d, pl.ds(pl.multiple_of(c * MZ, MZ), MZ), :] = real * grad_scale
            sg[1, d, pl.ds(pl.multiple_of(c * MZ, MZ), MZ), :] = imag * grad_scale
        return carry

    lax.fori_loop(0, spec.shape[1], outer, 0)

    def spread_modes(l):
        for r in range(2 * GROUP):
            value = sg[r // GROUP, r % GROUP, pl.ds(l, spec.shape[1], stride=MZ), :].T
            kk = sg_ref.shape[2] // (2 * GROUP)
            for j in range(sg_ref.shape[0]):
                sg_ref[j, l, pl.ds(r, kk, stride=2 * GROUP), :] = value[j * kk : (j + 1) * kk]

    def spread_some(l, carry):
        spread_modes(l)
        return carry

    lax.fori_loop(0, MZ - groups, spread_some, 0)
    for offset in range(1, py):
        sum_y(offset).wait()
    pt_src[2] = sum(pt_land[1, i] for i in range(py))
    pt_land[2, idp] = pt_src[2]
    for offset in range(1, samples):
        sum_dp(offset).start()

    def last(g, carry):
        @pl.when(g + 1 < groups)
        def _():
            forward_gather(1, g + 1)

        spread_modes(MZ - groups + g)
        finish_gather(1, g)
        build(g)
        field_load(cb_hbm, sb, cb_sem, g).wait()

        def pair(p, inner):
            first = g * GROUP + 2 * p

            def rows(r, deep):
                some = pl.ds(pl.multiple_of(r * CHUNK, CHUNK), CHUNK)
                field = dot(uh[some, :], gf[p])
                for h in range(2):
                    value = sb[first + h, some, :].astype(F32) + field[:, h * nx : (h + 1) * nx]
                    sb[first + h, some, :] = (value + mix[first + h, some, :]).astype(BF16)
                return deep

            lax.fori_loop(0, cells // CHUNK, rows, 0)
            return inner

        lax.fori_loop(0, 2, pair, 0)
        return carry

    lax.fori_loop(0, groups, last, 0)

    for offset in range(1, samples):
        sum_dp(offset).wait()
    pt_ref[...] = sum(pt_land[2, i] for i in range(samples))
    end_reduce_sends(1)
    end_gather_sends(1)


def finish_kernel(point_scale, ia_ref, gb_ref, sg_ref, pt_ref, ia_hbm, gb_hbm, sg_hbm, point_ref, sems):
    copies = []
    for which, (src, dst) in enumerate(((ia_ref, ia_hbm), (gb_ref, gb_hbm), (sg_ref, sg_hbm))):
        parts = sems.shape[1]
        each = src.shape[0] // parts
        for i in range(parts):
            some = pl.ds(i * each, each)
            copies.append(pltpu.make_async_copy(src.at[some], dst.at[some], sems.at[which, i]))
    for copy in copies:
        copy.start()
    value = pt_ref[...]
    chans = point_ref.shape[0]
    row = lax.broadcasted_iota(jnp.int32, (value.shape[1], chans), 0)
    column = lax.broadcasted_iota(jnp.int32, (value.shape[1], chans), 1)
    ones = (row // SUB == column).astype(BF16)
    total = jnp.zeros(point_ref.shape, F32)
    for _ in range(3):
        part = value.astype(BF16)
        total += dot(part, ones)
        value -= part.astype(F32)
    point_ref[...] = total * point_scale
    for copy in copies:
        copy.wait()


def fused_device(state_a, state_b, cotan_a, cotan_b, spectral_weight, point_weight):
    samples, px, py = (lax.axis_size(name) for name in ("dp", "px", "py"))
    _, chans, ys, zs, nx = state_b.shape
    ny, nz = ys * px, zs * py
    cells, modes = ys * zs, MY * MZ
    groups = chans // GROUP
    kk = MX // px
    tall = modes // py
    total = nx * ny * nz
    scales = (
        1.0 / math.sqrt(total), 1.0 / math.sqrt(MX * MY * MZ), math.sqrt(MX * MY * MZ / (samples * total)),
    )
    th, uh, turn = (jnp.asarray(t) for t in base_tables((ys, zs, ny, nz)))
    (fh, fl), (xh, xl) = wide_tables(px, nx)
    fh, fl, xh, xl = (jnp.asarray(t) for t in (fh, fl, xh, xl))
    side = chans * SUB
    jj, ll = tall // MZ, MZ
    weight = spectral_weight.reshape(jj, ll, kk * 2 * chans, chans)
    spread = (jj, ll, kk * 2 * GROUP, chans)
    fields = [value.reshape(chans, cells, nx) for value in (state_b, state_a, cotan_a, cotan_b)]
    field = jax.ShapeDtypeStruct((chans, cells, nx), BF16)
    any_spec = pl.BlockSpec(memory_space=pl.ANY)
    vmem_spec = pl.BlockSpec(memory_space=pltpu.VMEM)
    dma = pltpu.SemaphoreType.DMA
    near = py - 1
    input_a, grad_b, sg, point = pl.pallas_call(
        lambda *refs: fused_kernel(scales, *refs),
        in_specs=[any_spec] * 12 + [vmem_spec],
        out_specs=[vmem_spec] * 4,
        out_shape=[
            pltpu.VMEM(field.shape, BF16), pltpu.VMEM(field.shape, BF16),
            pltpu.VMEM(spread, F32), pltpu.VMEM((chans, side), F32),
        ],
        scratch_shapes=[
            pltpu.VMEM((chans, cells, nx), BF16), pltpu.VMEM((chans, cells, nx), F32),
            pltpu.VMEM(th.shape, BF16), pltpu.VMEM(uh.shape, BF16), pltpu.VMEM(fh.shape, BF16),
            pltpu.VMEM(fl.shape, BF16), pltpu.VMEM(xh.shape, BF16), pltpu.VMEM(xl.shape, BF16),
            pltpu.VMEM((side, side), BF16),
            pltpu.VMEM((WEIGHT_SLOTS, jj) + weight.shape[2:], BF16), pltpu.VMEM((2, chans, MZ, chans, 128), BF16),
            pltpu.VMEM(turn.shape[1:], F32),
            pltpu.VMEM((px, groups, py, tall, 128), F32),
            pltpu.VMEM((groups, py, tall, 128), F32),
            pltpu.VMEM((near, groups, tall, 128), F32),
            pltpu.VMEM((px, py, groups, tall, 128), F32),
            pltpu.VMEM((2, chans, MZ, 128), F32),
            pltpu.VMEM((samples - 1, 2, chans, MZ, 128), F32),
            pltpu.VMEM((2, chans * MZ, 128), F32),
            pltpu.VMEM((samples, 2, GROUP, MZ, 128), F32),
            pltpu.VMEM((samples - 1, 2, GROUP, MZ, 128), F32),
            pltpu.VMEM((2 * GROUP, MZ, 128), F32),
            pltpu.VMEM((2, 2 * modes, 2 * nx), BF16),
            pltpu.VMEM((2, 2 * modes, 2 * nx), F32),
            pltpu.VMEM((side, side), F32),
            pltpu.VMEM((2, GROUP, chans * MZ, 128), F32),
            pltpu.VMEM((3, chans, side), F32),
            pltpu.VMEM((3, max(py, samples), chans, side), F32),
            dma((7,)), dma((WEIGHT_SLOTS,)), dma((groups,)), dma((groups,)), dma((groups,)), dma((groups,)),
            dma((2, groups)), dma((2, groups)), dma((2, near, groups)), dma((2, near, groups)),
            dma((2, near, groups)), dma((2, near, groups)), dma((2, py, groups)), dma((2, py, groups)),
            dma((2, samples - 1)), dma((2, samples - 1)), dma((1 + near + samples - 1,)), dma((1 + near + samples - 1,)),
        ],
        compiler_params=pltpu.CompilerParams(
            vmem_limit_bytes=FUSED_LIMIT, collective_id=4, has_side_effects=True
        ),
        interpret=INTERPRET,
        name="fused",
    )(*fields, th, uh, fh, fl, xh, xl, weight, turn, point_weight)
    point_scale = 1.0 / math.sqrt(samples * total)
    input_a, grad_b, spectral_grad, point_total = pl.pallas_call(
        lambda *refs: finish_kernel(point_scale, *refs),
        in_specs=[vmem_spec] * 4,
        out_specs=[any_spec] * 3 + [vmem_spec],
        out_shape=[
            field, field, jax.ShapeDtypeStruct(spread, F32), jax.ShapeDtypeStruct((chans, chans), F32),
        ],
        scratch_shapes=[dma((3, groups))],
        compiler_params=pltpu.CompilerParams(vmem_limit_bytes=FINISH_LIMIT),
        interpret=INTERPRET,
        name="finish",
    )(input_a, grad_b, sg, point)
    spectral_grad = spectral_grad.reshape(jj, ll, kk, 2, GROUP, chans).transpose(0, 1, 2, 3, 5, 4)
    full = state_b.shape
    return (input_a.reshape(full), grad_b.reshape(full), spectral_grad, point_total)


def solution(mesh):
    sizes = dict(mesh.shape)

    def body(*values):
        fits = fused_fits(values[1].shape, values[1].shape[0], sizes["dp"], sizes["px"], sizes["py"])
        return (fused_device if fits else general_device)(*values)

    return jax.shard_map(
        body,
        mesh=mesh,
        in_specs=(
            P("dp", None, "px", "py", None),
            P("dp", None, "px", "py", None),
            P("dp", None, "px", "py", None),
            P("dp", None, "px", "py", None),
            P("py", None, "px", None, None, None),
            P(),
        ),
        out_specs=(
            P("dp", None, "px", "py", None),
            P("dp", None, "px", "py", None),
            P("py", None, "px", None, None, "dp"),
            P(),
        ),
        check_vma=False,
    )
```

```python
import math

import jax
import jax.numpy as jnp
import numpy as np
from jax import lax
from jax.experimental import pallas as pl
from jax.experimental.pallas import tpu as pltpu
from jax.sharding import PartitionSpec as P

MX = 32
MY = 32
MZ = 8
GROUP = 4
SUB = 16
LIMIT = 56 * 1024 * 1024
INTERPRET = False
F32 = jnp.float32
BF16 = jnp.bfloat16


def kept(length_all, length_kept, position):
    return jnp.where(position < length_kept // 2, position, length_all - length_kept + position)


def angle(product, length_all):
    return (product % length_all).astype(F32) * (2.0 * math.pi / length_all)


def synthesis_table(shape):
    ys, zs, ny, nz = shape
    mode = lax.broadcasted_iota(jnp.int32, (1, MY * MZ), 1)
    fy = kept(ny, MY, mode // MZ)
    fz = kept(nz, MZ, mode % MZ)
    y = lax.axis_index("px") * ys + lax.broadcasted_iota(jnp.int32, (ys, 1), 0)
    z = lax.axis_index("py") * zs + lax.broadcasted_iota(jnp.int32, (zs, 1), 0)
    ay = angle(fy * y, ny)
    az = angle(fz * z, nz)
    cy, sy = jnp.cos(ay)[:, None, :], jnp.sin(ay)[:, None, :]
    cz, sz = jnp.cos(az)[None], jnp.sin(az)[None]
    table = jnp.concatenate([cy * cz - sy * sz, -(sy * cz + cy * sz)], axis=2)
    return table.reshape(ys * zs, 2 * MY * MZ)


def analysis_table(shape):
    ys, zs, ny, nz = shape
    cell = lax.broadcasted_iota(jnp.int32, (1, ys * zs), 1)
    y = lax.axis_index("px") * ys + cell // zs
    z = lax.axis_index("py") * zs + cell % zs
    fy = kept(ny, MY, lax.broadcasted_iota(jnp.int32, (MY, 1), 0))
    fz = kept(nz, MZ, lax.broadcasted_iota(jnp.int32, (MZ, 1), 0))
    ay = angle(fy * y, ny)
    az = angle(fz * z, nz)
    cy, sy = jnp.cos(ay)[:, None, :], jnp.sin(ay)[:, None, :]
    cz, sz = jnp.cos(az)[None], jnp.sin(az)[None]
    table = jnp.stack([cy * cz - sy * sz, -(sy * cz + cy * sz)])
    return table.reshape(2 * MY * MZ, ys * zs)


def x_tables(px, nx):
    kk = MX // px
    k = np.arange(MX).reshape(px, kk)
    phase = 2.0 * np.pi / nx * (k[:, :, None] * np.arange(nx) % nx)
    cosine, sine = np.cos(phase), np.sin(phase)
    table = np.zeros((2, px, GROUP, 2, kk, GROUP, nx))
    for c in range(GROUP):
        table[0, :, c, 0, :, c] = cosine
        table[0, :, c, 1, :, c] = -sine
        table[1, :, c, 0, :, c] = sine
        table[1, :, c, 1, :, c] = cosine
    table = table.reshape(2, 2 * MX * GROUP, GROUP * nx)
    high = table.astype(BF16)
    low = (table - high.astype(np.float64)).astype(BF16)
    return high, low


def dot(a, b):
    return jnp.dot(a, b, preferred_element_type=F32)


def cut(value):
    high = value.astype(BF16)
    return high, (value - high.astype(F32)).astype(BF16)


def dot3(a, high, low):
    ahigh, alow = cut(a)
    return dot(ahigh, high) + dot(alow, high) + dot(ahigh, low)


def to_modes(b0, b1, xh_ref, xl_ref):
    return dot3(b0, xh_ref[0], xl_ref[0]) + dot3(b1, xh_ref[1], xl_ref[1])


def store_modes(out_ref, group, value, px, py):
    wide = value.shape[1] // px
    tall = value.shape[0] // py
    for i in range(px):
        for j in range(py):
            out_ref[i * py + j, group] = value[j * tall : (j + 1) * tall, i * wide : (i + 1) * wide]


def build_fields(spec_ref, xh_ref, xl_ref, gh_ref, px, py):
    modes = MY * MZ
    for g in range(spec_ref.shape[1]):
        rows = []
        for j in range(py):
            rows.append(jnp.concatenate([spec_ref[i * py + j, g] for i in range(px)], axis=1))
        value = jnp.concatenate(rows, axis=0)
        for t in range(2):
            high = dot3(value, xh_ref[t], xl_ref[t]).astype(BF16)
            half = high.shape[1] // 2
            for h in range(2):
                gh_ref[2 * g + h, t * modes : (t + 1) * modes] = high[:, h * half : (h + 1) * half]


def pair_of(ref, start):
    chans, _, nx = ref.shape
    first = ref[:, pl.ds(start, SUB), :].reshape(chans * SUB, nx)
    second = ref[:, pl.ds(start + SUB, SUB), :].reshape(chans * SUB, nx)
    return jnp.concatenate([first, second], axis=1)


def channel_mix(kron_ref, in_ref, out_ref):
    chans, rows, nx = in_ref.shape

    def body(q, carry):
        start = pl.multiple_of(q * 2 * SUB, 2 * SUB)
        value = dot(kron_ref[...], pair_of(in_ref, start))
        out_ref[:, pl.ds(start, SUB), :] = value[:, :nx].reshape(chans, SUB, nx)
        out_ref[:, pl.ds(start + SUB, SUB), :] = value[:, nx:].reshape(chans, SUB, nx)
        return carry

    lax.fori_loop(0, rows // (2 * SUB), body, 0)


def position(py):
    return lax.axis_index("px") * py + lax.axis_index("py")


def partner(px, py, offset):
    other = lax.rem(position(py) + offset, px * py)
    return other, {"px": lax.div(other, py), "py": lax.rem(other, py)}


def greet(px, py):
    barrier = pltpu.get_barrier_semaphore()
    for offset in range(1, px * py):
        pl.semaphore_signal(
            barrier, inc=1, device_id=partner(px, py, offset)[1], device_id_type=pl.DeviceIdType.MESH
        )
    pl.semaphore_wait(barrier, px * py - 1)


def scatter_copy(px, py, offset, group, part_ref, land_ref, send_sem, recv_sem):
    other, device = partner(px, py, offset)
    return pltpu.make_async_remote_copy(
        part_ref.at[other, group], land_ref.at[offset, group], send_sem.at[offset, group], recv_sem.at[offset, group],
        device_id=device, device_id_type=pl.DeviceIdType.MESH,
    )


def scatter_kernel(px, py, part_ref, out_ref, land_ref, send_sem, recv_sem):
    count = px * py
    greet(px, py)
    groups = part_ref.shape[1]
    for g in range(groups):
        for offset in range(1, count):
            scatter_copy(px, py, offset, g, part_ref, land_ref, send_sem, recv_sem).start()
    out_ref[...] = part_ref[position(py)]
    for g in range(groups):
        for offset in range(1, count):
            scatter_copy(px, py, offset, g, part_ref, land_ref, send_sem, recv_sem).wait()
            out_ref[g] += land_ref[offset, g]


def gather_kernel(px, py, own_ref, out_ref, land_ref, send_sem, recv_sem):
    count = px * py
    greet(px, py)
    copies = []
    for offset in range(1, count):
        copies.append(
            pltpu.make_async_remote_copy(
                own_ref, land_ref.at[offset], send_sem.at[offset], recv_sem.at[offset],
                device_id=partner(px, py, offset)[1], device_id_type=pl.DeviceIdType.MESH,
            )
        )
        copies[-1].start()
    here = position(py)
    out_ref[here] = own_ref[...]
    for offset in range(1, count):
        copies[offset - 1].wait()
        out_ref[lax.rem(here + count - offset, count)] = land_ref[offset]


def mix_kernel(s_ref, w_ref, out_ref):
    chans = s_ref.shape[1]
    real = jnp.zeros(out_ref.shape[1:], F32)
    imag = jnp.zeros(out_ref.shape[1:], F32)
    for c in range(chans):
        s_real, s_imag = s_ref[0, c : c + 1], s_ref[1, c : c + 1]
        w_real, w_imag = w_ref[0, c].astype(F32), w_ref[1, c].astype(F32)
        real += s_real * w_real - s_imag * w_imag
        imag += s_real * w_imag + s_imag * w_real
    out_ref[0] = real
    out_ref[1] = imag


def adjoint_kernel(b_ref, w_ref, out_ref):
    b_real, b_imag = b_ref[0], b_ref[1]
    for c in range(w_ref.shape[1]):
        w_real, w_imag = w_ref[0, c].astype(F32), w_ref[1, c].astype(F32)
        out_ref[0, c : c + 1] = jnp.sum(b_real * w_real + b_imag * w_imag, axis=0, keepdims=True)
        out_ref[1, c : c + 1] = jnp.sum(b_imag * w_real - b_real * w_imag, axis=0, keepdims=True)


def forward_kernel(
    px, py, v_ref, th_ref, xh_ref, xl_ref, out_ref, part_ref, land_ref, send_sem, recv_sem
):
    modes = MY * MZ
    parts = []
    for p in range(GROUP // 2):
        value = jnp.concatenate([v_ref[2 * p], v_ref[2 * p + 1]], axis=1)
        parts.append(dot(th_ref[...], value))
    b0 = jnp.concatenate([part[:modes] for part in parts], axis=1)
    b1 = jnp.concatenate([part[modes:] for part in parts], axis=1)
    step = pl.program_id(0)
    store_modes(part_ref, step, to_modes(b0, b1, xh_ref, xl_ref), px, py)
    count = px * py

    @pl.when(step == 0)
    def _():
        greet(px, py)

    for offset in range(1, count):
        scatter_copy(px, py, offset, step, part_ref, land_ref, send_sem, recv_sem).start()

    @pl.when(step == pl.num_programs(0) - 1)
    def _():
        out_ref[...] = part_ref[position(py)]
        for g in range(part_ref.shape[1]):
            for offset in range(1, count):
                scatter_copy(px, py, offset, g, part_ref, land_ref, send_sem, recv_sem).wait()
                out_ref[g] += land_ref[offset, g]


def middle_kernel(
    px, py, steps, spec_ref, vb_ref, va_ref, ca_ref, uh_ref, th_ref, xh_ref, xl_ref, fh_ref, fl_ref,
    kron_ref, ia_ref, sl_ref, back_ref, point_ref, gh_ref, acc_ref, mix_ref,
):
    step = pl.program_id(0)
    modes = MY * MZ
    nx = vb_ref.shape[2]
    chans, rows = vb_ref.shape[:2]

    @pl.when(step == 0)
    def _():
        build_fields(spec_ref, xh_ref, xl_ref, gh_ref, px, py)
        acc_ref[...] = jnp.zeros_like(acc_ref)
        point_ref[...] = jnp.zeros_like(point_ref)

    channel_mix(kron_ref, vb_ref, mix_ref)
    c0 = math.sqrt(2.0 / math.pi)

    def body(p, carry):
        field = dot(uh_ref[...], gh_ref[p])
        slopes = []
        for h in range(2):
            d = 2 * p + h
            v = field[:, h * nx : (h + 1) * nx] + mix_ref[d]
            v2 = v * v
            t = jnp.tanh(v * (c0 + (c0 * 0.044715) * v2))
            half = 0.5 + 0.5 * t
            ia_ref[d] = (va_ref[d].astype(F32) - v * half).astype(BF16)
            deriv = half + (0.5 * v) * (1.0 - t * t) * (c0 + (3.0 * c0 * 0.044715) * v2)
            slope = (ca_ref[d].astype(F32) * deriv).astype(BF16)
            sl_ref[d] = slope
            slopes.append(slope)
        both = jnp.concatenate(slopes, axis=1)
        acc_ref[p] += dot(th_ref[...], both)
        return carry

    lax.fori_loop(0, chans // 2, body, 0)

    def point_body(q, carry):
        start = pl.multiple_of(q * 2 * SUB, 2 * SUB)
        point_ref[...] += lax.dot_general(
            pair_of(vb_ref, start), pair_of(sl_ref, start), (((1,), (1,)), ((), ())), preferred_element_type=F32
        )
        return carry

    lax.fori_loop(0, rows // (2 * SUB), point_body, 0)

    @pl.when(step == steps - 1)
    def _():
        for g in range(chans // GROUP):
            parts = [acc_ref[2 * g + h] for h in range(2)]
            b0 = jnp.concatenate([part[:modes] for part in parts], axis=1)
            b1 = jnp.concatenate([part[modes:] for part in parts], axis=1)
            store_modes(back_ref, g, to_modes(b0, b1, fh_ref, fl_ref), px, py)


def last_kernel(
    px, py, spec_ref, sl_ref, cb_ref, uh_ref, xh_ref, xl_ref, kron_ref, out_ref, gh_ref, mix_ref
):
    nx = sl_ref.shape[2]

    @pl.when(pl.program_id(0) == 0)
    def _():
        build_fields(spec_ref, xh_ref, xl_ref, gh_ref, px, py)

    channel_mix(kron_ref, sl_ref, mix_ref)

    def body(p, carry):
        field = dot(uh_ref[...], gh_ref[p])
        for h in range(2):
            d = 2 * p + h
            value = cb_ref[d].astype(F32) + field[:, h * nx : (h + 1) * nx] + mix_ref[d]
            out_ref[d] = value.astype(BF16)
        return carry

    lax.fori_loop(0, sl_ref.shape[0] // 2, body, 0)


def whole(shape):
    return pl.BlockSpec(shape, lambda i: (0,) * len(shape), pipeline_mode=pl.Buffered(1))


def general_device(state_a, state_b, cotan_a, cotan_b, spectral_weight, point_weight):
    samples, px, py = (lax.axis_size(name) for name in ("dp", "px", "py"))
    _, chans, ys, zs, nx = state_b.shape
    ny, nz = ys * px, zs * py
    cells, modes = ys * zs, MY * MZ
    groups = chans // GROUP
    kk = MX // px
    tall, wide = modes // py, 2 * MX * GROUP // px
    own = tall * kk
    scale_f = 1.0 / math.sqrt(nx * ny * nz)
    scale_i = 1.0 / math.sqrt(MX * MY * MZ)
    grad_scale = math.sqrt(MX * MY * MZ / (samples * nx * ny * nz))
    point_scale = 1.0 / math.sqrt(samples * nx * ny * nz)
    shape = (ys, zs, ny, nz)
    th = analysis_table(shape).astype(BF16)
    uh = synthesis_table(shape).astype(BF16)
    xh, xl = x_tables(px, nx)
    fh, fl = (jnp.asarray(np.ascontiguousarray(table.transpose(0, 2, 1))) for table in (xh, xl))
    xh, xl = jnp.asarray(xh), jnp.asarray(xl)
    eye = jnp.eye(SUB, dtype=BF16)
    kron_f = (point_weight.T[:, None, :, None] * eye[None, :, None, :]).reshape(chans * SUB, chans * SUB)
    kron_b = (point_weight[:, None, :, None] * eye[None, :, None, :]).reshape(chans * SUB, chans * SUB)
    field_a, field_b, cot_a, cot_b = (
        value.reshape(chans, cells, nx) for value in (state_a, state_b, cotan_a, cotan_b)
    )
    part_shape = jax.ShapeDtypeStruct((px * py, groups, tall, wide), F32)
    params = pltpu.CompilerParams(vmem_limit_bytes=LIMIT)

    count = px * py
    own_shape = jax.ShapeDtypeStruct((groups, tall, wide), F32)
    exchange = [
        pltpu.VMEM(part_shape.shape, F32),
        pltpu.SemaphoreType.DMA((count, groups)),
        pltpu.SemaphoreType.DMA((count, groups)),
    ]

    def linked(number):
        return pltpu.CompilerParams(vmem_limit_bytes=LIMIT, collective_id=number, has_side_effects=True)

    def to_channels(value):
        value = value.reshape(groups, tall, GROUP, 2, kk).transpose(3, 0, 2, 1, 4)
        return value.reshape(2, chans, own)

    def gather(value, number):
        value = value.reshape(2, groups, GROUP, tall, kk).transpose(1, 3, 2, 0, 4)
        value = value.reshape(groups, tall, wide)
        return pl.pallas_call(
            lambda *refs: gather_kernel(px, py, *refs),
            in_specs=[pl.BlockSpec(memory_space=pltpu.VMEM)],
            out_specs=pl.BlockSpec(memory_space=pltpu.VMEM),
            out_shape=part_shape,
            scratch_shapes=[
                pltpu.VMEM(part_shape.shape, F32), pltpu.SemaphoreType.DMA((count,)), pltpu.SemaphoreType.DMA((count,)),
            ],
            compiler_params=linked(number),
            interpret=INTERPRET,
            name="gather",
        )(value)

    def mode_product(kernel, value, name):
        return pl.pallas_call(
            kernel,
            out_shape=jax.ShapeDtypeStruct((2, chans, own), F32),
            compiler_params=params,
            interpret=INTERPRET,
            name=name,
        )(value, weight)

    spectrum = pl.pallas_call(
        lambda *refs: forward_kernel(px, py, *refs),
        grid=(groups,),
        in_specs=[
            pl.BlockSpec((GROUP, cells, nx), lambda i: (i, 0, 0)),
            whole(th.shape), whole(fh.shape), whole(fl.shape),
        ],
        out_specs=whole(own_shape.shape),
        out_shape=own_shape,
        scratch_shapes=[pltpu.VMEM(part_shape.shape, F32)] + exchange,
        compiler_params=linked(0),
        interpret=INTERPRET,
        name="forward",
    )(field_b, th, fh, fl)
    weight = spectral_weight.transpose(3, 4, 5, 0, 1, 2).reshape(2, chans, chans, own)
    spectrum = to_channels(spectrum) * scale_f
    mixed = gather(mode_product(mix_kernel, spectrum, "mix") * scale_i, 1)

    rows = min(256, cells)
    steps = cells // rows
    block = pl.BlockSpec((chans, rows, nx), lambda i: (0, i, 0))
    u_block = pl.BlockSpec((rows, 2 * modes), lambda i: (i, 0))
    t_block = pl.BlockSpec((2 * modes, rows), lambda i: (0, i))
    field_shape = jax.ShapeDtypeStruct((chans, cells, nx), BF16)
    side = chans * SUB
    g_scratch = [pltpu.VMEM((chans // 2, 2 * modes, 2 * nx), BF16)]
    input_a, slope, back_part, point = pl.pallas_call(
        lambda *refs: middle_kernel(px, py, steps, *refs),
        grid=(steps,),
        in_specs=[
            whole(part_shape.shape), block, block, block, u_block, t_block,
            whole(xh.shape), whole(xl.shape), whole(fh.shape), whole(fl.shape), whole((side, side)),
        ],
        out_specs=[block, block, whole(part_shape.shape), whole((side, side))],
        out_shape=[field_shape, field_shape, part_shape, jax.ShapeDtypeStruct((side, side), F32)],
        scratch_shapes=g_scratch
        + [pltpu.VMEM((chans // 2, 2 * modes, 2 * nx), F32), pltpu.VMEM((chans, rows, nx), F32)],
        compiler_params=params,
        interpret=INTERPRET,
        name="middle",
    )(mixed, field_b, field_a, cot_a, uh, th, xh, xl, fh, fl, kron_f)

    back = pl.pallas_call(
        lambda *refs: scatter_kernel(px, py, *refs),
        in_specs=[pl.BlockSpec(memory_space=pltpu.VMEM)],
        out_specs=pl.BlockSpec(memory_space=pltpu.VMEM),
        out_shape=own_shape,
        scratch_shapes=exchange,
        compiler_params=linked(2),
        interpret=INTERPRET,
        name="scatter",
    )(back_part)
    back = to_channels(back) * scale_i
    grad_spec = gather(mode_product(adjoint_kernel, back, "adjoint") * scale_f, 3)
    grad_b = pl.pallas_call(
        lambda *refs: last_kernel(px, py, *refs),
        grid=(steps,),
        in_specs=[
            whole(part_shape.shape), block, block, u_block,
            whole(xh.shape), whole(xl.shape), whole((side, side)),
        ],
        out_specs=block,
        out_shape=field_shape,
        scratch_shapes=g_scratch + [pltpu.VMEM((chans, rows, nx), F32)],
        compiler_params=params,
        interpret=INTERPRET,
        name="last",
    )(grad_spec, slope, cot_b, uh, xh, xl, kron_b)

    share = chans // samples
    spec_all = lax.all_gather(spectrum, "dp", axis=0)
    back_all = lax.all_gather(back, "dp", axis=0)
    back_own = lax.dynamic_slice_in_dim(back_all, lax.axis_index("dp") * share, share, axis=2)
    p_real, p_imag = spec_all[:, 0, :, None], spec_all[:, 1, :, None]
    q_real, q_imag = back_own[:, 0, None], back_own[:, 1, None]
    grad_real = jnp.sum(p_real * q_real + p_imag * q_imag, axis=0)
    grad_imag = jnp.sum(p_real * q_imag - p_imag * q_real, axis=0)
    grad = jnp.stack([grad_real, grad_imag]) * grad_scale
    spectral_grad = grad.reshape(2, chans, share, tall // MZ, MZ, kk).transpose(3, 4, 5, 0, 1, 2)

    point = jnp.sum(point.reshape(chans, SUB, chans, SUB) * jnp.eye(SUB, dtype=F32)[None, :, None, :], axis=(1, 3))
    point_total = lax.psum(point, ("dp", "px", "py")) * point_scale
    full = state_b.shape
    return (input_a.reshape(full), grad_b.reshape(full), spectral_grad, point_total)


MESH = pl.DeviceIdType.MESH
TALL = 512
FINE = 256
WEIGHT_SLOTS = 2
FUSED_LIMIT = 44900 * 1024
FINISH_LIMIT = 8 * 1024 * 1024


def fused_fits(shape, local_samples, samples, px, py):
    _, chans, ys, zs, nx = shape
    kk = MX // px
    tall = MY * MZ // py
    return (
        local_samples == 1
        and 2 * kk * GROUP == 128
        and nx == 128
        and MZ == 8
        and tall // MZ == 128 // kk
        and samples * GROUP == chans
        and (ys * zs) % TALL == 0
    )


def base_tables(shape):
    ys, zs, ny, nz = shape
    fy = np.where(np.arange(MY) < MY // 2, np.arange(MY), ny - MY + np.arange(MY))
    fz = np.where(np.arange(MZ) < MZ // 2, np.arange(MZ), nz - MZ + np.arange(MZ))
    ay = 2.0 * np.pi / ny * (fy[:, None] * np.arange(ys) % ny)
    az = 2.0 * np.pi / nz * (fz[:, None] * np.arange(zs) % nz)
    both = ay[:, None, :, None] + az[None, :, None, :]
    table = np.stack([np.cos(both), -np.sin(both)]).reshape(2 * MY * MZ, ys * zs).astype(BF16)
    py = 2.0 * np.pi / ny * (fy[None] * (np.arange(ny // ys) * ys)[:, None] % ny)
    pz = 2.0 * np.pi / nz * (fz[None] * (np.arange(nz // zs) * zs)[:, None] % nz)
    turn = py[:, None, :, None] + pz[None, :, None, :]
    turn = np.stack([np.cos(turn), np.sin(turn)], axis=2).reshape(-1, 2, MY * MZ, 1)
    turn = np.broadcast_to(turn, turn.shape[:3] + (128,)).astype(np.float32)
    return table, np.ascontiguousarray(table.T), np.ascontiguousarray(turn)


def wide_tables(px, nx):
    high, low = x_tables(px, nx)
    inverse = [np.concatenate([t[0], t[1]], axis=1) for t in (high, low)]
    forward = [np.ascontiguousarray(t.T) for t in inverse]
    return forward, inverse


def swap_bits(tiles, first):
    lane = lax.broadcasted_iota(jnp.int32, tiles[0].shape, 1)
    tiles = list(tiles)
    for i in range(len(tiles).bit_length() - 1):
        shift = 1 << (first + i)
        upper = lane // shift % 2 == 1
        for t in range(len(tiles)):
            if not t >> i & 1:
                u = t | 1 << i
                low, high = tiles[t], tiles[u]
                tiles[t] = jnp.where(upper, pltpu.roll(high, shift, 1), low)
                tiles[u] = jnp.where(upper, high, pltpu.roll(low, 128 - shift, 1))
    return tiles


def flip(tiles):
    return swap_bits(tiles, 7 - (len(tiles).bit_length() - 1))


def rows_of(ref, start):
    chans, _, nx = ref.shape
    parts = [ref[:, pl.ds(start + u * SUB, SUB), :].reshape(chans * SUB, nx) for u in range(TALL // SUB)]
    return jnp.concatenate(parts, axis=1)


def gelu_pair(v, first, cotan):
    c0 = math.sqrt(2.0 / math.pi)
    v2 = v * v
    half = 0.5 + 0.5 * jnp.tanh(v * (c0 + (c0 * 0.044715) * v2))
    rebuilt = (first.astype(F32) - v * half).astype(BF16)
    inner = v * (2.0 * c0 + (6.0 * c0 * 0.044715) * v2)
    slope = (cotan.astype(F32) * (half + (half * (1.0 - half)) * inner)).astype(BF16)
    return rebuilt, slope


def fused_kernel(
    scales, sb_hbm, sa_hbm, ca_hbm, cb_hbm, th_hbm, uh_hbm, fh_hbm, fl_hbm, xh_hbm, xl_hbm, w_hbm, turn_hbm, pw_ref,
    fa, sb, sg_ref, pt_ref, fc, mix, th, uh, fh, fl, xh, xl, kron, w_raw, w, turn, part, land_x, land_y, gath, spec, spec_land, mode, back,
    back_land, grad, gf, acc, point, sg, pt_src, pt_land,
    in_sem, w_sem, sb_sem, sa_sem, ca_sem, cb_sem, rx_s, rx_r, ry_s, ry_r, gy_s, gy_r, gx_s, gx_r,
    dp_s, dp_r, pt_s, pt_r,
):
    scale_f, scale_i, grad_scale = scales
    groups = part.shape[1]
    py = part.shape[2]
    tall = part.shape[3]
    cells, nx = sb.shape[1:]
    samples = spec_land.shape[0] + 1
    modes = MY * MZ
    ix, iy, idp = lax.axis_index("px"), lax.axis_index("py"), lax.axis_index("dp")
    other_x = 1 - ix

    def near_y(offset):
        return lax.rem(iy + offset, py)

    def near_dp(offset):
        return lax.rem(idp + offset, samples)

    def chan(g):
        return pl.ds(g * GROUP, GROUP)

    def load(index, src, dst):
        return pltpu.make_async_copy(src, dst, in_sem.at[index])

    tables = [
        load(0, th_hbm, th), load(1, fh_hbm, fh), load(2, fl_hbm, fl),
        load(3, turn_hbm.at[ix * py + iy], turn), load(4, xh_hbm, xh), load(5, xl_hbm, xl), load(6, uh_hbm, uh),
    ]

    def load_weight(l):
        slot = lax.rem(l, WEIGHT_SLOTS)
        return pltpu.make_async_copy(w_hbm.at[:, l], w_raw.at[slot], w_sem.at[slot])

    def field_load(src, dst, sem, g):
        return pltpu.make_async_copy(src.at[chan(g)], dst.at[chan(g)], sem.at[g])

    barrier = pltpu.get_barrier_semaphore()
    pl.semaphore_signal(barrier, inc=1, device_id={"px": other_x}, device_id_type=MESH)
    for offset in range(1, py):
        pl.semaphore_signal(barrier, inc=1, device_id={"py": near_y(offset)}, device_id_type=MESH)
    for offset in range(1, samples):
        pl.semaphore_signal(barrier, inc=1, device_id={"dp": near_dp(offset)}, device_id_type=MESH)

    field_load(sb_hbm, sb, sb_sem, 0).start()
    for i in range(4):
        tables[i].start()
    for g in range(1, groups):
        field_load(sb_hbm, sb, sb_sem, g).start()
    for l in range(WEIGHT_SLOTS - 1):
        load_weight(l).start()
    for i in range(4, len(tables)):
        tables[i].start()
    for g in range(groups):
        field_load(sa_hbm, fa, sa_sem, g).start()
        field_load(ca_hbm, fc, ca_sem, g).start()
    pl.semaphore_wait(barrier, 1 + (py - 1) + (samples - 1))

    def remote(src, dst, send, recv, device):
        return pltpu.make_async_remote_copy(src, dst, send, recv, device_id=device, device_id_type=MESH)

    def reduce_x(f, g):
        return remote(
            part.at[other_x, g], land_x.at[g], rx_s.at[f, g], rx_r.at[f, g], {"px": other_x}
        )

    def reduce_y(f, g, offset):
        to = near_y(offset)
        return remote(
            part.at[ix, g, to], land_y.at[offset - 1, g], ry_s.at[f, offset - 1, g], ry_r.at[f, offset - 1, g],
            {"py": to},
        )

    def gather_y(f, g, offset):
        block = gath.at[ix, iy, g]
        return remote(block, block, gy_s.at[f, offset - 1, g], gy_r.at[f, offset - 1, g], {"py": near_y(offset)})

    def gather_x(f, g, offset):
        block = gath.at[ix, lax.rem(iy + py - offset, py), g]
        return remote(block, block, gx_s.at[f, offset, g], gx_r.at[f, offset, g], {"px": other_x})

    def after_x(f, g):
        reduce_x(f, g).wait_recv()
        part[ix, g] += land_x[g]
        for offset in range(1, py):
            reduce_y(f, g, offset).start()

    def finish_reduce(f, g):
        for offset in range(1, py):
            reduce_y(f, g, offset).wait_recv()
        value = part[ix, g, iy]
        for offset in range(1, py):
            value = value + land_y[offset - 1, g]
        return flip([value[8 * i : 8 * i + 8] for i in range(tall // 8)])

    def end_reduce_sends(f):
        for g in range(groups):
            reduce_x(f, g).wait_send()
            for offset in range(1, py):
                reduce_y(f, g, offset).wait_send()

    def start_gather(f, g, tiles):
        for i, tile in enumerate(flip(tiles)):
            gath[ix, iy, g, 8 * i : 8 * i + 8] = tile
        for offset in range(1, py):
            gather_y(f, g, offset).start()
        gather_x(f, g, 0).start()

    def forward_gather(f, g):
        for offset in range(1, py):
            gather_y(f, g, offset).wait_recv()
            gather_x(f, g, offset).start()

    def finish_gather(f, g):
        for offset in range(py):
            gather_x(f, g, offset).wait_recv()

    def end_gather_sends(f):
        for g in range(groups):
            for offset in range(1, py):
                gather_y(f, g, offset).wait_send()
            for offset in range(py):
                gather_x(f, g, offset).wait_send()

    def turns():
        cosine = jnp.concatenate([turn[0]] * GROUP, axis=1)
        sine = jnp.concatenate([turn[1]] * GROUP, axis=1)
        return cosine, sine

    def analyse(src, first, slot):
        value = jnp.concatenate([src[first], src[first + 1]], axis=1)
        acc[slot] = dot(th[...], value)

    def to_part(g):
        cosine, sine = turns()
        b0 = jnp.concatenate([acc[0, :modes], acc[1, :modes]], axis=1)
        b1 = jnp.concatenate([acc[0, modes:], acc[1, modes:]], axis=1)
        both = jnp.concatenate([b0 * cosine + b1 * sine, b1 * cosine - b0 * sine], axis=1)
        value = dot3(both, fh[...], fl[...])
        for i in range(2):
            part[i, g] = value[:, i * 128 : (i + 1) * 128].reshape(py, tall, 128)

    def build(g):
        value = jnp.concatenate([gath[i, :, g].reshape(modes, 128) for i in range(2)], axis=1)
        high, low = cut(value)
        cosine, sine = turns()
        wide = GROUP * nx
        both = dot(high, xh[...]) + dot(low, xh[...]) + dot(high, xl[...])
        g0, g1 = both[:, :wide], both[:, wide:]
        for t, field in enumerate((g0 * cosine - g1 * sine, g1 * cosine + g0 * sine)):
            field = field.astype(BF16)
            for h in range(2):
                gf[h, t * modes : (t + 1) * modes] = field[:, h * 2 * nx : (h + 1) * 2 * nx]

    def mix_rows(table, src, lo, hi):
        def step(q, carry):
            start = pl.multiple_of(q * TALL, TALL)
            value = dot(table[...], rows_of(src, start))
            for u in range(TALL // SUB):
                mix[:, pl.ds(start + u * SUB, SUB), :] = value[:, u * nx : (u + 1) * nx].reshape(-1, SUB, nx)
            return carry

        lax.fori_loop(lo, hi, step, 0)

    steps = cells // TALL
    side = point.shape[0]
    row = lax.broadcasted_iota(jnp.int32, (side, side), 0)
    column = lax.broadcasted_iota(jnp.int32, (side, side), 1)
    same = row % SUB == column % SUB

    for i in range(4):
        tables[i].wait()

    def forward(g, carry):
        field_load(sb_hbm, sb, sb_sem, g).wait()
        for p in range(2):
            analyse(sb, g * GROUP + 2 * p, p)
        to_part(g)
        reduce_x(0, g).start()

        @pl.when(g >= 1)
        def _():
            after_x(0, g - 1)

        return carry

    lax.fori_loop(0, groups, forward, 0)

    def turn_weight(l, carry):
        ahead = l + WEIGHT_SLOTS - 1

        @pl.when(ahead < MZ)
        def _():
            load_weight(ahead).start()

        load_weight(l).wait()
        slot = lax.rem(l, WEIGHT_SLOTS)
        chans = spec.shape[1]
        inner = 2 * chans
        kk = w_raw.shape[2] // inner
        tiles = []
        for t in range(inner):
            low, k = t // kk, t % kk
            some = range(low, w_raw.shape[1], inner // kk)
            rows = [w_raw[slot, j, k * inner : (k + 1) * inner, :] for j in some]
            tiles.append(jnp.concatenate(rows, axis=0).astype(F32).T)
        for r, tile in enumerate(swap_bits(tiles, 0)):
            w[r // chans, r % chans, l] = tile.astype(BF16)
        return carry

    lax.fori_loop(0, MZ // 2, turn_weight, 0)
    after_x(0, groups - 1)
    lax.fori_loop(MZ // 2, MZ, turn_weight, 0)
    spread = (row // SUB == column)[:, :SUB].astype(BF16)
    gathered = (lax.broadcasted_iota(jnp.int32, (SUB, side), 1) // SUB
                == lax.broadcasted_iota(jnp.int32, (SUB, side), 0)).astype(BF16)
    turned = lax.dot_general(spread, pw_ref[...], (((1,), (1,)), ((), ())), preferred_element_type=F32)
    kron[...] = jnp.where(same, dot(turned.astype(BF16), gathered), 0.0).astype(BF16)

    def take_spectrum(g, carry):
        tiles = finish_reduce(0, g)
        for q, tile in enumerate(tiles):
            spec[q % 2, g * GROUP + q // 2] = tile * scale_f
        return carry

    lax.fori_loop(0, groups, take_spectrum, 0)

    def blend(l, carry):
        real = jnp.zeros(w.shape[3:], F32)
        imag = jnp.zeros(w.shape[3:], F32)
        for c in range(spec.shape[1]):
            w_real, w_imag = w[0, c, l].astype(F32), w[1, c, l].astype(F32)
            s_real, s_imag = spec[0, c, pl.ds(l, 1), :], spec[1, c, pl.ds(l, 1), :]
            real += s_real * w_real - s_imag * w_imag
            imag += s_real * w_imag + s_imag * w_real
        mode[0, pl.ds(l, real.shape[0], stride=MZ), :] = real * scale_i
        mode[1, pl.ds(l, real.shape[0], stride=MZ), :] = imag * scale_i
        return carry

    lax.fori_loop(0, MZ, blend, 0)
    for g in range(groups):
        start_gather(0, g, [mode[q % 2, (g * GROUP + q // 2) * MZ :][:MZ] for q in range(2 * GROUP)])

    def send_spec(offset):
        return remote(
            spec, spec_land.at[offset - 1], dp_s.at[0, offset - 1], dp_r.at[0, offset - 1], {"dp": near_dp(offset)}
        )

    def send_back(offset):
        to = near_dp(offset)
        return remote(
            back.at[to], back_land.at[offset - 1], dp_s.at[1, offset - 1], dp_r.at[1, offset - 1], {"dp": to}
        )

    for offset in range(1, samples):
        send_spec(offset).start()
    end_reduce_sends(0)
    for i in range(4, len(tables)):
        tables[i].wait()
    mix_rows(kron, sb, 0, steps)
    forward_gather(0, 0)

    def middle(g, carry):
        @pl.when(g + 1 < groups)
        def _():
            forward_gather(0, g + 1)

        finish_gather(0, g)
        build(g)
        field_load(sa_hbm, fa, sa_sem, g).wait()
        field_load(ca_hbm, fc, ca_sem, g).wait()

        def pair(p, inner):
            first = g * GROUP + 2 * p

            total = None
            for start in range(0, cells, FINE):
                some = slice(start, start + FINE)
                field = dot(uh[some], gf[p])
                slopes = []
                for h in range(2):
                    v = field[:, h * nx : (h + 1) * nx] + mix[first + h, some]
                    rebuilt, slope = gelu_pair(v, fa[first + h, some], fc[first + h, some])
                    fa[first + h, some] = rebuilt
                    fc[first + h, some] = slope
                    slopes.append(slope)
                piece = dot(th[:, some], jnp.concatenate(slopes, axis=1))
                total = piece if total is None else total + piece
            acc[p] = total
            return inner

        lax.fori_loop(0, 2, pair, 0)
        to_part(g)
        reduce_x(1, g).start()

        @pl.when(g >= 1)
        def _():
            after_x(1, g - 1)

        return carry

    lax.fori_loop(0, groups, middle, 0)
    end_gather_sends(0)

    point[...] = jnp.zeros_like(point)

    def point_rows(lo, hi):
        def step(q, carry):
            start = pl.multiple_of(q * TALL, TALL)
            left, right = rows_of(sb, start), rows_of(fc, start)
            point[...] += lax.dot_general(left, right, (((1,), (1,)), ((), ())), preferred_element_type=F32)
            return carry

        lax.fori_loop(lo, hi, step, 0)

    point_rows(0, steps)
    after_x(1, groups - 1)
    for g in range(groups):
        field_load(cb_hbm, sb, cb_sem, g).start()
    kron[...] = jnp.where(same, dot(dot(spread, pw_ref[...]).astype(BF16), gathered), 0.0).astype(BF16)
    mix_rows(kron, fc, 0, steps)
    diagonal = jnp.where(same, point[...], 0.0)
    pt_src[0] = jnp.sum(diagonal.reshape(-1, SUB, point.shape[1]), axis=1)

    def sum_x():
        return remote(pt_src.at[0], pt_land.at[0, 0], pt_s.at[0], pt_r.at[0], {"px": other_x})

    def sum_y(offset):
        return remote(
            pt_src.at[1], pt_land.at[1, iy], pt_s.at[offset], pt_r.at[offset], {"py": near_y(offset)}
        )

    def sum_dp(offset):
        return remote(
            pt_src.at[2], pt_land.at[2, idp], pt_s.at[py - 1 + offset], pt_r.at[py - 1 + offset],
            {"dp": near_dp(offset)},
        )

    sum_x().start()

    def take_back(g, carry):
        tiles = finish_reduce(1, g)
        for q, tile in enumerate(tiles):
            back[g, q % 2, q // 2] = tile * scale_i
            mode[q % 2, pl.ds(pl.multiple_of((g * GROUP + q // 2) * MZ, MZ), MZ), :] = tile * scale_i
        return carry

    lax.fori_loop(0, groups, take_back, 0)
    for offset in range(1, samples):
        send_back(offset).start()
    sum_x().wait()
    pt_src[1] = pt_src[0] + pt_land[0, 0]
    pt_land[1, iy] = pt_src[1]
    for offset in range(1, py):
        sum_y(offset).start()

    def adjoint(g, carry):
        for l in range(MZ):
            b_real, b_imag = (mode[i, pl.ds(l, w.shape[3], stride=MZ), :] for i in range(2))
            for c in range(GROUP):
                w_real, w_imag = w[0, g * GROUP + c, l].astype(F32), w[1, g * GROUP + c, l].astype(F32)
                real = jnp.sum(b_real * w_real + b_imag * w_imag, axis=0, keepdims=True)
                imag = jnp.sum(b_imag * w_real - b_real * w_imag, axis=0, keepdims=True)
                grad[2 * c, l : l + 1] = real * scale_f
                grad[2 * c + 1, l : l + 1] = imag * scale_f
        start_gather(1, g, [grad[q] for q in range(2 * GROUP)])
        return carry

    lax.fori_loop(0, groups, adjoint, 0)

    for offset in range(1, samples):
        send_spec(offset).wait()
        send_back(offset).wait()

    def outer(c, carry):
        for d in range(GROUP):
            real = jnp.zeros((8, 128), F32)
            imag = jnp.zeros((8, 128), F32)
            for s in range(samples):
                if s == 0:
                    p_real, p_imag = spec[0, c], spec[1, c]
                    q_real, q_imag = back[idp, 0, d], back[idp, 1, d]
                else:
                    p_real, p_imag = spec_land[s - 1, 0, c], spec_land[s - 1, 1, c]
                    q_real, q_imag = back_land[s - 1, 0, d], back_land[s - 1, 1, d]
                real += p_real * q_real + p_imag * q_imag
                imag += p_real * q_imag - p_imag * q_real
            sg[0, d, pl.ds(pl.multiple_of(c * MZ, MZ), MZ), :] = real * grad_scale
            sg[1, d, pl.ds(pl.multiple_of(c * MZ, MZ), MZ), :] = imag * grad_scale
        return carry

    lax.fori_loop(0, spec.shape[1], outer, 0)

    def spread_some(l, carry):
        kk = sg_ref.shape[2] // (2 * GROUP)
        for r in range(2 * GROUP):
            value = sg[r // GROUP, r % GROUP, pl.ds(l, spec.shape[1], stride=MZ), :].T
            for j in range(sg_ref.shape[0]):
                sg_ref[j, l, pl.ds(r, kk, stride=2 * GROUP), :] = value[j * kk : (j + 1) * kk]
        return carry

    lax.fori_loop(0, MZ // 2, spread_some, 0)
    forward_gather(1, 0)
    lax.fori_loop(MZ // 2, MZ, spread_some, 0)
    for offset in range(1, py):
        sum_y(offset).wait()
    pt_src[2] = sum(pt_land[1, i] for i in range(py))
    pt_land[2, idp] = pt_src[2]
    for offset in range(1, samples):
        sum_dp(offset).start()

    def last(g, carry):
        @pl.when(g + 1 < groups)
        def _():
            forward_gather(1, g + 1)

        finish_gather(1, g)
        build(g)
        field_load(cb_hbm, sb, cb_sem, g).wait()

        def pair(p, inner):
            first = g * GROUP + 2 * p

            for start in range(0, cells, FINE):
                some = slice(start, start + FINE)
                field = dot(uh[some], gf[p])
                for h in range(2):
                    value = sb[first + h, some].astype(F32) + field[:, h * nx : (h + 1) * nx]
                    sb[first + h, some] = (value + mix[first + h, some]).astype(BF16)
            return inner

        lax.fori_loop(0, 2, pair, 0)
        return carry

    lax.fori_loop(0, groups, last, 0)

    for offset in range(1, samples):
        sum_dp(offset).wait()
    pt_ref[...] = sum(pt_land[2, i] for i in range(samples))
    end_reduce_sends(1)
    end_gather_sends(1)


def finish_kernel(point_scale, ia_ref, gb_ref, sg_ref, pt_ref, ia_hbm, gb_hbm, sg_hbm, point_ref, sems):
    copies = []
    for which, (src, dst) in enumerate(((ia_ref, ia_hbm), (gb_ref, gb_hbm), (sg_ref, sg_hbm))):
        parts = sems.shape[1]
        each = src.shape[0] // parts
        for i in range(parts):
            some = pl.ds(i * each, each)
            copies.append(pltpu.make_async_copy(src.at[some], dst.at[some], sems.at[which, i]))
    for copy in copies:
        copy.start()
    value = pt_ref[...]
    chans = point_ref.shape[0]
    row = lax.broadcasted_iota(jnp.int32, (value.shape[1], chans), 0)
    column = lax.broadcasted_iota(jnp.int32, (value.shape[1], chans), 1)
    ones = (row // SUB == column).astype(BF16)
    total = jnp.zeros(point_ref.shape, F32)
    for _ in range(3):
        part = value.astype(BF16)
        total += dot(part, ones)
        value -= part.astype(F32)
    point_ref[...] = total * point_scale
    for copy in copies:
        copy.wait()


def fused_device(state_a, state_b, cotan_a, cotan_b, spectral_weight, point_weight):
    samples, px, py = (lax.axis_size(name) for name in ("dp", "px", "py"))
    _, chans, ys, zs, nx = state_b.shape
    ny, nz = ys * px, zs * py
    cells, modes = ys * zs, MY * MZ
    groups = chans // GROUP
    kk = MX // px
    tall = modes // py
    total = nx * ny * nz
    scales = (
        1.0 / math.sqrt(total), 1.0 / math.sqrt(MX * MY * MZ), math.sqrt(MX * MY * MZ / (samples * total)),
    )
    th, uh, turn = (jnp.asarray(t) for t in base_tables((ys, zs, ny, nz)))
    (fh, fl), (xh, xl) = wide_tables(px, nx)
    fh, fl, xh, xl = (jnp.asarray(t) for t in (fh, fl, xh, xl))
    side = chans * SUB
    jj, ll = tall // MZ, MZ
    weight = spectral_weight.reshape(jj, ll, kk * 2 * chans, chans)
    spread = (jj, ll, kk * 2 * GROUP, chans)
    fields = [value.reshape(chans, cells, nx) for value in (state_b, state_a, cotan_a, cotan_b)]
    field = jax.ShapeDtypeStruct((chans, cells, nx), BF16)
    any_spec = pl.BlockSpec(memory_space=pl.ANY)
    vmem_spec = pl.BlockSpec(memory_space=pltpu.VMEM)
    dma = pltpu.SemaphoreType.DMA
    near = py - 1
    input_a, grad_b, sg, point = pl.pallas_call(
        lambda *refs: fused_kernel(scales, *refs),
        in_specs=[any_spec] * 12 + [vmem_spec],
        out_specs=[vmem_spec] * 4,
        out_shape=[
            pltpu.VMEM(field.shape, BF16), pltpu.VMEM(field.shape, BF16),
            pltpu.VMEM(spread, F32), pltpu.VMEM((chans, side), F32),
        ],
        scratch_shapes=[
            pltpu.VMEM((chans, cells, nx), BF16), pltpu.VMEM((chans, cells, nx), F32),
            pltpu.VMEM(th.shape, BF16), pltpu.VMEM(uh.shape, BF16), pltpu.VMEM(fh.shape, BF16),
            pltpu.VMEM(fl.shape, BF16), pltpu.VMEM(xh.shape, BF16), pltpu.VMEM(xl.shape, BF16),
            pltpu.VMEM((side, side), BF16),
            pltpu.VMEM((WEIGHT_SLOTS, jj) + weight.shape[2:], BF16), pltpu.VMEM((2, chans, MZ, chans, 128), BF16),
            pltpu.VMEM(turn.shape[1:], F32),
            pltpu.VMEM((px, groups, py, tall, 128), F32),
            pltpu.VMEM((groups, py, tall, 128), F32),
            pltpu.VMEM((near, groups, tall, 128), F32),
            pltpu.VMEM((px, py, groups, tall, 128), F32),
            pltpu.VMEM((2, chans, MZ, 128), F32),
            pltpu.VMEM((samples - 1, 2, chans, MZ, 128), F32),
            pltpu.VMEM((2, chans * MZ, 128), F32),
            pltpu.VMEM((samples, 2, GROUP, MZ, 128), F32),
            pltpu.VMEM((samples - 1, 2, GROUP, MZ, 128), F32),
            pltpu.VMEM((2 * GROUP, MZ, 128), F32),
            pltpu.VMEM((2, 2 * modes, 2 * nx), BF16),
            pltpu.VMEM((2, 2 * modes, 2 * nx), F32),
            pltpu.VMEM((side, side), F32),
            pltpu.VMEM((2, GROUP, chans * MZ, 128), F32),
            pltpu.VMEM((3, chans, side), F32),
            pltpu.VMEM((3, max(py, samples), chans, side), F32),
            dma((7,)), dma((WEIGHT_SLOTS,)), dma((groups,)), dma((groups,)), dma((groups,)), dma((groups,)),
            dma((2, groups)), dma((2, groups)), dma((2, near, groups)), dma((2, near, groups)),
            dma((2, near, groups)), dma((2, near, groups)), dma((2, py, groups)), dma((2, py, groups)),
            dma((2, samples - 1)), dma((2, samples - 1)), dma((1 + near + samples - 1,)), dma((1 + near + samples - 1,)),
        ],
        compiler_params=pltpu.CompilerParams(
            vmem_limit_bytes=FUSED_LIMIT, collective_id=4, has_side_effects=True
        ),
        interpret=INTERPRET,
        name="fused",
    )(*fields, th, uh, fh, fl, xh, xl, weight, turn, point_weight)
    point_scale = 1.0 / math.sqrt(samples * total)
    input_a, grad_b, spectral_grad, point_total = pl.pallas_call(
        lambda *refs: finish_kernel(point_scale, *refs),
        in_specs=[vmem_spec] * 4,
        out_specs=[any_spec] * 3 + [vmem_spec],
        out_shape=[
            field, field, jax.ShapeDtypeStruct(spread, F32), jax.ShapeDtypeStruct((chans, chans), F32),
        ],
        scratch_shapes=[dma((3, groups))],
        compiler_params=pltpu.CompilerParams(vmem_limit_bytes=FINISH_LIMIT),
        interpret=INTERPRET,
        name="finish",
    )(input_a, grad_b, sg, point)
    spectral_grad = spectral_grad.reshape(jj, ll, kk, 2, GROUP, chans).transpose(0, 1, 2, 3, 5, 4)
    full = state_b.shape
    return (input_a.reshape(full), grad_b.reshape(full), spectral_grad, point_total)


def solution(mesh):
    sizes = dict(mesh.shape)

    def body(*values):
        fits = fused_fits(values[1].shape, values[1].shape[0], sizes["dp"], sizes["px"], sizes["py"])
        return (fused_device if fits else general_device)(*values)

    return jax.shard_map(
        body,
        mesh=mesh,
        in_specs=(
            P("dp", None, "px", "py", None),
            P("dp", None, "px", "py", None),
            P("dp", None, "px", "py", None),
            P("dp", None, "px", "py", None),
            P("py", None, "px", None, None, None),
            P(),
        ),
        out_specs=(
            P("dp", None, "px", "py", None),
            P("dp", None, "px", "py", None),
            P("py", None, "px", None, None, "dp"),
            P(),
        ),
        check_vma=False,
    )
```

```python
import math

import jax
import jax.numpy as jnp
import numpy as np
from jax import lax
from jax.experimental import pallas as pl
from jax.experimental.pallas import tpu as pltpu
from jax.sharding import PartitionSpec as P

MX = 32
MY = 32
MZ = 8
GROUP = 4
SUB = 16
LIMIT = 56 * 1024 * 1024
INTERPRET = False
F32 = jnp.float32
BF16 = jnp.bfloat16


def kept(length_all, length_kept, position):
    return jnp.where(position < length_kept // 2, position, length_all - length_kept + position)


def angle(product, length_all):
    return (product % length_all).astype(F32) * (2.0 * math.pi / length_all)


def synthesis_table(shape):
    ys, zs, ny, nz = shape
    mode = lax.broadcasted_iota(jnp.int32, (1, MY * MZ), 1)
    fy = kept(ny, MY, mode // MZ)
    fz = kept(nz, MZ, mode % MZ)
    y = lax.axis_index("px") * ys + lax.broadcasted_iota(jnp.int32, (ys, 1), 0)
    z = lax.axis_index("py") * zs + lax.broadcasted_iota(jnp.int32, (zs, 1), 0)
    ay = angle(fy * y, ny)
    az = angle(fz * z, nz)
    cy, sy = jnp.cos(ay)[:, None, :], jnp.sin(ay)[:, None, :]
    cz, sz = jnp.cos(az)[None], jnp.sin(az)[None]
    table = jnp.concatenate([cy * cz - sy * sz, -(sy * cz + cy * sz)], axis=2)
    return table.reshape(ys * zs, 2 * MY * MZ)


def analysis_table(shape):
    ys, zs, ny, nz = shape
    cell = lax.broadcasted_iota(jnp.int32, (1, ys * zs), 1)
    y = lax.axis_index("px") * ys + cell // zs
    z = lax.axis_index("py") * zs + cell % zs
    fy = kept(ny, MY, lax.broadcasted_iota(jnp.int32, (MY, 1), 0))
    fz = kept(nz, MZ, lax.broadcasted_iota(jnp.int32, (MZ, 1), 0))
    ay = angle(fy * y, ny)
    az = angle(fz * z, nz)
    cy, sy = jnp.cos(ay)[:, None, :], jnp.sin(ay)[:, None, :]
    cz, sz = jnp.cos(az)[None], jnp.sin(az)[None]
    table = jnp.stack([cy * cz - sy * sz, -(sy * cz + cy * sz)])
    return table.reshape(2 * MY * MZ, ys * zs)


def x_tables(px, nx):
    kk = MX // px
    k = np.arange(MX).reshape(px, kk)
    phase = 2.0 * np.pi / nx * (k[:, :, None] * np.arange(nx) % nx)
    cosine, sine = np.cos(phase), np.sin(phase)
    table = np.zeros((2, px, GROUP, 2, kk, GROUP, nx))
    for c in range(GROUP):
        table[0, :, c, 0, :, c] = cosine
        table[0, :, c, 1, :, c] = -sine
        table[1, :, c, 0, :, c] = sine
        table[1, :, c, 1, :, c] = cosine
    table = table.reshape(2, 2 * MX * GROUP, GROUP * nx)
    high = table.astype(BF16)
    low = (table - high.astype(np.float64)).astype(BF16)
    return high, low


def dot(a, b):
    return jnp.dot(a, b, preferred_element_type=F32)


def cut(value):
    high = value.astype(BF16)
    return high, (value - high.astype(F32)).astype(BF16)


def dot3(a, high, low):
    ahigh, alow = cut(a)
    return dot(ahigh, high) + dot(alow, high) + dot(ahigh, low)


def to_modes(b0, b1, xh_ref, xl_ref):
    return dot3(b0, xh_ref[0], xl_ref[0]) + dot3(b1, xh_ref[1], xl_ref[1])


def store_modes(out_ref, group, value, px, py):
    wide = value.shape[1] // px
    tall = value.shape[0] // py
    for i in range(px):
        for j in range(py):
            out_ref[i * py + j, group] = value[j * tall : (j + 1) * tall, i * wide : (i + 1) * wide]


def build_fields(spec_ref, xh_ref, xl_ref, gh_ref, px, py):
    modes = MY * MZ
    for g in range(spec_ref.shape[1]):
        rows = []
        for j in range(py):
            rows.append(jnp.concatenate([spec_ref[i * py + j, g] for i in range(px)], axis=1))
        value = jnp.concatenate(rows, axis=0)
        for t in range(2):
            high = dot3(value, xh_ref[t], xl_ref[t]).astype(BF16)
            half = high.shape[1] // 2
            for h in range(2):
                gh_ref[2 * g + h, t * modes : (t + 1) * modes] = high[:, h * half : (h + 1) * half]


def pair_of(ref, start):
    chans, _, nx = ref.shape
    first = ref[:, pl.ds(start, SUB), :].reshape(chans * SUB, nx)
    second = ref[:, pl.ds(start + SUB, SUB), :].reshape(chans * SUB, nx)
    return jnp.concatenate([first, second], axis=1)


def channel_mix(kron_ref, in_ref, out_ref):
    chans, rows, nx = in_ref.shape

    def body(q, carry):
        start = pl.multiple_of(q * 2 * SUB, 2 * SUB)
        value = dot(kron_ref[...], pair_of(in_ref, start))
        out_ref[:, pl.ds(start, SUB), :] = value[:, :nx].reshape(chans, SUB, nx)
        out_ref[:, pl.ds(start + SUB, SUB), :] = value[:, nx:].reshape(chans, SUB, nx)
        return carry

    lax.fori_loop(0, rows // (2 * SUB), body, 0)


def position(py):
    return lax.axis_index("px") * py + lax.axis_index("py")


def partner(px, py, offset):
    other = lax.rem(position(py) + offset, px * py)
    return other, {"px": lax.div(other, py), "py": lax.rem(other, py)}


def greet(px, py):
    barrier = pltpu.get_barrier_semaphore()
    for offset in range(1, px * py):
        pl.semaphore_signal(
            barrier, inc=1, device_id=partner(px, py, offset)[1], device_id_type=pl.DeviceIdType.MESH
        )
    pl.semaphore_wait(barrier, px * py - 1)


def scatter_copy(px, py, offset, group, part_ref, land_ref, send_sem, recv_sem):
    other, device = partner(px, py, offset)
    return pltpu.make_async_remote_copy(
        part_ref.at[other, group], land_ref.at[offset, group], send_sem.at[offset, group], recv_sem.at[offset, group],
        device_id=device, device_id_type=pl.DeviceIdType.MESH,
    )


def scatter_kernel(px, py, part_ref, out_ref, land_ref, send_sem, recv_sem):
    count = px * py
    greet(px, py)
    groups = part_ref.shape[1]
    for g in range(groups):
        for offset in range(1, count):
            scatter_copy(px, py, offset, g, part_ref, land_ref, send_sem, recv_sem).start()
    out_ref[...] = part_ref[position(py)]
    for g in range(groups):
        for offset in range(1, count):
            scatter_copy(px, py, offset, g, part_ref, land_ref, send_sem, recv_sem).wait()
            out_ref[g] += land_ref[offset, g]


def gather_kernel(px, py, own_ref, out_ref, land_ref, send_sem, recv_sem):
    count = px * py
    greet(px, py)
    copies = []
    for offset in range(1, count):
        copies.append(
            pltpu.make_async_remote_copy(
                own_ref, land_ref.at[offset], send_sem.at[offset], recv_sem.at[offset],
                device_id=partner(px, py, offset)[1], device_id_type=pl.DeviceIdType.MESH,
            )
        )
        copies[-1].start()
    here = position(py)
    out_ref[here] = own_ref[...]
    for offset in range(1, count):
        copies[offset - 1].wait()
        out_ref[lax.rem(here + count - offset, count)] = land_ref[offset]


def mix_kernel(s_ref, w_ref, out_ref):
    chans = s_ref.shape[1]
    real = jnp.zeros(out_ref.shape[1:], F32)
    imag = jnp.zeros(out_ref.shape[1:], F32)
    for c in range(chans):
        s_real, s_imag = s_ref[0, c : c + 1], s_ref[1, c : c + 1]
        w_real, w_imag = w_ref[0, c].astype(F32), w_ref[1, c].astype(F32)
        real += s_real * w_real - s_imag * w_imag
        imag += s_real * w_imag + s_imag * w_real
    out_ref[0] = real
    out_ref[1] = imag


def adjoint_kernel(b_ref, w_ref, out_ref):
    b_real, b_imag = b_ref[0], b_ref[1]
    for c in range(w_ref.shape[1]):
        w_real, w_imag = w_ref[0, c].astype(F32), w_ref[1, c].astype(F32)
        out_ref[0, c : c + 1] = jnp.sum(b_real * w_real + b_imag * w_imag, axis=0, keepdims=True)
        out_ref[1, c : c + 1] = jnp.sum(b_imag * w_real - b_real * w_imag, axis=0, keepdims=True)


def forward_kernel(
    px, py, v_ref, th_ref, xh_ref, xl_ref, out_ref, part_ref, land_ref, send_sem, recv_sem
):
    modes = MY * MZ
    parts = []
    for p in range(GROUP // 2):
        value = jnp.concatenate([v_ref[2 * p], v_ref[2 * p + 1]], axis=1)
        parts.append(dot(th_ref[...], value))
    b0 = jnp.concatenate([part[:modes] for part in parts], axis=1)
    b1 = jnp.concatenate([part[modes:] for part in parts], axis=1)
    step = pl.program_id(0)
    store_modes(part_ref, step, to_modes(b0, b1, xh_ref, xl_ref), px, py)
    count = px * py

    @pl.when(step == 0)
    def _():
        greet(px, py)

    for offset in range(1, count):
        scatter_copy(px, py, offset, step, part_ref, land_ref, send_sem, recv_sem).start()

    @pl.when(step == pl.num_programs(0) - 1)
    def _():
        out_ref[...] = part_ref[position(py)]
        for g in range(part_ref.shape[1]):
            for offset in range(1, count):
                scatter_copy(px, py, offset, g, part_ref, land_ref, send_sem, recv_sem).wait()
                out_ref[g] += land_ref[offset, g]


def middle_kernel(
    px, py, steps, spec_ref, vb_ref, va_ref, ca_ref, uh_ref, th_ref, xh_ref, xl_ref, fh_ref, fl_ref,
    kron_ref, ia_ref, sl_ref, back_ref, point_ref, gh_ref, acc_ref, mix_ref,
):
    step = pl.program_id(0)
    modes = MY * MZ
    nx = vb_ref.shape[2]
    chans, rows = vb_ref.shape[:2]

    @pl.when(step == 0)
    def _():
        build_fields(spec_ref, xh_ref, xl_ref, gh_ref, px, py)
        acc_ref[...] = jnp.zeros_like(acc_ref)
        point_ref[...] = jnp.zeros_like(point_ref)

    channel_mix(kron_ref, vb_ref, mix_ref)
    c0 = math.sqrt(2.0 / math.pi)

    def body(p, carry):
        field = dot(uh_ref[...], gh_ref[p])
        slopes = []
        for h in range(2):
            d = 2 * p + h
            v = field[:, h * nx : (h + 1) * nx] + mix_ref[d]
            v2 = v * v
            t = jnp.tanh(v * (c0 + (c0 * 0.044715) * v2))
            half = 0.5 + 0.5 * t
            ia_ref[d] = (va_ref[d].astype(F32) - v * half).astype(BF16)
            deriv = half + (0.5 * v) * (1.0 - t * t) * (c0 + (3.0 * c0 * 0.044715) * v2)
            slope = (ca_ref[d].astype(F32) * deriv).astype(BF16)
            sl_ref[d] = slope
            slopes.append(slope)
        both = jnp.concatenate(slopes, axis=1)
        acc_ref[p] += dot(th_ref[...], both)
        return carry

    lax.fori_loop(0, chans // 2, body, 0)

    def point_body(q, carry):
        start = pl.multiple_of(q * 2 * SUB, 2 * SUB)
        point_ref[...] += lax.dot_general(
            pair_of(vb_ref, start), pair_of(sl_ref, start), (((1,), (1,)), ((), ())), preferred_element_type=F32
        )
        return carry

    lax.fori_loop(0, rows // (2 * SUB), point_body, 0)

    @pl.when(step == steps - 1)
    def _():
        for g in range(chans // GROUP):
            parts = [acc_ref[2 * g + h] for h in range(2)]
            b0 = jnp.concatenate([part[:modes] for part in parts], axis=1)
            b1 = jnp.concatenate([part[modes:] for part in parts], axis=1)
            store_modes(back_ref, g, to_modes(b0, b1, fh_ref, fl_ref), px, py)


def last_kernel(
    px, py, spec_ref, sl_ref, cb_ref, uh_ref, xh_ref, xl_ref, kron_ref, out_ref, gh_ref, mix_ref
):
    nx = sl_ref.shape[2]

    @pl.when(pl.program_id(0) == 0)
    def _():
        build_fields(spec_ref, xh_ref, xl_ref, gh_ref, px, py)

    channel_mix(kron_ref, sl_ref, mix_ref)

    def body(p, carry):
        field = dot(uh_ref[...], gh_ref[p])
        for h in range(2):
            d = 2 * p + h
            value = cb_ref[d].astype(F32) + field[:, h * nx : (h + 1) * nx] + mix_ref[d]
            out_ref[d] = value.astype(BF16)
        return carry

    lax.fori_loop(0, sl_ref.shape[0] // 2, body, 0)


def whole(shape):
    return pl.BlockSpec(shape, lambda i: (0,) * len(shape), pipeline_mode=pl.Buffered(1))


def general_device(state_a, state_b, cotan_a, cotan_b, spectral_weight, point_weight):
    samples, px, py = (lax.axis_size(name) for name in ("dp", "px", "py"))
    _, chans, ys, zs, nx = state_b.shape
    ny, nz = ys * px, zs * py
    cells, modes = ys * zs, MY * MZ
    groups = chans // GROUP
    kk = MX // px
    tall, wide = modes // py, 2 * MX * GROUP // px
    own = tall * kk
    scale_f = 1.0 / math.sqrt(nx * ny * nz)
    scale_i = 1.0 / math.sqrt(MX * MY * MZ)
    grad_scale = math.sqrt(MX * MY * MZ / (samples * nx * ny * nz))
    point_scale = 1.0 / math.sqrt(samples * nx * ny * nz)
    shape = (ys, zs, ny, nz)
    th = analysis_table(shape).astype(BF16)
    uh = synthesis_table(shape).astype(BF16)
    xh, xl = x_tables(px, nx)
    fh, fl = (jnp.asarray(np.ascontiguousarray(table.transpose(0, 2, 1))) for table in (xh, xl))
    xh, xl = jnp.asarray(xh), jnp.asarray(xl)
    eye = jnp.eye(SUB, dtype=BF16)
    kron_f = (point_weight.T[:, None, :, None] * eye[None, :, None, :]).reshape(chans * SUB, chans * SUB)
    kron_b = (point_weight[:, None, :, None] * eye[None, :, None, :]).reshape(chans * SUB, chans * SUB)
    field_a, field_b, cot_a, cot_b = (
        value.reshape(chans, cells, nx) for value in (state_a, state_b, cotan_a, cotan_b)
    )
    part_shape = jax.ShapeDtypeStruct((px * py, groups, tall, wide), F32)
    params = pltpu.CompilerParams(vmem_limit_bytes=LIMIT)

    count = px * py
    own_shape = jax.ShapeDtypeStruct((groups, tall, wide), F32)
    exchange = [
        pltpu.VMEM(part_shape.shape, F32),
        pltpu.SemaphoreType.DMA((count, groups)),
        pltpu.SemaphoreType.DMA((count, groups)),
    ]

    def linked(number):
        return pltpu.CompilerParams(vmem_limit_bytes=LIMIT, collective_id=number, has_side_effects=True)

    def to_channels(value):
        value = value.reshape(groups, tall, GROUP, 2, kk).transpose(3, 0, 2, 1, 4)
        return value.reshape(2, chans, own)

    def gather(value, number):
        value = value.reshape(2, groups, GROUP, tall, kk).transpose(1, 3, 2, 0, 4)
        value = value.reshape(groups, tall, wide)
        return pl.pallas_call(
            lambda *refs: gather_kernel(px, py, *refs),
            in_specs=[pl.BlockSpec(memory_space=pltpu.VMEM)],
            out_specs=pl.BlockSpec(memory_space=pltpu.VMEM),
            out_shape=part_shape,
            scratch_shapes=[
                pltpu.VMEM(part_shape.shape, F32), pltpu.SemaphoreType.DMA((count,)), pltpu.SemaphoreType.DMA((count,)),
            ],
            compiler_params=linked(number),
            interpret=INTERPRET,
            name="gather",
        )(value)

    def mode_product(kernel, value, name):
        return pl.pallas_call(
            kernel,
            out_shape=jax.ShapeDtypeStruct((2, chans, own), F32),
            compiler_params=params,
            interpret=INTERPRET,
            name=name,
        )(value, weight)

    spectrum = pl.pallas_call(
        lambda *refs: forward_kernel(px, py, *refs),
        grid=(groups,),
        in_specs=[
            pl.BlockSpec((GROUP, cells, nx), lambda i: (i, 0, 0)),
            whole(th.shape), whole(fh.shape), whole(fl.shape),
        ],
        out_specs=whole(own_shape.shape),
        out_shape=own_shape,
        scratch_shapes=[pltpu.VMEM(part_shape.shape, F32)] + exchange,
        compiler_params=linked(0),
        interpret=INTERPRET,
        name="forward",
    )(field_b, th, fh, fl)
    weight = spectral_weight.transpose(3, 4, 5, 0, 1, 2).reshape(2, chans, chans, own)
    spectrum = to_channels(spectrum) * scale_f
    mixed = gather(mode_product(mix_kernel, spectrum, "mix") * scale_i, 1)

    rows = min(256, cells)
    steps = cells // rows
    block = pl.BlockSpec((chans, rows, nx), lambda i: (0, i, 0))
    u_block = pl.BlockSpec((rows, 2 * modes), lambda i: (i, 0))
    t_block = pl.BlockSpec((2 * modes, rows), lambda i: (0, i))
    field_shape = jax.ShapeDtypeStruct((chans, cells, nx), BF16)
    side = chans * SUB
    g_scratch = [pltpu.VMEM((chans // 2, 2 * modes, 2 * nx), BF16)]
    input_a, slope, back_part, point = pl.pallas_call(
        lambda *refs: middle_kernel(px, py, steps, *refs),
        grid=(steps,),
        in_specs=[
            whole(part_shape.shape), block, block, block, u_block, t_block,
            whole(xh.shape), whole(xl.shape), whole(fh.shape), whole(fl.shape), whole((side, side)),
        ],
        out_specs=[block, block, whole(part_shape.shape), whole((side, side))],
        out_shape=[field_shape, field_shape, part_shape, jax.ShapeDtypeStruct((side, side), F32)],
        scratch_shapes=g_scratch
        + [pltpu.VMEM((chans // 2, 2 * modes, 2 * nx), F32), pltpu.VMEM((chans, rows, nx), F32)],
        compiler_params=params,
        interpret=INTERPRET,
        name="middle",
    )(mixed, field_b, field_a, cot_a, uh, th, xh, xl, fh, fl, kron_f)

    back = pl.pallas_call(
        lambda *refs: scatter_kernel(px, py, *refs),
        in_specs=[pl.BlockSpec(memory_space=pltpu.VMEM)],
        out_specs=pl.BlockSpec(memory_space=pltpu.VMEM),
        out_shape=own_shape,
        scratch_shapes=exchange,
        compiler_params=linked(2),
        interpret=INTERPRET,
        name="scatter",
    )(back_part)
    back = to_channels(back) * scale_i
    grad_spec = gather(mode_product(adjoint_kernel, back, "adjoint") * scale_f, 3)
    grad_b = pl.pallas_call(
        lambda *refs: last_kernel(px, py, *refs),
        grid=(steps,),
        in_specs=[
            whole(part_shape.shape), block, block, u_block,
            whole(xh.shape), whole(xl.shape), whole((side, side)),
        ],
        out_specs=block,
        out_shape=field_shape,
        scratch_shapes=g_scratch + [pltpu.VMEM((chans, rows, nx), F32)],
        compiler_params=params,
        interpret=INTERPRET,
        name="last",
    )(grad_spec, slope, cot_b, uh, xh, xl, kron_b)

    share = chans // samples
    spec_all = lax.all_gather(spectrum, "dp", axis=0)
    back_all = lax.all_gather(back, "dp", axis=0)
    back_own = lax.dynamic_slice_in_dim(back_all, lax.axis_index("dp") * share, share, axis=2)
    p_real, p_imag = spec_all[:, 0, :, None], spec_all[:, 1, :, None]
    q_real, q_imag = back_own[:, 0, None], back_own[:, 1, None]
    grad_real = jnp.sum(p_real * q_real + p_imag * q_imag, axis=0)
    grad_imag = jnp.sum(p_real * q_imag - p_imag * q_real, axis=0)
    grad = jnp.stack([grad_real, grad_imag]) * grad_scale
    spectral_grad = grad.reshape(2, chans, share, tall // MZ, MZ, kk).transpose(3, 4, 5, 0, 1, 2)

    point = jnp.sum(point.reshape(chans, SUB, chans, SUB) * jnp.eye(SUB, dtype=F32)[None, :, None, :], axis=(1, 3))
    point_total = lax.psum(point, ("dp", "px", "py")) * point_scale
    full = state_b.shape
    return (input_a.reshape(full), grad_b.reshape(full), spectral_grad, point_total)


MESH = pl.DeviceIdType.MESH
TALL = 512
FINE = 256
WEIGHT_SLOTS = 2
FUSED_LIMIT = 44900 * 1024
FINISH_LIMIT = 8 * 1024 * 1024


def fused_fits(shape, local_samples, samples, px, py):
    _, chans, ys, zs, nx = shape
    kk = MX // px
    tall = MY * MZ // py
    return (
        local_samples == 1
        and 2 * kk * GROUP == 128
        and nx == 128
        and MZ == 8
        and tall // MZ == 128 // kk
        and samples * GROUP == chans
        and (ys * zs) % TALL == 0
    )


def base_tables(shape):
    ys, zs, ny, nz = shape
    fy = np.where(np.arange(MY) < MY // 2, np.arange(MY), ny - MY + np.arange(MY))
    fz = np.where(np.arange(MZ) < MZ // 2, np.arange(MZ), nz - MZ + np.arange(MZ))
    ay = 2.0 * np.pi / ny * (fy[:, None] * np.arange(ys) % ny)
    az = 2.0 * np.pi / nz * (fz[:, None] * np.arange(zs) % nz)
    both = ay[:, None, :, None] + az[None, :, None, :]
    table = np.stack([np.cos(both), -np.sin(both)]).reshape(2 * MY * MZ, ys * zs).astype(BF16)
    py = 2.0 * np.pi / ny * (fy[None] * (np.arange(ny // ys) * ys)[:, None] % ny)
    pz = 2.0 * np.pi / nz * (fz[None] * (np.arange(nz // zs) * zs)[:, None] % nz)
    turn = py[:, None, :, None] + pz[None, :, None, :]
    turn = np.stack([np.cos(turn), np.sin(turn)], axis=2).reshape(-1, 2, MY * MZ, 1)
    turn = np.broadcast_to(turn, turn.shape[:3] + (128,)).astype(np.float32)
    return table, np.ascontiguousarray(table.T), np.ascontiguousarray(turn)


def wide_tables(px, nx):
    high, low = x_tables(px, nx)
    inverse = [np.concatenate([t[0], t[1]], axis=1) for t in (high, low)]
    forward = [np.ascontiguousarray(t.T) for t in inverse]
    return forward, inverse


def swap_bits(tiles, first):
    lane = lax.broadcasted_iota(jnp.int32, tiles[0].shape, 1)
    tiles = list(tiles)
    for i in range(len(tiles).bit_length() - 1):
        shift = 1 << (first + i)
        upper = lane // shift % 2 == 1
        for t in range(len(tiles)):
            if not t >> i & 1:
                u = t | 1 << i
                low, high = tiles[t], tiles[u]
                tiles[t] = jnp.where(upper, pltpu.roll(high, shift, 1), low)
                tiles[u] = jnp.where(upper, high, pltpu.roll(low, 128 - shift, 1))
    return tiles


def flip(tiles):
    return swap_bits(tiles, 7 - (len(tiles).bit_length() - 1))


def rows_of(ref, start):
    chans, _, nx = ref.shape
    parts = [ref[:, pl.ds(start + u * SUB, SUB), :].reshape(chans * SUB, nx) for u in range(TALL // SUB)]
    return jnp.concatenate(parts, axis=1)


def gelu_pair(v, first, cotan):
    c0 = math.sqrt(2.0 / math.pi)
    v2 = v * v
    half = 0.5 + 0.5 * jnp.tanh(v * (c0 + (c0 * 0.044715) * v2))
    rebuilt = (first.astype(F32) - v * half).astype(BF16)
    inner = v * (2.0 * c0 + (6.0 * c0 * 0.044715) * v2)
    slope = (cotan.astype(F32) * (half + (half * (1.0 - half)) * inner)).astype(BF16)
    return rebuilt, slope


def fused_kernel(
    scales, sb_hbm, sa_hbm, ca_hbm, cb_hbm, th_hbm, uh_hbm, fh_hbm, fl_hbm, xh_hbm, xl_hbm, w_hbm, turn_hbm, pw_ref,
    fa, sb, sg_ref, pt_ref, fc, mix, th, uh, fh, fl, xh, xl, kron, w_raw, w, turn, part, land_x, land_y, gath, spec, spec_land, mode, back,
    back_land, grad, gf, acc, point, sg, pt_src, pt_land,
    in_sem, w_sem, sb_sem, sa_sem, ca_sem, cb_sem, rx_s, rx_r, ry_s, ry_r, gy_s, gy_r, gx_s, gx_r,
    dp_s, dp_r, pt_s, pt_r,
):
    scale_f, scale_i, grad_scale = scales
    groups = part.shape[1]
    py = part.shape[2]
    tall = part.shape[3]
    cells, nx = sb.shape[1:]
    samples = spec_land.shape[0] + 1
    modes = MY * MZ
    ix, iy, idp = lax.axis_index("px"), lax.axis_index("py"), lax.axis_index("dp")
    other_x = 1 - ix

    def near_y(offset):
        return lax.rem(iy + offset, py)

    def near_dp(offset):
        return lax.rem(idp + offset, samples)

    def chan(g):
        return pl.ds(g * GROUP, GROUP)

    def load(index, src, dst):
        return pltpu.make_async_copy(src, dst, in_sem.at[index])

    tables = [
        load(0, th_hbm, th), load(1, fh_hbm, fh), load(2, fl_hbm, fl),
        load(3, turn_hbm.at[ix * py + iy], turn), load(4, xh_hbm, xh), load(5, xl_hbm, xl), load(6, uh_hbm, uh),
    ]

    def load_weight(l):
        slot = lax.rem(l, WEIGHT_SLOTS)
        return pltpu.make_async_copy(w_hbm.at[:, l], w_raw.at[slot], w_sem.at[slot])

    def field_load(src, dst, sem, g):
        return pltpu.make_async_copy(src.at[chan(g)], dst.at[chan(g)], sem.at[g])

    barrier = pltpu.get_barrier_semaphore()
    pl.semaphore_signal(barrier, inc=1, device_id={"px": other_x}, device_id_type=MESH)
    for offset in range(1, py):
        pl.semaphore_signal(barrier, inc=1, device_id={"py": near_y(offset)}, device_id_type=MESH)
    for offset in range(1, samples):
        pl.semaphore_signal(barrier, inc=1, device_id={"dp": near_dp(offset)}, device_id_type=MESH)

    field_load(sb_hbm, sb, sb_sem, 0).start()
    for i in range(4):
        tables[i].start()
    for g in range(1, groups):
        field_load(sb_hbm, sb, sb_sem, g).start()
    for l in range(WEIGHT_SLOTS - 1):
        load_weight(l).start()
    for i in range(4, len(tables)):
        tables[i].start()
    for g in range(groups):
        field_load(sa_hbm, fa, sa_sem, g).start()
        field_load(ca_hbm, fc, ca_sem, g).start()
    pl.semaphore_wait(barrier, 1 + (py - 1) + (samples - 1))

    def remote(src, dst, send, recv, device):
        return pltpu.make_async_remote_copy(src, dst, send, recv, device_id=device, device_id_type=MESH)

    def reduce_x(f, g):
        return remote(
            part.at[other_x, g], land_x.at[g], rx_s.at[f, g], rx_r.at[f, g], {"px": other_x}
        )

    def reduce_y(f, g, offset):
        to = near_y(offset)
        return remote(
            part.at[ix, g, to], land_y.at[offset - 1, g], ry_s.at[f, offset - 1, g], ry_r.at[f, offset - 1, g],
            {"py": to},
        )

    def gather_y(f, g, offset):
        block = gath.at[ix, iy, g]
        return remote(block, block, gy_s.at[f, offset - 1, g], gy_r.at[f, offset - 1, g], {"py": near_y(offset)})

    def gather_x(f, g, offset):
        block = gath.at[ix, lax.rem(iy + py - offset, py), g]
        return remote(block, block, gx_s.at[f, offset, g], gx_r.at[f, offset, g], {"px": other_x})

    def after_x(f, g):
        reduce_x(f, g).wait_recv()
        part[ix, g] += land_x[g]
        for offset in range(1, py):
            reduce_y(f, g, offset).start()

    def finish_reduce(f, g):
        for offset in range(1, py):
            reduce_y(f, g, offset).wait_recv()
        value = part[ix, g, iy]
        for offset in range(1, py):
            value = value + land_y[offset - 1, g]
        return flip([value[8 * i : 8 * i + 8] for i in range(tall // 8)])

    def end_reduce_sends(f):
        for g in range(groups):
            reduce_x(f, g).wait_send()
            for offset in range(1, py):
                reduce_y(f, g, offset).wait_send()

    def start_gather(f, g, tiles):
        for i, tile in enumerate(flip(tiles)):
            gath[ix, iy, g, 8 * i : 8 * i + 8] = tile
        for offset in range(1, py):
            gather_y(f, g, offset).start()
        gather_x(f, g, 0).start()

    def forward_gather(f, g):
        for offset in range(1, py):
            gather_y(f, g, offset).wait_recv()
            gather_x(f, g, offset).start()

    def finish_gather(f, g):
        for offset in range(py):
            gather_x(f, g, offset).wait_recv()

    def end_gather_sends(f):
        for g in range(groups):
            for offset in range(1, py):
                gather_y(f, g, offset).wait_send()
            for offset in range(py):
                gather_x(f, g, offset).wait_send()

    def turns():
        cosine = jnp.concatenate([turn[0]] * GROUP, axis=1)
        sine = jnp.concatenate([turn[1]] * GROUP, axis=1)
        return cosine, sine

    def analyse(src, first, slot):
        value = jnp.concatenate([src[first], src[first + 1]], axis=1)
        acc[slot] = dot(th[...], value)

    def to_part(g):
        cosine, sine = turns()
        b0 = jnp.concatenate([acc[0, :modes], acc[1, :modes]], axis=1)
        b1 = jnp.concatenate([acc[0, modes:], acc[1, modes:]], axis=1)
        both = jnp.concatenate([b0 * cosine + b1 * sine, b1 * cosine - b0 * sine], axis=1)
        value = dot3(both, fh[...], fl[...])
        for i in range(2):
            part[i, g] = value[:, i * 128 : (i + 1) * 128].reshape(py, tall, 128)

    def build(g):
        value = jnp.concatenate([gath[i, :, g].reshape(modes, 128) for i in range(2)], axis=1)
        high, low = cut(value)
        cosine, sine = turns()
        wide = GROUP * nx
        both = dot(high, xh[...]) + dot(low, xh[...]) + dot(high, xl[...])
        g0, g1 = both[:, :wide], both[:, wide:]
        for t, field in enumerate((g0 * cosine - g1 * sine, g1 * cosine + g0 * sine)):
            field = field.astype(BF16)
            for h in range(2):
                gf[h, t * modes : (t + 1) * modes] = field[:, h * 2 * nx : (h + 1) * 2 * nx]

    def mix_rows(table, src, lo, hi):
        def step(q, carry):
            start = pl.multiple_of(q * TALL, TALL)
            value = dot(table[...], rows_of(src, start))
            for u in range(TALL // SUB):
                mix[:, pl.ds(start + u * SUB, SUB), :] = value[:, u * nx : (u + 1) * nx].reshape(-1, SUB, nx)
            return carry

        lax.fori_loop(lo, hi, step, 0)

    steps = cells // TALL
    side = point.shape[0]
    row = lax.broadcasted_iota(jnp.int32, (side, side), 0)
    column = lax.broadcasted_iota(jnp.int32, (side, side), 1)
    same = row % SUB == column % SUB

    for i in range(4):
        tables[i].wait()

    def forward(g, carry):
        field_load(sb_hbm, sb, sb_sem, g).wait()
        for p in range(2):
            analyse(sb, g * GROUP + 2 * p, p)
        to_part(g)
        reduce_x(0, g).start()

        @pl.when(g >= 1)
        def _():
            after_x(0, g - 1)

        return carry

    lax.fori_loop(0, groups, forward, 0)

    def turn_weight(l, carry):
        ahead = l + WEIGHT_SLOTS - 1

        @pl.when(ahead < MZ)
        def _():
            load_weight(ahead).start()

        load_weight(l).wait()
        slot = lax.rem(l, WEIGHT_SLOTS)
        chans = spec.shape[1]
        inner = 2 * chans
        kk = w_raw.shape[2] // inner
        tiles = []
        for t in range(inner):
            low, k = t // kk, t % kk
            some = range(low, w_raw.shape[1], inner // kk)
            rows = [w_raw[slot, j, k * inner : (k + 1) * inner, :] for j in some]
            tiles.append(jnp.concatenate(rows, axis=0).astype(F32).T)
        for r, tile in enumerate(swap_bits(tiles, 0)):
            w[r // chans, r % chans, l] = tile.astype(BF16)
        return carry

    lax.fori_loop(0, MZ // 2, turn_weight, 0)
    after_x(0, groups - 1)
    lax.fori_loop(MZ // 2, MZ, turn_weight, 0)
    spread = (row // SUB == column)[:, :SUB].astype(BF16)
    gathered = (lax.broadcasted_iota(jnp.int32, (SUB, side), 1) // SUB
                == lax.broadcasted_iota(jnp.int32, (SUB, side), 0)).astype(BF16)
    turned = lax.dot_general(spread, pw_ref[...], (((1,), (1,)), ((), ())), preferred_element_type=F32)
    kron[...] = jnp.where(same, dot(turned.astype(BF16), gathered), 0.0).astype(BF16)

    def take_spectrum(g, carry):
        tiles = finish_reduce(0, g)
        for q, tile in enumerate(tiles):
            spec[q % 2, g * GROUP + q // 2] = tile * scale_f
        return carry

    lax.fori_loop(0, groups, take_spectrum, 0)

    def blend(l, carry):
        real = jnp.zeros(w.shape[3:], F32)
        imag = jnp.zeros(w.shape[3:], F32)
        for c in range(spec.shape[1]):
            w_real, w_imag = w[0, c, l].astype(F32), w[1, c, l].astype(F32)
            s_real, s_imag = spec[0, c, pl.ds(l, 1), :], spec[1, c, pl.ds(l, 1), :]
            real += s_real * w_real - s_imag * w_imag
            imag += s_real * w_imag + s_imag * w_real
        mode[0, pl.ds(l, real.shape[0], stride=MZ), :] = real * scale_i
        mode[1, pl.ds(l, real.shape[0], stride=MZ), :] = imag * scale_i
        return carry

    lax.fori_loop(0, MZ, blend, 0)
    for g in range(groups):
        start_gather(0, g, [mode[q % 2, (g * GROUP + q // 2) * MZ :][:MZ] for q in range(2 * GROUP)])

    def send_spec(offset):
        return remote(
            spec, spec_land.at[offset - 1], dp_s.at[0, offset - 1], dp_r.at[0, offset - 1], {"dp": near_dp(offset)}
        )

    def send_back(offset):
        to = near_dp(offset)
        return remote(
            back.at[to], back_land.at[offset - 1], dp_s.at[1, offset - 1], dp_r.at[1, offset - 1], {"dp": to}
        )

    for offset in range(1, samples):
        send_spec(offset).start()
    end_reduce_sends(0)
    for i in range(4, len(tables)):
        tables[i].wait()
    mix_rows(kron, sb, 0, steps)
    forward_gather(0, 0)

    def middle(g, carry):
        @pl.when(g + 1 < groups)
        def _():
            forward_gather(0, g + 1)

        finish_gather(0, g)
        build(g)
        field_load(sa_hbm, fa, sa_sem, g).wait()
        field_load(ca_hbm, fc, ca_sem, g).wait()

        def pair(p):
            first = g * GROUP + 2 * p

            total = None
            for start in range(0, cells, FINE):
                some = slice(start, start + FINE)
                field = dot(uh[some], gf[p])
                slopes = []
                for h in range(2):
                    v = field[:, h * nx : (h + 1) * nx] + mix[first + h, some]
                    rebuilt, slope = gelu_pair(v, fa[first + h, some], fc[first + h, some])
                    fa[first + h, some] = rebuilt
                    fc[first + h, some] = slope
                    slopes.append(slope)
                piece = dot(th[:, some], jnp.concatenate(slopes, axis=1))
                total = piece if total is None else total + piece
            acc[p] = total

        for p in range(2):
            pair(p)
        to_part(g)
        reduce_x(1, g).start()

        @pl.when(g >= 1)
        def _():
            after_x(1, g - 1)

        return carry

    lax.fori_loop(0, groups, middle, 0)
    end_gather_sends(0)

    point[...] = jnp.zeros_like(point)

    def point_rows(lo, hi):
        def step(q, carry):
            start = pl.multiple_of(q * TALL, TALL)
            left, right = rows_of(sb, start), rows_of(fc, start)
            point[...] += lax.dot_general(left, right, (((1,), (1,)), ((), ())), preferred_element_type=F32)
            return carry

        lax.fori_loop(lo, hi, step, 0)

    point_rows(0, steps)
    after_x(1, groups - 1)
    for g in range(groups):
        field_load(cb_hbm, sb, cb_sem, g).start()
    kron[...] = jnp.where(same, dot(dot(spread, pw_ref[...]).astype(BF16), gathered), 0.0).astype(BF16)
    mix_rows(kron, fc, 0, steps)
    diagonal = jnp.where(same, point[...], 0.0)
    pt_src[0] = jnp.sum(diagonal.reshape(-1, SUB, point.shape[1]), axis=1)

    def sum_x():
        return remote(pt_src.at[0], pt_land.at[0, 0], pt_s.at[0], pt_r.at[0], {"px": other_x})

    def sum_y(offset):
        return remote(
            pt_src.at[1], pt_land.at[1, iy], pt_s.at[offset], pt_r.at[offset], {"py": near_y(offset)}
        )

    def sum_dp(offset):
        return remote(
            pt_src.at[2], pt_land.at[2, idp], pt_s.at[py - 1 + offset], pt_r.at[py - 1 + offset],
            {"dp": near_dp(offset)},
        )

    sum_x().start()

    def take_back(g, carry):
        tiles = finish_reduce(1, g)
        for q, tile in enumerate(tiles):
            back[g, q % 2, q // 2] = tile * scale_i
            mode[q % 2, pl.ds(pl.multiple_of((g * GROUP + q // 2) * MZ, MZ), MZ), :] = tile * scale_i
        return carry

    lax.fori_loop(0, groups, take_back, 0)
    for offset in range(1, samples):
        send_back(offset).start()
    sum_x().wait()
    pt_src[1] = pt_src[0] + pt_land[0, 0]
    pt_land[1, iy] = pt_src[1]
    for offset in range(1, py):
        sum_y(offset).start()

    def adjoint(g, carry):
        for l in range(MZ):
            b_real, b_imag = (mode[i, pl.ds(l, w.shape[3], stride=MZ), :] for i in range(2))
            for c in range(GROUP):
                w_real, w_imag = w[0, g * GROUP + c, l].astype(F32), w[1, g * GROUP + c, l].astype(F32)
                real = jnp.sum(b_real * w_real + b_imag * w_imag, axis=0, keepdims=True)
                imag = jnp.sum(b_imag * w_real - b_real * w_imag, axis=0, keepdims=True)
                grad[2 * c, l : l + 1] = real * scale_f
                grad[2 * c + 1, l : l + 1] = imag * scale_f
        start_gather(1, g, [grad[q] for q in range(2 * GROUP)])
        return carry

    lax.fori_loop(0, groups, adjoint, 0)

    for offset in range(1, samples):
        send_spec(offset).wait()
        send_back(offset).wait()

    def outer(c, carry):
        for d in range(GROUP):
            real = jnp.zeros((8, 128), F32)
            imag = jnp.zeros((8, 128), F32)
            for s in range(samples):
                if s == 0:
                    p_real, p_imag = spec[0, c], spec[1, c]
                    q_real, q_imag = back[idp, 0, d], back[idp, 1, d]
                else:
                    p_real, p_imag = spec_land[s - 1, 0, c], spec_land[s - 1, 1, c]
                    q_real, q_imag = back_land[s - 1, 0, d], back_land[s - 1, 1, d]
                real += p_real * q_real + p_imag * q_imag
                imag += p_real * q_imag - p_imag * q_real
            sg[0, d, pl.ds(pl.multiple_of(c * MZ, MZ), MZ), :] = real * grad_scale
            sg[1, d, pl.ds(pl.multiple_of(c * MZ, MZ), MZ), :] = imag * grad_scale
        return carry

    lax.fori_loop(0, spec.shape[1], outer, 0)

    def spread_some(l, carry):
        kk = sg_ref.shape[2] // (2 * GROUP)
        for r in range(2 * GROUP):
            value = sg[r // GROUP, r % GROUP, pl.ds(l, spec.shape[1], stride=MZ), :].T
            for j in range(sg_ref.shape[0]):
                sg_ref[j, l, pl.ds(r, kk, stride=2 * GROUP), :] = value[j * kk : (j + 1) * kk]
        return carry

    lax.fori_loop(0, MZ // 2, spread_some, 0)
    forward_gather(1, 0)
    lax.fori_loop(MZ // 2, MZ, spread_some, 0)
    for offset in range(1, py):
        sum_y(offset).wait()
    pt_src[2] = sum(pt_land[1, i] for i in range(py))
    pt_land[2, idp] = pt_src[2]
    for offset in range(1, samples):
        sum_dp(offset).start()

    def last(g, carry):
        @pl.when(g + 1 < groups)
        def _():
            forward_gather(1, g + 1)

        finish_gather(1, g)
        build(g)
        field_load(cb_hbm, sb, cb_sem, g).wait()

        def pair(p):
            first = g * GROUP + 2 * p

            for start in range(0, cells, FINE):
                some = slice(start, start + FINE)
                field = dot(uh[some], gf[p])
                for h in range(2):
                    value = sb[first + h, some].astype(F32) + field[:, h * nx : (h + 1) * nx]
                    sb[first + h, some] = (value + mix[first + h, some]).astype(BF16)

        for p in range(2):
            pair(p)
        return carry

    lax.fori_loop(0, groups, last, 0)

    for offset in range(1, samples):
        sum_dp(offset).wait()
    pt_ref[...] = sum(pt_land[2, i] for i in range(samples))
    end_reduce_sends(1)
    end_gather_sends(1)


def finish_kernel(point_scale, ia_ref, gb_ref, sg_ref, pt_ref, ia_hbm, gb_hbm, sg_hbm, point_ref, sems):
    copies = []
    for which, (src, dst) in enumerate(((ia_ref, ia_hbm), (gb_ref, gb_hbm), (sg_ref, sg_hbm))):
        parts = sems.shape[1]
        each = src.shape[0] // parts
        for i in range(parts):
            some = pl.ds(i * each, each)
            copies.append(pltpu.make_async_copy(src.at[some], dst.at[some], sems.at[which, i]))
    for copy in copies:
        copy.start()
    value = pt_ref[...]
    chans = point_ref.shape[0]
    row = lax.broadcasted_iota(jnp.int32, (value.shape[1], chans), 0)
    column = lax.broadcasted_iota(jnp.int32, (value.shape[1], chans), 1)
    ones = (row // SUB == column).astype(BF16)
    total = jnp.zeros(point_ref.shape, F32)
    for _ in range(3):
        part = value.astype(BF16)
        total += dot(part, ones)
        value -= part.astype(F32)
    point_ref[...] = total * point_scale
    for copy in copies:
        copy.wait()


def fused_device(state_a, state_b, cotan_a, cotan_b, spectral_weight, point_weight):
    samples, px, py = (lax.axis_size(name) for name in ("dp", "px", "py"))
    _, chans, ys, zs, nx = state_b.shape
    ny, nz = ys * px, zs * py
    cells, modes = ys * zs, MY * MZ
    groups = chans // GROUP
    kk = MX // px
    tall = modes // py
    total = nx * ny * nz
    scales = (
        1.0 / math.sqrt(total), 1.0 / math.sqrt(MX * MY * MZ), math.sqrt(MX * MY * MZ / (samples * total)),
    )
    th, uh, turn = (jnp.asarray(t) for t in base_tables((ys, zs, ny, nz)))
    (fh, fl), (xh, xl) = wide_tables(px, nx)
    fh, fl, xh, xl = (jnp.asarray(t) for t in (fh, fl, xh, xl))
    side = chans * SUB
    jj, ll = tall // MZ, MZ
    weight = spectral_weight.reshape(jj, ll, kk * 2 * chans, chans)
    spread = (jj, ll, kk * 2 * GROUP, chans)
    fields = [value.reshape(chans, cells, nx) for value in (state_b, state_a, cotan_a, cotan_b)]
    field = jax.ShapeDtypeStruct((chans, cells, nx), BF16)
    any_spec = pl.BlockSpec(memory_space=pl.ANY)
    vmem_spec = pl.BlockSpec(memory_space=pltpu.VMEM)
    dma = pltpu.SemaphoreType.DMA
    near = py - 1
    input_a, grad_b, sg, point = pl.pallas_call(
        lambda *refs: fused_kernel(scales, *refs),
        in_specs=[any_spec] * 12 + [vmem_spec],
        out_specs=[vmem_spec] * 4,
        out_shape=[
            pltpu.VMEM(field.shape, BF16), pltpu.VMEM(field.shape, BF16),
            pltpu.VMEM(spread, F32), pltpu.VMEM((chans, side), F32),
        ],
        scratch_shapes=[
            pltpu.VMEM((chans, cells, nx), BF16), pltpu.VMEM((chans, cells, nx), F32),
            pltpu.VMEM(th.shape, BF16), pltpu.VMEM(uh.shape, BF16), pltpu.VMEM(fh.shape, BF16),
            pltpu.VMEM(fl.shape, BF16), pltpu.VMEM(xh.shape, BF16), pltpu.VMEM(xl.shape, BF16),
            pltpu.VMEM((side, side), BF16),
            pltpu.VMEM((WEIGHT_SLOTS, jj) + weight.shape[2:], BF16), pltpu.VMEM((2, chans, MZ, chans, 128), BF16),
            pltpu.VMEM(turn.shape[1:], F32),
            pltpu.VMEM((px, groups, py, tall, 128), F32),
            pltpu.VMEM((groups, py, tall, 128), F32),
            pltpu.VMEM((near, groups, tall, 128), F32),
            pltpu.VMEM((px, py, groups, tall, 128), F32),
            pltpu.VMEM((2, chans, MZ, 128), F32),
            pltpu.VMEM((samples - 1, 2, chans, MZ, 128), F32),
            pltpu.VMEM((2, chans * MZ, 128), F32),
            pltpu.VMEM((samples, 2, GROUP, MZ, 128), F32),
            pltpu.VMEM((samples - 1, 2, GROUP, MZ, 128), F32),
            pltpu.VMEM((2 * GROUP, MZ, 128), F32),
            pltpu.VMEM((2, 2 * modes, 2 * nx), BF16),
            pltpu.VMEM((2, 2 * modes, 2 * nx), F32),
            pltpu.VMEM((side, side), F32),
            pltpu.VMEM((2, GROUP, chans * MZ, 128), F32),
            pltpu.VMEM((3, chans, side), F32),
            pltpu.VMEM((3, max(py, samples), chans, side), F32),
            dma((7,)), dma((WEIGHT_SLOTS,)), dma((groups,)), dma((groups,)), dma((groups,)), dma((groups,)),
            dma((2, groups)), dma((2, groups)), dma((2, near, groups)), dma((2, near, groups)),
            dma((2, near, groups)), dma((2, near, groups)), dma((2, py, groups)), dma((2, py, groups)),
            dma((2, samples - 1)), dma((2, samples - 1)), dma((1 + near + samples - 1,)), dma((1 + near + samples - 1,)),
        ],
        compiler_params=pltpu.CompilerParams(
            vmem_limit_bytes=FUSED_LIMIT, collective_id=4, has_side_effects=True
        ),
        interpret=INTERPRET,
        name="fused",
    )(*fields, th, uh, fh, fl, xh, xl, weight, turn, point_weight)
    point_scale = 1.0 / math.sqrt(samples * total)
    input_a, grad_b, spectral_grad, point_total = pl.pallas_call(
        lambda *refs: finish_kernel(point_scale, *refs),
        in_specs=[vmem_spec] * 4,
        out_specs=[any_spec] * 3 + [vmem_spec],
        out_shape=[
            field, field, jax.ShapeDtypeStruct(spread, F32), jax.ShapeDtypeStruct((chans, chans), F32),
        ],
        scratch_shapes=[dma((3, groups))],
        compiler_params=pltpu.CompilerParams(vmem_limit_bytes=FINISH_LIMIT),
        interpret=INTERPRET,
        name="finish",
    )(input_a, grad_b, sg, point)
    spectral_grad = spectral_grad.reshape(jj, ll, kk, 2, GROUP, chans).transpose(0, 1, 2, 3, 5, 4)
    full = state_b.shape
    return (input_a.reshape(full), grad_b.reshape(full), spectral_grad, point_total)


def solution(mesh):
    sizes = dict(mesh.shape)

    def body(*values):
        fits = fused_fits(values[1].shape, values[1].shape[0], sizes["dp"], sizes["px"], sizes["py"])
        return (fused_device if fits else general_device)(*values)

    return jax.shard_map(
        body,
        mesh=mesh,
        in_specs=(
            P("dp", None, "px", "py", None),
            P("dp", None, "px", "py", None),
            P("dp", None, "px", "py", None),
            P("dp", None, "px", "py", None),
            P("py", None, "px", None, None, None),
            P(),
        ),
        out_specs=(
            P("dp", None, "px", "py", None),
            P("dp", None, "px", "py", None),
            P("py", None, "px", None, None, "dp"),
            P(),
        ),
        check_vma=False,
    )
```

```python
import math

import jax
import jax.numpy as jnp
import numpy as np
from jax import lax
from jax.experimental import pallas as pl
from jax.experimental.pallas import tpu as pltpu
from jax.sharding import PartitionSpec as P

MX = 32
MY = 32
MZ = 8
GROUP = 4
SUB = 16
LIMIT = 56 * 1024 * 1024
INTERPRET = False
F32 = jnp.float32
BF16 = jnp.bfloat16


def kept(length_all, length_kept, position):
    return jnp.where(position < length_kept // 2, position, length_all - length_kept + position)


def angle(product, length_all):
    return (product % length_all).astype(F32) * (2.0 * math.pi / length_all)


def synthesis_table(shape):
    ys, zs, ny, nz = shape
    mode = lax.broadcasted_iota(jnp.int32, (1, MY * MZ), 1)
    fy = kept(ny, MY, mode // MZ)
    fz = kept(nz, MZ, mode % MZ)
    y = lax.axis_index("px") * ys + lax.broadcasted_iota(jnp.int32, (ys, 1), 0)
    z = lax.axis_index("py") * zs + lax.broadcasted_iota(jnp.int32, (zs, 1), 0)
    ay = angle(fy * y, ny)
    az = angle(fz * z, nz)
    cy, sy = jnp.cos(ay)[:, None, :], jnp.sin(ay)[:, None, :]
    cz, sz = jnp.cos(az)[None], jnp.sin(az)[None]
    table = jnp.concatenate([cy * cz - sy * sz, -(sy * cz + cy * sz)], axis=2)
    return table.reshape(ys * zs, 2 * MY * MZ)


def analysis_table(shape):
    ys, zs, ny, nz = shape
    cell = lax.broadcasted_iota(jnp.int32, (1, ys * zs), 1)
    y = lax.axis_index("px") * ys + cell // zs
    z = lax.axis_index("py") * zs + cell % zs
    fy = kept(ny, MY, lax.broadcasted_iota(jnp.int32, (MY, 1), 0))
    fz = kept(nz, MZ, lax.broadcasted_iota(jnp.int32, (MZ, 1), 0))
    ay = angle(fy * y, ny)
    az = angle(fz * z, nz)
    cy, sy = jnp.cos(ay)[:, None, :], jnp.sin(ay)[:, None, :]
    cz, sz = jnp.cos(az)[None], jnp.sin(az)[None]
    table = jnp.stack([cy * cz - sy * sz, -(sy * cz + cy * sz)])
    return table.reshape(2 * MY * MZ, ys * zs)


def x_tables(px, nx):
    kk = MX // px
    k = np.arange(MX).reshape(px, kk)
    phase = 2.0 * np.pi / nx * (k[:, :, None] * np.arange(nx) % nx)
    cosine, sine = np.cos(phase), np.sin(phase)
    table = np.zeros((2, px, GROUP, 2, kk, GROUP, nx))
    for c in range(GROUP):
        table[0, :, c, 0, :, c] = cosine
        table[0, :, c, 1, :, c] = -sine
        table[1, :, c, 0, :, c] = sine
        table[1, :, c, 1, :, c] = cosine
    table = table.reshape(2, 2 * MX * GROUP, GROUP * nx)
    high = table.astype(BF16)
    low = (table - high.astype(np.float64)).astype(BF16)
    return high, low


def dot(a, b):
    return jnp.dot(a, b, preferred_element_type=F32)


def cut(value):
    high = value.astype(BF16)
    return high, (value - high.astype(F32)).astype(BF16)


def dot3(a, high, low):
    ahigh, alow = cut(a)
    return dot(ahigh, high) + dot(alow, high) + dot(ahigh, low)


def to_modes(b0, b1, xh_ref, xl_ref):
    return dot3(b0, xh_ref[0], xl_ref[0]) + dot3(b1, xh_ref[1], xl_ref[1])


def store_modes(out_ref, group, value, px, py):
    wide = value.shape[1] // px
    tall = value.shape[0] // py
    for i in range(px):
        for j in range(py):
            out_ref[i * py + j, group] = value[j * tall : (j + 1) * tall, i * wide : (i + 1) * wide]


def build_fields(spec_ref, xh_ref, xl_ref, gh_ref, px, py):
    modes = MY * MZ
    for g in range(spec_ref.shape[1]):
        rows = []
        for j in range(py):
            rows.append(jnp.concatenate([spec_ref[i * py + j, g] for i in range(px)], axis=1))
        value = jnp.concatenate(rows, axis=0)
        for t in range(2):
            high = dot3(value, xh_ref[t], xl_ref[t]).astype(BF16)
            half = high.shape[1] // 2
            for h in range(2):
                gh_ref[2 * g + h, t * modes : (t + 1) * modes] = high[:, h * half : (h + 1) * half]


def pair_of(ref, start):
    chans, _, nx = ref.shape
    first = ref[:, pl.ds(start, SUB), :].reshape(chans * SUB, nx)
    second = ref[:, pl.ds(start + SUB, SUB), :].reshape(chans * SUB, nx)
    return jnp.concatenate([first, second], axis=1)


def channel_mix(kron_ref, in_ref, out_ref):
    chans, rows, nx = in_ref.shape

    def body(q, carry):
        start = pl.multiple_of(q * 2 * SUB, 2 * SUB)
        value = dot(kron_ref[...], pair_of(in_ref, start))
        out_ref[:, pl.ds(start, SUB), :] = value[:, :nx].reshape(chans, SUB, nx)
        out_ref[:, pl.ds(start + SUB, SUB), :] = value[:, nx:].reshape(chans, SUB, nx)
        return carry

    lax.fori_loop(0, rows // (2 * SUB), body, 0)


def position(py):
    return lax.axis_index("px") * py + lax.axis_index("py")


def partner(px, py, offset):
    other = lax.rem(position(py) + offset, px * py)
    return other, {"px": lax.div(other, py), "py": lax.rem(other, py)}


def greet(px, py):
    barrier = pltpu.get_barrier_semaphore()
    for offset in range(1, px * py):
        pl.semaphore_signal(
            barrier, inc=1, device_id=partner(px, py, offset)[1], device_id_type=pl.DeviceIdType.MESH
        )
    pl.semaphore_wait(barrier, px * py - 1)


def scatter_copy(px, py, offset, group, part_ref, land_ref, send_sem, recv_sem):
    other, device = partner(px, py, offset)
    return pltpu.make_async_remote_copy(
        part_ref.at[other, group], land_ref.at[offset, group], send_sem.at[offset, group], recv_sem.at[offset, group],
        device_id=device, device_id_type=pl.DeviceIdType.MESH,
    )


def scatter_kernel(px, py, part_ref, out_ref, land_ref, send_sem, recv_sem):
    count = px * py
    greet(px, py)
    groups = part_ref.shape[1]
    for g in range(groups):
        for offset in range(1, count):
            scatter_copy(px, py, offset, g, part_ref, land_ref, send_sem, recv_sem).start()
    out_ref[...] = part_ref[position(py)]
    for g in range(groups):
        for offset in range(1, count):
            scatter_copy(px, py, offset, g, part_ref, land_ref, send_sem, recv_sem).wait()
            out_ref[g] += land_ref[offset, g]


def gather_kernel(px, py, own_ref, out_ref, land_ref, send_sem, recv_sem):
    count = px * py
    greet(px, py)
    copies = []
    for offset in range(1, count):
        copies.append(
            pltpu.make_async_remote_copy(
                own_ref, land_ref.at[offset], send_sem.at[offset], recv_sem.at[offset],
                device_id=partner(px, py, offset)[1], device_id_type=pl.DeviceIdType.MESH,
            )
        )
        copies[-1].start()
    here = position(py)
    out_ref[here] = own_ref[...]
    for offset in range(1, count):
        copies[offset - 1].wait()
        out_ref[lax.rem(here + count - offset, count)] = land_ref[offset]


def mix_kernel(s_ref, w_ref, out_ref):
    chans = s_ref.shape[1]
    real = jnp.zeros(out_ref.shape[1:], F32)
    imag = jnp.zeros(out_ref.shape[1:], F32)
    for c in range(chans):
        s_real, s_imag = s_ref[0, c : c + 1], s_ref[1, c : c + 1]
        w_real, w_imag = w_ref[0, c].astype(F32), w_ref[1, c].astype(F32)
        real += s_real * w_real - s_imag * w_imag
        imag += s_real * w_imag + s_imag * w_real
    out_ref[0] = real
    out_ref[1] = imag


def adjoint_kernel(b_ref, w_ref, out_ref):
    b_real, b_imag = b_ref[0], b_ref[1]
    for c in range(w_ref.shape[1]):
        w_real, w_imag = w_ref[0, c].astype(F32), w_ref[1, c].astype(F32)
        out_ref[0, c : c + 1] = jnp.sum(b_real * w_real + b_imag * w_imag, axis=0, keepdims=True)
        out_ref[1, c : c + 1] = jnp.sum(b_imag * w_real - b_real * w_imag, axis=0, keepdims=True)


def forward_kernel(
    px, py, v_ref, th_ref, xh_ref, xl_ref, out_ref, part_ref, land_ref, send_sem, recv_sem
):
    modes = MY * MZ
    parts = []
    for p in range(GROUP // 2):
        value = jnp.concatenate([v_ref[2 * p], v_ref[2 * p + 1]], axis=1)
        parts.append(dot(th_ref[...], value))
    b0 = jnp.concatenate([part[:modes] for part in parts], axis=1)
    b1 = jnp.concatenate([part[modes:] for part in parts], axis=1)
    step = pl.program_id(0)
    store_modes(part_ref, step, to_modes(b0, b1, xh_ref, xl_ref), px, py)
    count = px * py

    @pl.when(step == 0)
    def _():
        greet(px, py)

    for offset in range(1, count):
        scatter_copy(px, py, offset, step, part_ref, land_ref, send_sem, recv_sem).start()

    @pl.when(step == pl.num_programs(0) - 1)
    def _():
        out_ref[...] = part_ref[position(py)]
        for g in range(part_ref.shape[1]):
            for offset in range(1, count):
                scatter_copy(px, py, offset, g, part_ref, land_ref, send_sem, recv_sem).wait()
                out_ref[g] += land_ref[offset, g]


def middle_kernel(
    px, py, steps, spec_ref, vb_ref, va_ref, ca_ref, uh_ref, th_ref, xh_ref, xl_ref, fh_ref, fl_ref,
    kron_ref, ia_ref, sl_ref, back_ref, point_ref, gh_ref, acc_ref, mix_ref,
):
    step = pl.program_id(0)
    modes = MY * MZ
    nx = vb_ref.shape[2]
    chans, rows = vb_ref.shape[:2]

    @pl.when(step == 0)
    def _():
        build_fields(spec_ref, xh_ref, xl_ref, gh_ref, px, py)
        acc_ref[...] = jnp.zeros_like(acc_ref)
        point_ref[...] = jnp.zeros_like(point_ref)

    channel_mix(kron_ref, vb_ref, mix_ref)
    c0 = math.sqrt(2.0 / math.pi)

    def body(p, carry):
        field = dot(uh_ref[...], gh_ref[p])
        slopes = []
        for h in range(2):
            d = 2 * p + h
            v = field[:, h * nx : (h + 1) * nx] + mix_ref[d]
            v2 = v * v
            t = jnp.tanh(v * (c0 + (c0 * 0.044715) * v2))
            half = 0.5 + 0.5 * t
            ia_ref[d] = (va_ref[d].astype(F32) - v * half).astype(BF16)
            deriv = half + (0.5 * v) * (1.0 - t * t) * (c0 + (3.0 * c0 * 0.044715) * v2)
            slope = (ca_ref[d].astype(F32) * deriv).astype(BF16)
            sl_ref[d] = slope
            slopes.append(slope)
        both = jnp.concatenate(slopes, axis=1)
        acc_ref[p] += dot(th_ref[...], both)
        return carry

    lax.fori_loop(0, chans // 2, body, 0)

    def point_body(q, carry):
        start = pl.multiple_of(q * 2 * SUB, 2 * SUB)
        point_ref[...] += lax.dot_general(
            pair_of(vb_ref, start), pair_of(sl_ref, start), (((1,), (1,)), ((), ())), preferred_element_type=F32
        )
        return carry

    lax.fori_loop(0, rows // (2 * SUB), point_body, 0)

    @pl.when(step == steps - 1)
    def _():
        for g in range(chans // GROUP):
            parts = [acc_ref[2 * g + h] for h in range(2)]
            b0 = jnp.concatenate([part[:modes] for part in parts], axis=1)
            b1 = jnp.concatenate([part[modes:] for part in parts], axis=1)
            store_modes(back_ref, g, to_modes(b0, b1, fh_ref, fl_ref), px, py)


def last_kernel(
    px, py, spec_ref, sl_ref, cb_ref, uh_ref, xh_ref, xl_ref, kron_ref, out_ref, gh_ref, mix_ref
):
    nx = sl_ref.shape[2]

    @pl.when(pl.program_id(0) == 0)
    def _():
        build_fields(spec_ref, xh_ref, xl_ref, gh_ref, px, py)

    channel_mix(kron_ref, sl_ref, mix_ref)

    def body(p, carry):
        field = dot(uh_ref[...], gh_ref[p])
        for h in range(2):
            d = 2 * p + h
            value = cb_ref[d].astype(F32) + field[:, h * nx : (h + 1) * nx] + mix_ref[d]
            out_ref[d] = value.astype(BF16)
        return carry

    lax.fori_loop(0, sl_ref.shape[0] // 2, body, 0)


def whole(shape):
    return pl.BlockSpec(shape, lambda i: (0,) * len(shape), pipeline_mode=pl.Buffered(1))


def general_device(state_a, state_b, cotan_a, cotan_b, spectral_weight, point_weight):
    samples, px, py = (lax.axis_size(name) for name in ("dp", "px", "py"))
    _, chans, ys, zs, nx = state_b.shape
    ny, nz = ys * px, zs * py
    cells, modes = ys * zs, MY * MZ
    groups = chans // GROUP
    kk = MX // px
    tall, wide = modes // py, 2 * MX * GROUP // px
    own = tall * kk
    scale_f = 1.0 / math.sqrt(nx * ny * nz)
    scale_i = 1.0 / math.sqrt(MX * MY * MZ)
    grad_scale = math.sqrt(MX * MY * MZ / (samples * nx * ny * nz))
    point_scale = 1.0 / math.sqrt(samples * nx * ny * nz)
    shape = (ys, zs, ny, nz)
    th = analysis_table(shape).astype(BF16)
    uh = synthesis_table(shape).astype(BF16)
    xh, xl = x_tables(px, nx)
    fh, fl = (jnp.asarray(np.ascontiguousarray(table.transpose(0, 2, 1))) for table in (xh, xl))
    xh, xl = jnp.asarray(xh), jnp.asarray(xl)
    eye = jnp.eye(SUB, dtype=BF16)
    kron_f = (point_weight.T[:, None, :, None] * eye[None, :, None, :]).reshape(chans * SUB, chans * SUB)
    kron_b = (point_weight[:, None, :, None] * eye[None, :, None, :]).reshape(chans * SUB, chans * SUB)
    field_a, field_b, cot_a, cot_b = (
        value.reshape(chans, cells, nx) for value in (state_a, state_b, cotan_a, cotan_b)
    )
    part_shape = jax.ShapeDtypeStruct((px * py, groups, tall, wide), F32)
    params = pltpu.CompilerParams(vmem_limit_bytes=LIMIT)

    count = px * py
    own_shape = jax.ShapeDtypeStruct((groups, tall, wide), F32)
    exchange = [
        pltpu.VMEM(part_shape.shape, F32),
        pltpu.SemaphoreType.DMA((count, groups)),
        pltpu.SemaphoreType.DMA((count, groups)),
    ]

    def linked(number):
        return pltpu.CompilerParams(vmem_limit_bytes=LIMIT, collective_id=number, has_side_effects=True)

    def to_channels(value):
        value = value.reshape(groups, tall, GROUP, 2, kk).transpose(3, 0, 2, 1, 4)
        return value.reshape(2, chans, own)

    def gather(value, number):
        value = value.reshape(2, groups, GROUP, tall, kk).transpose(1, 3, 2, 0, 4)
        value = value.reshape(groups, tall, wide)
        return pl.pallas_call(
            lambda *refs: gather_kernel(px, py, *refs),
            in_specs=[pl.BlockSpec(memory_space=pltpu.VMEM)],
            out_specs=pl.BlockSpec(memory_space=pltpu.VMEM),
            out_shape=part_shape,
            scratch_shapes=[
                pltpu.VMEM(part_shape.shape, F32), pltpu.SemaphoreType.DMA((count,)), pltpu.SemaphoreType.DMA((count,)),
            ],
            compiler_params=linked(number),
            interpret=INTERPRET,
            name="gather",
        )(value)

    def mode_product(kernel, value, name):
        return pl.pallas_call(
            kernel,
            out_shape=jax.ShapeDtypeStruct((2, chans, own), F32),
            compiler_params=params,
            interpret=INTERPRET,
            name=name,
        )(value, weight)

    spectrum = pl.pallas_call(
        lambda *refs: forward_kernel(px, py, *refs),
        grid=(groups,),
        in_specs=[
            pl.BlockSpec((GROUP, cells, nx), lambda i: (i, 0, 0)),
            whole(th.shape), whole(fh.shape), whole(fl.shape),
        ],
        out_specs=whole(own_shape.shape),
        out_shape=own_shape,
        scratch_shapes=[pltpu.VMEM(part_shape.shape, F32)] + exchange,
        compiler_params=linked(0),
        interpret=INTERPRET,
        name="forward",
    )(field_b, th, fh, fl)
    weight = spectral_weight.transpose(3, 4, 5, 0, 1, 2).reshape(2, chans, chans, own)
    spectrum = to_channels(spectrum) * scale_f
    mixed = gather(mode_product(mix_kernel, spectrum, "mix") * scale_i, 1)

    rows = min(256, cells)
    steps = cells // rows
    block = pl.BlockSpec((chans, rows, nx), lambda i: (0, i, 0))
    u_block = pl.BlockSpec((rows, 2 * modes), lambda i: (i, 0))
    t_block = pl.BlockSpec((2 * modes, rows), lambda i: (0, i))
    field_shape = jax.ShapeDtypeStruct((chans, cells, nx), BF16)
    side = chans * SUB
    g_scratch = [pltpu.VMEM((chans // 2, 2 * modes, 2 * nx), BF16)]
    input_a, slope, back_part, point = pl.pallas_call(
        lambda *refs: middle_kernel(px, py, steps, *refs),
        grid=(steps,),
        in_specs=[
            whole(part_shape.shape), block, block, block, u_block, t_block,
            whole(xh.shape), whole(xl.shape), whole(fh.shape), whole(fl.shape), whole((side, side)),
        ],
        out_specs=[block, block, whole(part_shape.shape), whole((side, side))],
        out_shape=[field_shape, field_shape, part_shape, jax.ShapeDtypeStruct((side, side), F32)],
        scratch_shapes=g_scratch
        + [pltpu.VMEM((chans // 2, 2 * modes, 2 * nx), F32), pltpu.VMEM((chans, rows, nx), F32)],
        compiler_params=params,
        interpret=INTERPRET,
        name="middle",
    )(mixed, field_b, field_a, cot_a, uh, th, xh, xl, fh, fl, kron_f)

    back = pl.pallas_call(
        lambda *refs: scatter_kernel(px, py, *refs),
        in_specs=[pl.BlockSpec(memory_space=pltpu.VMEM)],
        out_specs=pl.BlockSpec(memory_space=pltpu.VMEM),
        out_shape=own_shape,
        scratch_shapes=exchange,
        compiler_params=linked(2),
        interpret=INTERPRET,
        name="scatter",
    )(back_part)
    back = to_channels(back) * scale_i
    grad_spec = gather(mode_product(adjoint_kernel, back, "adjoint") * scale_f, 3)
    grad_b = pl.pallas_call(
        lambda *refs: last_kernel(px, py, *refs),
        grid=(steps,),
        in_specs=[
            whole(part_shape.shape), block, block, u_block,
            whole(xh.shape), whole(xl.shape), whole((side, side)),
        ],
        out_specs=block,
        out_shape=field_shape,
        scratch_shapes=g_scratch + [pltpu.VMEM((chans, rows, nx), F32)],
        compiler_params=params,
        interpret=INTERPRET,
        name="last",
    )(grad_spec, slope, cot_b, uh, xh, xl, kron_b)

    share = chans // samples
    spec_all = lax.all_gather(spectrum, "dp", axis=0)
    back_all = lax.all_gather(back, "dp", axis=0)
    back_own = lax.dynamic_slice_in_dim(back_all, lax.axis_index("dp") * share, share, axis=2)
    p_real, p_imag = spec_all[:, 0, :, None], spec_all[:, 1, :, None]
    q_real, q_imag = back_own[:, 0, None], back_own[:, 1, None]
    grad_real = jnp.sum(p_real * q_real + p_imag * q_imag, axis=0)
    grad_imag = jnp.sum(p_real * q_imag - p_imag * q_real, axis=0)
    grad = jnp.stack([grad_real, grad_imag]) * grad_scale
    spectral_grad = grad.reshape(2, chans, share, tall // MZ, MZ, kk).transpose(3, 4, 5, 0, 1, 2)

    point = jnp.sum(point.reshape(chans, SUB, chans, SUB) * jnp.eye(SUB, dtype=F32)[None, :, None, :], axis=(1, 3))
    point_total = lax.psum(point, ("dp", "px", "py")) * point_scale
    full = state_b.shape
    return (input_a.reshape(full), grad_b.reshape(full), spectral_grad, point_total)


MESH = pl.DeviceIdType.MESH
TALL = 512
FINE = 256
WEIGHT_SLOTS = 2
FUSED_LIMIT = 44900 * 1024
FINISH_LIMIT = 8 * 1024 * 1024


def fused_fits(shape, local_samples, samples, px, py):
    _, chans, ys, zs, nx = shape
    kk = MX // px
    tall = MY * MZ // py
    return (
        local_samples == 1
        and 2 * kk * GROUP == 128
        and nx == 128
        and MZ == 8
        and tall // MZ == 128 // kk
        and samples * GROUP == chans
        and (ys * zs) % TALL == 0
    )


def base_tables(shape):
    ys, zs, ny, nz = shape
    fy = np.where(np.arange(MY) < MY // 2, np.arange(MY), ny - MY + np.arange(MY))
    fz = np.where(np.arange(MZ) < MZ // 2, np.arange(MZ), nz - MZ + np.arange(MZ))
    ay = 2.0 * np.pi / ny * (fy[:, None] * np.arange(ys) % ny)
    az = 2.0 * np.pi / nz * (fz[:, None] * np.arange(zs) % nz)
    both = ay[:, None, :, None] + az[None, :, None, :]
    table = np.stack([np.cos(both), -np.sin(both)]).reshape(2 * MY * MZ, ys * zs).astype(BF16)
    py = 2.0 * np.pi / ny * (fy[None] * (np.arange(ny // ys) * ys)[:, None] % ny)
    pz = 2.0 * np.pi / nz * (fz[None] * (np.arange(nz // zs) * zs)[:, None] % nz)
    turn = py[:, None, :, None] + pz[None, :, None, :]
    turn = np.stack([np.cos(turn), np.sin(turn)], axis=2).reshape(-1, 2, MY * MZ, 1)
    turn = np.broadcast_to(turn, turn.shape[:3] + (128,)).astype(np.float32)
    return table, np.ascontiguousarray(table.T), np.ascontiguousarray(turn)


def wide_tables(px, nx):
    high, low = x_tables(px, nx)
    inverse = [np.concatenate([t[0], t[1]], axis=1) for t in (high, low)]
    forward = [np.ascontiguousarray(t.T) for t in inverse]
    return forward, inverse


def swap_bits(tiles, first):
    lane = lax.broadcasted_iota(jnp.int32, tiles[0].shape, 1)
    tiles = list(tiles)
    for i in range(len(tiles).bit_length() - 1):
        shift = 1 << (first + i)
        upper = lane // shift % 2 == 1
        for t in range(len(tiles)):
            if not t >> i & 1:
                u = t | 1 << i
                low, high = tiles[t], tiles[u]
                tiles[t] = jnp.where(upper, pltpu.roll(high, shift, 1), low)
                tiles[u] = jnp.where(upper, high, pltpu.roll(low, 128 - shift, 1))
    return tiles


def flip(tiles):
    return swap_bits(tiles, 7 - (len(tiles).bit_length() - 1))


def rows_of(ref, start):
    chans, _, nx = ref.shape
    parts = [ref[:, pl.ds(start + u * SUB, SUB), :].reshape(chans * SUB, nx) for u in range(TALL // SUB)]
    return jnp.concatenate(parts, axis=1)


def gelu_pair(v, first, cotan):
    c0 = math.sqrt(2.0 / math.pi)
    v2 = v * v
    half = 0.5 + 0.5 * jnp.tanh(v * (c0 + (c0 * 0.044715) * v2))
    rebuilt = (first.astype(F32) - v * half).astype(BF16)
    inner = v * (2.0 * c0 + (6.0 * c0 * 0.044715) * v2)
    slope = (cotan.astype(F32) * (half + (half * (1.0 - half)) * inner)).astype(BF16)
    return rebuilt, slope


def fused_kernel(
    scales, sb_hbm, sa_hbm, ca_hbm, cb_hbm, th_hbm, uh_hbm, fh_hbm, fl_hbm, xh_hbm, xl_hbm, w_hbm, turn_hbm, pw_ref,
    fa, sb, sg_ref, pt_ref, fc, mix, th, uh, fh, fl, xh, xl, kron, w_raw, w, turn, part, land_x, land_y, gath, spec, spec_land, mode, back,
    back_land, grad, gf, acc, point, sg, pt_src, pt_land,
    in_sem, w_sem, sb_sem, sa_sem, ca_sem, cb_sem, rx_s, rx_r, ry_s, ry_r, gy_s, gy_r, gx_s, gx_r,
    dp_s, dp_r, pt_s, pt_r,
):
    scale_f, scale_i, grad_scale = scales
    groups = part.shape[1]
    py = part.shape[2]
    tall = part.shape[3]
    cells, nx = sb.shape[1:]
    samples = spec_land.shape[0] + 1
    modes = MY * MZ
    ix, iy, idp = lax.axis_index("px"), lax.axis_index("py"), lax.axis_index("dp")
    other_x = 1 - ix

    def near_y(offset):
        return lax.rem(iy + offset, py)

    def near_dp(offset):
        return lax.rem(idp + offset, samples)

    def chan(g):
        return pl.ds(g * GROUP, GROUP)

    def load(index, src, dst):
        return pltpu.make_async_copy(src, dst, in_sem.at[index])

    tables = [
        load(0, th_hbm, th), load(1, fh_hbm, fh), load(2, fl_hbm, fl),
        load(3, turn_hbm.at[ix * py + iy], turn), load(4, xh_hbm, xh), load(5, xl_hbm, xl), load(6, uh_hbm, uh),
    ]

    def load_weight(l):
        slot = lax.rem(l, WEIGHT_SLOTS)
        return pltpu.make_async_copy(w_hbm.at[:, l], w_raw.at[slot], w_sem.at[slot])

    def field_load(src, dst, sem, g):
        return pltpu.make_async_copy(src.at[chan(g)], dst.at[chan(g)], sem.at[g])

    barrier = pltpu.get_barrier_semaphore()
    pl.semaphore_signal(barrier, inc=1, device_id={"px": other_x}, device_id_type=MESH)
    for offset in range(1, py):
        pl.semaphore_signal(barrier, inc=1, device_id={"py": near_y(offset)}, device_id_type=MESH)
    for offset in range(1, samples):
        pl.semaphore_signal(barrier, inc=1, device_id={"dp": near_dp(offset)}, device_id_type=MESH)

    field_load(sb_hbm, sb, sb_sem, 0).start()
    for i in range(4):
        tables[i].start()
    for g in range(1, groups):
        field_load(sb_hbm, sb, sb_sem, g).start()
    for l in range(WEIGHT_SLOTS - 1):
        load_weight(l).start()
    for i in range(4, len(tables)):
        tables[i].start()
    pl.semaphore_wait(barrier, 1 + (py - 1) + (samples - 1))

    def remote(src, dst, send, recv, device):
        return pltpu.make_async_remote_copy(src, dst, send, recv, device_id=device, device_id_type=MESH)

    def reduce_x(f, g):
        return remote(
            part.at[other_x, g], land_x.at[g], rx_s.at[f, g], rx_r.at[f, g], {"px": other_x}
        )

    def reduce_y(f, g, offset):
        to = near_y(offset)
        return remote(
            part.at[ix, g, to], land_y.at[offset - 1, g], ry_s.at[f, offset - 1, g], ry_r.at[f, offset - 1, g],
            {"py": to},
        )

    def gather_y(f, g, offset):
        block = gath.at[ix, iy, g]
        return remote(block, block, gy_s.at[f, offset - 1, g], gy_r.at[f, offset - 1, g], {"py": near_y(offset)})

    def gather_x(f, g, offset):
        block = gath.at[ix, lax.rem(iy + py - offset, py), g]
        return remote(block, block, gx_s.at[f, offset, g], gx_r.at[f, offset, g], {"px": other_x})

    def after_x(f, g):
        reduce_x(f, g).wait_recv()
        part[ix, g] += land_x[g]
        for offset in range(1, py):
            reduce_y(f, g, offset).start()

    def finish_reduce(f, g):
        for offset in range(1, py):
            reduce_y(f, g, offset).wait_recv()
        value = part[ix, g, iy]
        for offset in range(1, py):
            value = value + land_y[offset - 1, g]
        return flip([value[8 * i : 8 * i + 8] for i in range(tall // 8)])

    def end_reduce_sends(f):
        for g in range(groups):
            reduce_x(f, g).wait_send()
            for offset in range(1, py):
                reduce_y(f, g, offset).wait_send()

    def start_gather(f, g, tiles):
        for i, tile in enumerate(flip(tiles)):
            gath[ix, iy, g, 8 * i : 8 * i + 8] = tile
        for offset in range(1, py):
            gather_y(f, g, offset).start()
        gather_x(f, g, 0).start()

    def forward_gather(f, g):
        for offset in range(1, py):
            gather_y(f, g, offset).wait_recv()
            gather_x(f, g, offset).start()

    def finish_gather(f, g):
        for offset in range(py):
            gather_x(f, g, offset).wait_recv()

    def end_gather_sends(f):
        for g in range(groups):
            for offset in range(1, py):
                gather_y(f, g, offset).wait_send()
            for offset in range(py):
                gather_x(f, g, offset).wait_send()

    def turns():
        cosine = jnp.concatenate([turn[0]] * GROUP, axis=1)
        sine = jnp.concatenate([turn[1]] * GROUP, axis=1)
        return cosine, sine

    def analyse(src, first, slot):
        value = jnp.concatenate([src[first], src[first + 1]], axis=1)
        acc[slot] = dot(th[...], value)

    def to_part(g):
        cosine, sine = turns()
        b0 = jnp.concatenate([acc[0, :modes], acc[1, :modes]], axis=1)
        b1 = jnp.concatenate([acc[0, modes:], acc[1, modes:]], axis=1)
        both = jnp.concatenate([b0 * cosine + b1 * sine, b1 * cosine - b0 * sine], axis=1)
        value = dot3(both, fh[...], fl[...])
        for i in range(2):
            part[i, g] = value[:, i * 128 : (i + 1) * 128].reshape(py, tall, 128)

    def build(g):
        value = jnp.concatenate([gath[i, :, g].reshape(modes, 128) for i in range(2)], axis=1)
        high, low = cut(value)
        cosine, sine = turns()
        wide = GROUP * nx
        both = dot(high, xh[...]) + dot(low, xh[...]) + dot(high, xl[...])
        g0, g1 = both[:, :wide], both[:, wide:]
        for t, field in enumerate((g0 * cosine - g1 * sine, g1 * cosine + g0 * sine)):
            field = field.astype(BF16)
            for h in range(2):
                gf[h, t * modes : (t + 1) * modes] = field[:, h * 2 * nx : (h + 1) * 2 * nx]

    def mix_rows(table, src, lo, hi):
        def step(q, carry):
            start = pl.multiple_of(q * TALL, TALL)
            value = dot(table[...], rows_of(src, start))
            for u in range(TALL // SUB):
                mix[:, pl.ds(start + u * SUB, SUB), :] = value[:, u * nx : (u + 1) * nx].reshape(-1, SUB, nx)
            return carry

        lax.fori_loop(lo, hi, step, 0)

    steps = cells // TALL
    side = point.shape[0]
    row = lax.broadcasted_iota(jnp.int32, (side, side), 0)
    column = lax.broadcasted_iota(jnp.int32, (side, side), 1)
    same = row % SUB == column % SUB

    for i in range(4):
        tables[i].wait()

    def forward(g, carry):
        field_load(sb_hbm, sb, sb_sem, g).wait()
        for p in range(2):
            analyse(sb, g * GROUP + 2 * p, p)
        to_part(g)
        reduce_x(0, g).start()

        @pl.when(g >= 1)
        def _():
            after_x(0, g - 1)

        return carry

    lax.fori_loop(0, groups, forward, 0)
    for g in range(groups):
        field_load(sa_hbm, fa, sa_sem, g).start()
        field_load(ca_hbm, fc, ca_sem, g).start()

    def turn_weight(l, carry):
        ahead = l + WEIGHT_SLOTS - 1

        @pl.when(ahead < MZ)
        def _():
            load_weight(ahead).start()

        load_weight(l).wait()
        slot = lax.rem(l, WEIGHT_SLOTS)
        chans = spec.shape[1]
        inner = 2 * chans
        kk = w_raw.shape[2] // inner
        tiles = []
        for t in range(inner):
            low, k = t // kk, t % kk
            some = range(low, w_raw.shape[1], inner // kk)
            rows = [w_raw[slot, j, k * inner : (k + 1) * inner, :] for j in some]
            tiles.append(jnp.concatenate(rows, axis=0).astype(F32).T)
        for r, tile in enumerate(swap_bits(tiles, 0)):
            w[r // chans, r % chans, l] = tile.astype(BF16)
        return carry

    lax.fori_loop(0, MZ // 2, turn_weight, 0)
    after_x(0, groups - 1)
    lax.fori_loop(MZ // 2, MZ, turn_weight, 0)
    spread = (row // SUB == column)[:, :SUB].astype(BF16)
    gathered = (lax.broadcasted_iota(jnp.int32, (SUB, side), 1) // SUB
                == lax.broadcasted_iota(jnp.int32, (SUB, side), 0)).astype(BF16)
    turned = lax.dot_general(spread, pw_ref[...], (((1,), (1,)), ((), ())), preferred_element_type=F32)
    kron[...] = jnp.where(same, dot(turned.astype(BF16), gathered), 0.0).astype(BF16)

    def take_spectrum(g, carry):
        tiles = finish_reduce(0, g)
        for q, tile in enumerate(tiles):
            spec[q % 2, g * GROUP + q // 2] = tile * scale_f
        return carry

    lax.fori_loop(0, groups, take_spectrum, 0)

    def blend(l, carry):
        real = jnp.zeros(w.shape[3:], F32)
        imag = jnp.zeros(w.shape[3:], F32)
        for c in range(spec.shape[1]):
            w_real, w_imag = w[0, c, l].astype(F32), w[1, c, l].astype(F32)
            s_real, s_imag = spec[0, c, pl.ds(l, 1), :], spec[1, c, pl.ds(l, 1), :]
            real += s_real * w_real - s_imag * w_imag
            imag += s_real * w_imag + s_imag * w_real
        mode[0, pl.ds(l, real.shape[0], stride=MZ), :] = real * scale_i
        mode[1, pl.ds(l, real.shape[0], stride=MZ), :] = imag * scale_i
        return carry

    lax.fori_loop(0, MZ, blend, 0)
    for g in range(groups):
        start_gather(0, g, [mode[q % 2, (g * GROUP + q // 2) * MZ :][:MZ] for q in range(2 * GROUP)])

    def send_spec(offset):
        return remote(
            spec, spec_land.at[offset - 1], dp_s.at[0, offset - 1], dp_r.at[0, offset - 1], {"dp": near_dp(offset)}
        )

    def send_back(offset):
        to = near_dp(offset)
        return remote(
            back.at[to], back_land.at[offset - 1], dp_s.at[1, offset - 1], dp_r.at[1, offset - 1], {"dp": to}
        )

    for offset in range(1, samples):
        send_spec(offset).start()
    end_reduce_sends(0)
    for i in range(4, len(tables)):
        tables[i].wait()
    mix_rows(kron, sb, 0, steps)
    forward_gather(0, 0)

    def middle(g, carry):
        @pl.when(g + 1 < groups)
        def _():
            forward_gather(0, g + 1)

        finish_gather(0, g)
        build(g)
        field_load(sa_hbm, fa, sa_sem, g).wait()
        field_load(ca_hbm, fc, ca_sem, g).wait()

        def pair(p):
            first = g * GROUP + 2 * p

            total = None
            for start in range(0, cells, FINE):
                some = slice(start, start + FINE)
                field = dot(uh[some], gf[p])
                slopes = []
                for h in range(2):
                    v = field[:, h * nx : (h + 1) * nx] + mix[first + h, some]
                    rebuilt, slope = gelu_pair(v, fa[first + h, some], fc[first + h, some])
                    fa[first + h, some] = rebuilt
                    fc[first + h, some] = slope
                    slopes.append(slope)
                piece = dot(th[:, some], jnp.concatenate(slopes, axis=1))
                total = piece if total is None else total + piece
            acc[p] = total

        for p in range(2):
            pair(p)
        to_part(g)
        reduce_x(1, g).start()

        @pl.when(g >= 1)
        def _():
            after_x(1, g - 1)

        return carry

    lax.fori_loop(0, groups, middle, 0)
    end_gather_sends(0)

    point[...] = jnp.zeros_like(point)

    def point_rows(lo, hi):
        def step(q, carry):
            start = pl.multiple_of(q * TALL, TALL)
            left, right = rows_of(sb, start), rows_of(fc, start)
            point[...] += lax.dot_general(left, right, (((1,), (1,)), ((), ())), preferred_element_type=F32)
            return carry

        lax.fori_loop(lo, hi, step, 0)

    point_rows(0, steps)
    after_x(1, groups - 1)
    for g in range(groups):
        field_load(cb_hbm, sb, cb_sem, g).start()
    kron[...] = jnp.where(same, dot(dot(spread, pw_ref[...]).astype(BF16), gathered), 0.0).astype(BF16)
    mix_rows(kron, fc, 0, steps)
    diagonal = jnp.where(same, point[...], 0.0)
    pt_src[0] = jnp.sum(diagonal.reshape(-1, SUB, point.shape[1]), axis=1)

    def sum_x():
        return remote(pt_src.at[0], pt_land.at[0, 0], pt_s.at[0], pt_r.at[0], {"px": other_x})

    def sum_y(offset):
        return remote(
            pt_src.at[1], pt_land.at[1, iy], pt_s.at[offset], pt_r.at[offset], {"py": near_y(offset)}
        )

    def sum_dp(offset):
        return remote(
            pt_src.at[2], pt_land.at[2, idp], pt_s.at[py - 1 + offset], pt_r.at[py - 1 + offset],
            {"dp": near_dp(offset)},
        )

    sum_x().start()

    def take_back(g, carry):
        tiles = finish_reduce(1, g)
        for q, tile in enumerate(tiles):
            back[g, q % 2, q // 2] = tile * scale_i
            mode[q % 2, pl.ds(pl.multiple_of((g * GROUP + q // 2) * MZ, MZ), MZ), :] = tile * scale_i
        return carry

    lax.fori_loop(0, groups, take_back, 0)
    for offset in range(1, samples):
        send_back(offset).start()
    sum_x().wait()
    pt_src[1] = pt_src[0] + pt_land[0, 0]
    pt_land[1, iy] = pt_src[1]
    for offset in range(1, py):
        sum_y(offset).start()

    def adjoint(g, carry):
        for l in range(MZ):
            b_real, b_imag = (mode[i, pl.ds(l, w.shape[3], stride=MZ), :] for i in range(2))
            for c in range(GROUP):
                w_real, w_imag = w[0, g * GROUP + c, l].astype(F32), w[1, g * GROUP + c, l].astype(F32)
                real = jnp.sum(b_real * w_real + b_imag * w_imag, axis=0, keepdims=True)
                imag = jnp.sum(b_imag * w_real - b_real * w_imag, axis=0, keepdims=True)
                grad[2 * c, l : l + 1] = real * scale_f
                grad[2 * c + 1, l : l + 1] = imag * scale_f
        start_gather(1, g, [grad[q] for q in range(2 * GROUP)])
        return carry

    lax.fori_loop(0, groups, adjoint, 0)

    for offset in range(1, samples):
        send_spec(offset).wait()
        send_back(offset).wait()

    def outer(c, carry):
        for d in range(GROUP):
            real = jnp.zeros((8, 128), F32)
            imag = jnp.zeros((8, 128), F32)
            for s in range(samples):
                if s == 0:
                    p_real, p_imag = spec[0, c], spec[1, c]
                    q_real, q_imag = back[idp, 0, d], back[idp, 1, d]
                else:
                    p_real, p_imag = spec_land[s - 1, 0, c], spec_land[s - 1, 1, c]
                    q_real, q_imag = back_land[s - 1, 0, d], back_land[s - 1, 1, d]
                real += p_real * q_real + p_imag * q_imag
                imag += p_real * q_imag - p_imag * q_real
            sg[0, d, pl.ds(pl.multiple_of(c * MZ, MZ), MZ), :] = real * grad_scale
            sg[1, d, pl.ds(pl.multiple_of(c * MZ, MZ), MZ), :] = imag * grad_scale
        return carry

    lax.fori_loop(0, spec.shape[1], outer, 0)

    def spread_some(l, carry):
        kk = sg_ref.shape[2] // (2 * GROUP)
        for r in range(2 * GROUP):
            value = sg[r // GROUP, r % GROUP, pl.ds(l, spec.shape[1], stride=MZ), :].T
            for j in range(sg_ref.shape[0]):
                sg_ref[j, l, pl.ds(r, kk, stride=2 * GROUP), :] = value[j * kk : (j + 1) * kk]
        return carry

    lax.fori_loop(0, MZ // 2, spread_some, 0)
    forward_gather(1, 0)
    lax.fori_loop(MZ // 2, MZ, spread_some, 0)
    for offset in range(1, py):
        sum_y(offset).wait()
    pt_src[2] = sum(pt_land[1, i] for i in range(py))
    pt_land[2, idp] = pt_src[2]
    for offset in range(1, samples):
        sum_dp(offset).start()

    def last(g, carry):
        @pl.when(g + 1 < groups)
        def _():
            forward_gather(1, g + 1)

        finish_gather(1, g)
        build(g)
        field_load(cb_hbm, sb, cb_sem, g).wait()

        def pair(p):
            first = g * GROUP + 2 * p

            for start in range(0, cells, FINE):
                some = slice(start, start + FINE)
                field = dot(uh[some], gf[p])
                for h in range(2):
                    value = sb[first + h, some].astype(F32) + field[:, h * nx : (h + 1) * nx]
                    sb[first + h, some] = (value + mix[first + h, some]).astype(BF16)

        for p in range(2):
            pair(p)
        return carry

    lax.fori_loop(0, groups, last, 0)

    for offset in range(1, samples):
        sum_dp(offset).wait()
    pt_ref[...] = sum(pt_land[2, i] for i in range(samples))
    end_reduce_sends(1)
    end_gather_sends(1)


def finish_kernel(point_scale, ia_ref, gb_ref, sg_ref, pt_ref, ia_hbm, gb_hbm, sg_hbm, point_ref, sems):
    copies = []
    for which, (src, dst) in enumerate(((ia_ref, ia_hbm), (gb_ref, gb_hbm), (sg_ref, sg_hbm))):
        parts = sems.shape[1]
        each = src.shape[0] // parts
        for i in range(parts):
            some = pl.ds(i * each, each)
            copies.append(pltpu.make_async_copy(src.at[some], dst.at[some], sems.at[which, i]))
    for copy in copies:
        copy.start()
    value = pt_ref[...]
    chans = point_ref.shape[0]
    row = lax.broadcasted_iota(jnp.int32, (value.shape[1], chans), 0)
    column = lax.broadcasted_iota(jnp.int32, (value.shape[1], chans), 1)
    ones = (row // SUB == column).astype(BF16)
    total = jnp.zeros(point_ref.shape, F32)
    for _ in range(3):
        part = value.astype(BF16)
        total += dot(part, ones)
        value -= part.astype(F32)
    point_ref[...] = total * point_scale
    for copy in copies:
        copy.wait()


def fused_device(state_a, state_b, cotan_a, cotan_b, spectral_weight, point_weight):
    samples, px, py = (lax.axis_size(name) for name in ("dp", "px", "py"))
    _, chans, ys, zs, nx = state_b.shape
    ny, nz = ys * px, zs * py
    cells, modes = ys * zs, MY * MZ
    groups = chans // GROUP
    kk = MX // px
    tall = modes // py
    total = nx * ny * nz
    scales = (
        1.0 / math.sqrt(total), 1.0 / math.sqrt(MX * MY * MZ), math.sqrt(MX * MY * MZ / (samples * total)),
    )
    th, uh, turn = (jnp.asarray(t) for t in base_tables((ys, zs, ny, nz)))
    (fh, fl), (xh, xl) = wide_tables(px, nx)
    fh, fl, xh, xl = (jnp.asarray(t) for t in (fh, fl, xh, xl))
    side = chans * SUB
    jj, ll = tall // MZ, MZ
    weight = spectral_weight.reshape(jj, ll, kk * 2 * chans, chans)
    spread = (jj, ll, kk * 2 * GROUP, chans)
    fields = [value.reshape(chans, cells, nx) for value in (state_b, state_a, cotan_a, cotan_b)]
    field = jax.ShapeDtypeStruct((chans, cells, nx), BF16)
    any_spec = pl.BlockSpec(memory_space=pl.ANY)
    vmem_spec = pl.BlockSpec(memory_space=pltpu.VMEM)
    dma = pltpu.SemaphoreType.DMA
    near = py - 1
    input_a, grad_b, sg, point = pl.pallas_call(
        lambda *refs: fused_kernel(scales, *refs),
        in_specs=[any_spec] * 12 + [vmem_spec],
        out_specs=[vmem_spec] * 4,
        out_shape=[
            pltpu.VMEM(field.shape, BF16), pltpu.VMEM(field.shape, BF16),
            pltpu.VMEM(spread, F32), pltpu.VMEM((chans, side), F32),
        ],
        scratch_shapes=[
            pltpu.VMEM((chans, cells, nx), BF16), pltpu.VMEM((chans, cells, nx), F32),
            pltpu.VMEM(th.shape, BF16), pltpu.VMEM(uh.shape, BF16), pltpu.VMEM(fh.shape, BF16),
            pltpu.VMEM(fl.shape, BF16), pltpu.VMEM(xh.shape, BF16), pltpu.VMEM(xl.shape, BF16),
            pltpu.VMEM((side, side), BF16),
            pltpu.VMEM((WEIGHT_SLOTS, jj) + weight.shape[2:], BF16), pltpu.VMEM((2, chans, MZ, chans, 128), BF16),
            pltpu.VMEM(turn.shape[1:], F32),
            pltpu.VMEM((px, groups, py, tall, 128), F32),
            pltpu.VMEM((groups, py, tall, 128), F32),
            pltpu.VMEM((near, groups, tall, 128), F32),
            pltpu.VMEM((px, py, groups, tall, 128), F32),
            pltpu.VMEM((2, chans, MZ, 128), F32),
            pltpu.VMEM((samples - 1, 2, chans, MZ, 128), F32),
            pltpu.VMEM((2, chans * MZ, 128), F32),
            pltpu.VMEM((samples, 2, GROUP, MZ, 128), F32),
            pltpu.VMEM((samples - 1, 2, GROUP, MZ, 128), F32),
            pltpu.VMEM((2 * GROUP, MZ, 128), F32),
            pltpu.VMEM((2, 2 * modes, 2 * nx), BF16),
            pltpu.VMEM((2, 2 * modes, 2 * nx), F32),
            pltpu.VMEM((side, side), F32),
            pltpu.VMEM((2, GROUP, chans * MZ, 128), F32),
            pltpu.VMEM((3, chans, side), F32),
            pltpu.VMEM((3, max(py, samples), chans, side), F32),
            dma((7,)), dma((WEIGHT_SLOTS,)), dma((groups,)), dma((groups,)), dma((groups,)), dma((groups,)),
            dma((2, groups)), dma((2, groups)), dma((2, near, groups)), dma((2, near, groups)),
            dma((2, near, groups)), dma((2, near, groups)), dma((2, py, groups)), dma((2, py, groups)),
            dma((2, samples - 1)), dma((2, samples - 1)), dma((1 + near + samples - 1,)), dma((1 + near + samples - 1,)),
        ],
        compiler_params=pltpu.CompilerParams(
            vmem_limit_bytes=FUSED_LIMIT, collective_id=4, has_side_effects=True
        ),
        interpret=INTERPRET,
        name="fused",
    )(*fields, th, uh, fh, fl, xh, xl, weight, turn, point_weight)
    point_scale = 1.0 / math.sqrt(samples * total)
    input_a, grad_b, spectral_grad, point_total = pl.pallas_call(
        lambda *refs: finish_kernel(point_scale, *refs),
        in_specs=[vmem_spec] * 4,
        out_specs=[any_spec] * 3 + [vmem_spec],
        out_shape=[
            field, field, jax.ShapeDtypeStruct(spread, F32), jax.ShapeDtypeStruct((chans, chans), F32),
        ],
        scratch_shapes=[dma((3, groups))],
        compiler_params=pltpu.CompilerParams(vmem_limit_bytes=FINISH_LIMIT),
        interpret=INTERPRET,
        name="finish",
    )(input_a, grad_b, sg, point)
    spectral_grad = spectral_grad.reshape(jj, ll, kk, 2, GROUP, chans).transpose(0, 1, 2, 3, 5, 4)
    full = state_b.shape
    return (input_a.reshape(full), grad_b.reshape(full), spectral_grad, point_total)


def solution(mesh):
    sizes = dict(mesh.shape)

    def body(*values):
        fits = fused_fits(values[1].shape, values[1].shape[0], sizes["dp"], sizes["px"], sizes["py"])
        return (fused_device if fits else general_device)(*values)

    return jax.shard_map(
        body,
        mesh=mesh,
        in_specs=(
            P("dp", None, "px", "py", None),
            P("dp", None, "px", "py", None),
            P("dp", None, "px", "py", None),
            P("dp", None, "px", "py", None),
            P("py", None, "px", None, None, None),
            P(),
        ),
        out_specs=(
            P("dp", None, "px", "py", None),
            P("dp", None, "px", "py", None),
            P("py", None, "px", None, None, "dp"),
            P(),
        ),
        check_vma=False,
    )
```
